128 devices in a mesh: px: 8 (over z_hi, x), py: 16 (over z_lo, y, core).
Axes of the slice: x: 4, y: 4, z: 4 (z_hi: 2, z_lo: 2; z = z_hi * 2 + z_lo), core: 2. Of those that a mesh axis runs over, the one named last changes fastest.
Arguments:
- air_state: float32 [4, 32, 128, 1024], P(None, None, 'py', 'px'), may hold values from -6 to 6
- air_bulk: float32 [32, 128, 1024], P(None, 'py', 'px'), may hold values from 0.2 to 0.5
- air_buoyancy: float32 [32], replicated, may hold values from 0.3 to 0.6
- air_wind: float32 [2, 32], replicated, may hold values from 0.05 to 0.25
- ground_state: float32 [9, 16, 1024, 128], P(None, None, ('px', 'py')), may hold values from -6 to 6
- ground_moduli: float32 [2, 16, 1024, 128], P(None, None, ('px', 'py')), may hold values from 0.05 to 0.2
- ground_buoyancy: float32 [16, 1024, 128], P(None, ('px', 'py')), may hold values from 0.3 to 0.6
Outputs:
- air_after: float32 [4, 32, 128, 1024], P(None, None, 'py', 'px')
- ground_after: float32 [9, 16, 1024, 128], P(None, None, ('px', 'py'))
The draws below stay inside these ranges and needn't reach their ends.
All inputs are finite; a program needn't handle non-finite values.
Results may differ from the reference program's by a relative error of at most 0.00002.
Values sent between devices are 32-bit elements; how exact they have to be, the bound alone decides.
A program may use at most 128 MiB of HBM per device.

```python
import jax
import jax.numpy as jnp
from jax import lax

AZ = 32
GZ = 16
STEPS = 3
NX = 1024
NY = 128


def level_of(key, dims, shards, smallest, high):
    loudness, own = 1.0, jax.random.fold_in(key, 6)
    for position, shards_of in shards:
        steps = jnp.exp(jax.random.uniform(jax.random.fold_in(own, position), (shards_of,), jnp.float32, smallest / len(shards), high / len(shards)))
        loudness = loudness * jnp.repeat(steps, dims[position] // shards_of).reshape([-1 if axis == position else 1 for axis in range(len(dims))])
    return loudness


def centred(rng, extent, deviation, most, pieces=(), dtype=jnp.bfloat16):
    array = deviation * jax.random.normal(rng, extent, jnp.float32)
    if pieces:
        array = array * level_of(rng, extent, pieces, -0.22, 0.18)
    return jnp.clip(array, -most, most).astype(dtype)


def setup_inputs(seed: int = 0) -> dict:
    seeds = jax.random.split(jax.random.key(seed), 8)
    return {
        "air_state": centred(seeds[0], (4, AZ, NY, NX), 1.0, 6.0, ((2, 16), (3, 8)), jnp.float32),
        "air_bulk": jnp.clip(0.2 + 0.3 * jax.random.uniform(seeds[1], (AZ, NY, NX), jnp.float32) ** level_of(seeds[1], (AZ, NY, NX), ((1, 16), (2, 8)), -0.2, 0.2), 0.2, 0.5),
        "air_buoyancy": jnp.clip(jax.random.uniform(seeds[2], (AZ,), jnp.float32, 0.3, 0.6), 0.3, 0.6),
        "air_wind": jnp.clip(jax.random.uniform(seeds[3], (2, AZ), jnp.float32, 0.05, 0.25), 0.05, 0.25),
        "ground_state": centred(seeds[4], (9, GZ, NX, NY), 1.0, 6.0, ((2, 128),), jnp.float32),
        "ground_moduli": jnp.clip(0.05 + 0.15 * jax.random.uniform(seeds[5], (2, GZ, NX, NY), jnp.float32) ** level_of(seeds[5], (2, GZ, NX, NY), ((2, 128),), -0.2, 0.2), 0.05, 0.2),
        "ground_buoyancy": jnp.clip(0.3 + 0.3 * jax.random.uniform(seeds[6], (GZ, NX, NY), jnp.float32) ** level_of(seeds[6], (GZ, NX, NY), ((1, 128),), -0.2, 0.2), 0.3, 0.6),
    }


def middle(values):
    return values[:, 1:-1, 1:-1]


def beside(values, dimension, offset):
    if dimension == 1:
        return values[:, 1 + offset:values.shape[1] - 1 + offset, 1:-1]
    return values[:, 1:-1, 1 + offset:values.shape[2] - 1 + offset]


def lower_level(values):
    return jnp.concatenate([jnp.zeros_like(values[:1]), values[:-1]], 0)


def upper_level(values):
    return jnp.concatenate([values[1:], jnp.zeros_like(values[:1])], 0)


def clear_top(stress):
    component = lax.broadcasted_iota(jnp.int32, stress.shape, 0)
    layers = lax.broadcasted_iota(jnp.int32, stress.shape, 1)
    retain = (component < 4) | (layers < stress.shape[1] - 1)
    return jnp.where(retain, stress, jnp.zeros_like(stress))


def ground_velocity(velocity, padded_stress, buoyancy, pressure_plane, x_dim, y_dim):
    stress_xx = padded_stress[0]
    stress_yy = padded_stress[1]
    stress_zz = padded_stress[2]
    stress_xy = padded_stress[3]
    stress_xz = padded_stress[4]
    stress_yz = padded_stress[5]
    middle_xy = middle(stress_xy)
    middle_xz = middle(stress_xz)
    middle_yz = middle(stress_yz)
    middle_zz = middle(stress_zz)
    force_x = beside(stress_xx, x_dim, 1) - middle(stress_xx) + middle_xy - beside(stress_xy, y_dim, -1) + middle_xz - lower_level(middle_xz)
    force_y = middle_xy - beside(stress_xy, x_dim, -1) + beside(stress_yy, y_dim, 1) - middle(stress_yy) + middle_yz - lower_level(middle_yz)
    ghost_zz = jnp.concatenate([middle_zz[1:], -pressure_plane[None]], 0)
    force_z = middle_xz - beside(stress_xz, x_dim, -1) + middle_yz - beside(stress_yz, y_dim, -1) + ghost_zz - middle_zz
    return jnp.stack([velocity[0] + buoyancy * force_x, velocity[1] + buoyancy * force_y, velocity[2] + buoyancy * force_z])


def ground_stress(stress, padded_velocity, moduli, x_dim, y_dim):
    speed_x = padded_velocity[0]
    speed_y = padded_velocity[1]
    speed_z = padded_velocity[2]
    middle_x = middle(speed_x)
    middle_y = middle(speed_y)
    middle_z = middle(speed_z)
    lambda_mod = moduli[0]
    shear_mod = moduli[1]
    longitudinal = lambda_mod + 2.0 * shear_mod
    strain_x = middle_x - beside(speed_x, x_dim, -1)
    strain_y = middle_y - beside(speed_y, y_dim, -1)
    strain_z = middle_z - lower_level(middle_z)
    stress_xx = stress[0] + longitudinal * strain_x + lambda_mod * (strain_y + strain_z)
    stress_yy = stress[1] + longitudinal * strain_y + lambda_mod * (strain_x + strain_z)
    stress_zz = stress[2] + longitudinal * strain_z + lambda_mod * (strain_x + strain_y)
    stress_xy = stress[3] + shear_mod * (beside(speed_x, y_dim, 1) - middle_x + beside(speed_y, x_dim, 1) - middle_y)
    stress_xz = stress[4] + shear_mod * (upper_level(middle_x) - middle_x + beside(speed_z, x_dim, 1) - middle_z)
    stress_yz = stress[5] + shear_mod * (upper_level(middle_y) - middle_y + beside(speed_z, y_dim, 1) - middle_z)
    stress_xz = jnp.concatenate([stress_xz[:-1], jnp.zeros_like(stress_xz[-1:])], 0)
    stress_yz = jnp.concatenate([stress_yz[:-1], jnp.zeros_like(stress_yz[-1:])], 0)
    return jnp.stack([stress_xx, stress_yy, stress_zz, stress_xy, stress_xz, stress_yz])


def air_step(air_field, bulk, buoyancy, wind, surface):
    padded = jnp.pad(air_field, ((0, 0), (0, 0), (1, 1), (1, 1)))
    pressure = padded[0]
    flow_x = padded[1]
    flow_y = padded[2]
    flow_z = padded[3]
    wind_x = wind[0][:, None, None]
    wind_y = wind[1][:, None, None]
    air_buoy = buoyancy[:, None, None]
    press_mid = middle(pressure)
    east = middle(flow_x)
    east_next = east - wind_x * (east - beside(flow_x, 2, -1)) - wind_y * (east - beside(flow_x, 1, -1)) - air_buoy * (beside(pressure, 2, 1) - press_mid)
    north = middle(flow_y)
    north_next = north - wind_x * (north - beside(flow_y, 2, -1)) - wind_y * (north - beside(flow_y, 1, -1)) - air_buoy * (beside(pressure, 1, 1) - press_mid)
    upward = middle(flow_z)
    upward_next = upward - wind_x * (upward - beside(flow_z, 2, -1)) - wind_y * (upward - beside(flow_z, 1, -1)) - air_buoy * (press_mid - lower_level(press_mid))
    upward_next = jnp.concatenate([surface[None], upward_next[1:]], 0)
    east_west = jnp.pad(east_next, ((0, 0), (0, 0), (1, 0)))[:, :, :-1]
    north_south = jnp.pad(north_next, ((0, 0), (1, 0), (0, 0)))[:, :-1, :]
    press_next = press_mid - wind_x * (press_mid - beside(pressure, 2, -1)) - wind_y * (press_mid - beside(pressure, 1, -1)) - bulk * ((east_next - east_west) + (north_next - north_south) + (upper_level(upward_next) - upward_next))
    return jnp.stack([press_next, east_next, north_next, upward_next])


def reference(air_state, air_bulk, air_buoyancy, air_wind, ground_state, ground_moduli, ground_buoyancy):
    air_field = air_state
    velocity = ground_state[:3]
    stress = clear_top(ground_state[3:])
    for iteration in range(STEPS):
        pressure_plane = air_field[0, 0].T
        padded_stress = jnp.pad(stress, ((0, 0), (0, 0), (1, 1), (1, 1)))
        velocity = ground_velocity(velocity, padded_stress, ground_buoyancy, pressure_plane, 1, 2)
        surface = velocity[2, -1].T
        air_field = air_step(air_field, air_bulk, air_buoyancy, air_wind, surface)
        padded_velocity = jnp.pad(velocity, ((0, 0), (0, 0), (1, 1), (1, 1)))
        stress = ground_stress(stress, padded_velocity, ground_moduli, 1, 2)
    return air_field, jnp.concatenate([velocity, stress], 0)
```

```python
import jax
import jax.numpy as jnp
from jax import lax
from jax.sharding import PartitionSpec as P

STEPS = 3
RING = ("px", "py")


def before(a, axis):
    pad = [(0, 0)] * a.ndim
    pad[axis] = (1, 0)
    return lax.slice_in_dim(jnp.pad(a, pad), 0, a.shape[axis], axis=axis)


def after(a, axis):
    pad = [(0, 0)] * a.ndim
    pad[axis] = (0, 1)
    return lax.slice_in_dim(jnp.pad(a, pad), 1, a.shape[axis] + 1, axis=axis)


def trade(to_left, to_right):
    n = lax.axis_size(RING)
    from_right = lax.ppermute(to_left, RING, [(i, i - 1) for i in range(1, n)])
    from_left = lax.ppermute(to_right, RING, [(i, i + 1) for i in range(n - 1)])
    return from_left, from_right


def to_strips(block):
    f, z, ny, nx = block.shape
    parts = lax.axis_size("py")
    split = block.reshape(f, z, ny, parts, nx // parts)
    moved = lax.all_to_all(split, "py", 3, 3, tiled=True)
    return moved.transpose(0, 1, 4, 3, 2).reshape(f, z, nx // parts, parts * ny)


def from_strips(strip):
    f, z, nx, ny_all = strip.shape
    parts = lax.axis_size("py")
    split = strip.reshape(f, z, nx, parts, ny_all // parts)
    moved = lax.all_to_all(split, "py", 3, 3, tiled=True)
    return moved.transpose(0, 1, 4, 3, 2).reshape(f, z, ny_all // parts, parts * nx)


def widen(middle_part, left, right):
    parts = [middle_part]
    if left is not None:
        parts.insert(0, left)
    if right is not None:
        parts.append(right)
    return jnp.concatenate(parts, axis=1)


def ground_velocity(vx, vy, vz, sxx, syy, szz, sxy, sxz, syz, b, plane):
    force_x = after(sxx, 1) - sxx + sxy - before(sxy, 2) + sxz - before(sxz, 0)
    force_y = sxy - before(sxy, 1) + after(syy, 2) - syy + syz - before(syz, 0)
    ghost = jnp.concatenate([szz[1:], -plane[None]], 0)
    force_z = sxz - before(sxz, 1) + syz - before(syz, 2) + ghost - szz
    return vx + b * force_x, vy + b * force_y, vz + b * force_z


def ground_stress(stress, vx, vy, vz, lam, mu, width):
    mx = vx[:, 1 : width + 1]
    my = vy[:, 1 : width + 1]
    mz = vz[:, 1 : width + 1]
    longitudinal = lam + 2.0 * mu
    strain_x = mx - vx[:, 0:width]
    strain_y = my - before(my, 2)
    strain_z = mz - before(mz, 0)
    sxx = stress[0] + longitudinal * strain_x + lam * (strain_y + strain_z)
    syy = stress[1] + longitudinal * strain_y + lam * (strain_x + strain_z)
    szz = stress[2] + longitudinal * strain_z + lam * (strain_x + strain_y)
    sxy = stress[3] + mu * (after(mx, 2) - mx + vy[:, 2 : width + 2] - my)
    sxz = stress[4] + mu * (after(mx, 0) - mx + vz[:, 2 : width + 2] - mz)
    syz = stress[5] + mu * (after(my, 0) - my + after(mz, 2) - mz)
    top = lax.broadcasted_iota(jnp.int32, sxz.shape, 0) == sxz.shape[0] - 1
    sxz = jnp.where(top, jnp.zeros_like(sxz), sxz)
    syz = jnp.where(top, jnp.zeros_like(syz), syz)
    return jnp.stack([sxx, syy, szz, sxy, sxz, syz])


def air_update(u, v, w, p, bulk, lift, wind, surface, west_edge, width):
    wind_x = wind[0][:, None, None]
    wind_y = wind[1][:, None, None]
    lift = lift[:, None, None]
    u1 = u - wind_x * (u - before(u, 1)) - wind_y * (u - before(u, 2)) - lift * (after(p, 1) - p)
    v1 = v - wind_x * (v - before(v, 1)) - wind_y * (v - before(v, 2)) - lift * (after(p, 2) - p)
    w1 = w - wind_x * (w - before(w, 1)) - wind_y * (w - before(w, 2)) - lift * (p - before(p, 0))
    u1 = u1[:, 1 : width + 2]
    first = jnp.where(west_edge, jnp.zeros_like(u1[:, :1]), u1[:, :1])
    u1 = jnp.concatenate([first, u1[:, 1:]], 1)
    v1 = v1[:, 2 : width + 2]
    w1 = jnp.concatenate([surface[None], w1[1:, 2 : width + 2]], 0)
    pm = p[:, 2 : width + 2]
    wind_px = wind_x
    p1 = (
        pm
        - wind_px * (pm - p[:, 1 : width + 1])
        - wind_y * (pm - before(pm, 2))
        - bulk * ((u1[:, 1:] - u1[:, :-1]) + (v1 - before(v1, 2)) + (after(w1, 0) - w1))
    )
    return jnp.stack([p1, u1[:, 1:], v1, w1])


def body(air_state, air_bulk, air_buoyancy, air_wind, ground_state, ground_moduli, ground_buoyancy):
    west_edge = (lax.axis_index("px") == 0) & (lax.axis_index("py") == 0)
    moved = to_strips(jnp.concatenate([air_state, air_bulk[None]], 0))
    air = moved[:4]
    bulk = moved[4]
    width = air.shape[2]
    gz = ground_state.shape[1]
    az = air.shape[1]
    ny = air.shape[3]
    velocity = ground_state[:3]
    stress = ground_state[3:]
    top = lax.broadcasted_iota(jnp.int32, stress.shape, 1) == gz - 1
    clear = top & (lax.broadcasted_iota(jnp.int32, stress.shape, 0) >= 4)
    stress = jnp.where(clear, jnp.zeros_like(stress), stress)
    lam = ground_moduli[0]
    mu = ground_moduli[1]
    buoy = ground_buoyancy
    b_left = b_right = None
    for iteration in range(STEPS):
        vx, vy, vz = velocity[0], velocity[1], velocity[2]
        sxx, syy, szz, sxy, sxz, syz = (stress[i] for i in range(6))
        p, u, v, w = air[0], air[1], air[2], air[3]
        send_left = [
            jnp.stack([sxx, sxy, sxz, syy, syz, szz, vy, vz])[:, :, 0].reshape(-1, ny),
            p[:, 0],
        ]
        send_right = [
            jnp.stack([sxx, sxy, sxz, vx])[:, :, width - 1].reshape(-1, ny),
            u[:, width - 2 :].reshape(-1, ny),
            jnp.stack([v, w, p])[:, :, width - 1].reshape(-1, ny),
        ]
        if iteration == 0:
            send_left.append(buoy[:, 0])
            send_right.append(buoy[:, width - 1])
        from_left, from_right = trade(
            jnp.concatenate(send_left, 0), jnp.concatenate(send_right, 0)
        )
        r_g = from_right[: 8 * gz].reshape(8, gz, 1, ny)
        r_p = from_right[8 * gz : 8 * gz + az].reshape(az, 1, ny)
        l_g = from_left[: 4 * gz].reshape(4, gz, 1, ny)
        o = 4 * gz
        l_u = from_left[o : o + 2 * az].reshape(az, 2, ny)
        o += 2 * az
        l_vwp = from_left[o : o + 3 * az].reshape(3, az, 1, ny)
        if iteration == 0:
            b_right = from_right[8 * gz + az :].reshape(gz, 1, ny)
            b_left = from_left[o + 3 * az :].reshape(gz, 1, ny)
            b_e = widen(buoy, b_left, b_right)
        zero_g = jnp.zeros((gz, 1, ny), jnp.float32)
        zero_a = jnp.zeros((az, 1, ny), jnp.float32)
        sxx_e = widen(sxx, l_g[0], r_g[0])
        sxy_e = widen(sxy, l_g[1], r_g[1])
        sxz_e = widen(sxz, l_g[2], r_g[2])
        syy_e = widen(syy, zero_g, r_g[3])
        syz_e = widen(syz, zero_g, r_g[4])
        szz_e = widen(szz, zero_g, r_g[5])
        vx_e = widen(vx, l_g[3], zero_g)
        vy_e = widen(vy, zero_g, r_g[6])
        vz_e = widen(vz, zero_g, r_g[7])
        p_e = widen(p, jnp.concatenate([zero_a, l_vwp[2]], 1), r_p)
        plane_e = p_e[0, 1:]
        vx1, vy1, vz1 = ground_velocity(
            vx_e, vy_e, vz_e, sxx_e, syy_e, szz_e, sxy_e, sxz_e, syz_e, b_e, plane_e
        )
        surface = vz1[gz - 1, 1 : width + 1]
        u_e = widen(u, l_u, zero_a)
        v_e = widen(v, jnp.concatenate([zero_a, l_vwp[0]], 1), zero_a)
        w_e = widen(w, jnp.concatenate([zero_a, l_vwp[1]], 1), zero_a)
        air = air_update(
            u_e, v_e, w_e, p_e, bulk, air_buoyancy, air_wind, surface, west_edge, width
        )
        stress = ground_stress(stress, vx1, vy1, vz1, lam, mu, width)
        velocity = jnp.stack([vx1, vy1, vz1])[:, :, 1 : width + 1]
    ground = jnp.concatenate([velocity, stress], 0)
    return (from_strips(air), ground)


def solution(mesh):
    placed = (
        P(None, None, "py", "px"),
        P(None, "py", "px"),
        P(),
        P(),
        P(None, None, ("px", "py"), None),
        P(None, None, ("px", "py"), None),
        P(None, ("px", "py"), None),
    )
    return jax.shard_map(
        body,
        mesh=mesh,
        in_specs=placed,
        out_specs=(P(None, None, "py", "px"), P(None, None, ("px", "py"), None)),
        check_vma=False,
    )
```

```python
import os

import jax
import jax.numpy as jnp
from jax import lax
from jax.experimental import pallas as pl
from jax.experimental.pallas import tpu as pltpu
from jax.sharding import PartitionSpec as P

STEPS = 3
RING = ("px", "py")
INTERPRET = os.environ.get("STENCIL_INTERPRET") == "1"


def trade(to_left, to_right):
    n = lax.axis_size(RING)
    from_right = lax.ppermute(to_left, RING, [(i, i - 1) for i in range(1, n)])
    from_left = lax.ppermute(to_right, RING, [(i, i + 1) for i in range(n - 1)])
    return from_left, from_right


def to_strips(block):
    f, z, ny, nx = block.shape
    parts = lax.axis_size("py")
    split = block.reshape(f, z, ny, parts, nx // parts)
    moved = lax.all_to_all(split, "py", 3, 3, tiled=True)
    return moved.transpose(0, 4, 1, 3, 2).reshape(f, nx // parts, z, parts * ny)


def from_strips(strip):
    f, nx, z, ny_all = strip.shape
    parts = lax.axis_size("py")
    split = strip.reshape(f, nx, z, parts, ny_all // parts)
    moved = lax.all_to_all(split, "py", 3, 3, tiled=True)
    return moved.transpose(0, 2, 4, 3, 1).reshape(f, z, ny_all // parts, parts * nx)


def _rows(a):
    return lax.broadcasted_iota(jnp.int32, a.shape, 0)


def _lanes(a):
    return lax.broadcasted_iota(jnp.int32, a.shape, 1)


def bz(a):
    return jnp.where(_rows(a) == 0, 0.0, pltpu.roll(a, 1, 0))


def az(a):
    n = a.shape[0]
    return jnp.where(_rows(a) == n - 1, 0.0, pltpu.roll(a, n - 1, 0))


def by(a):
    return jnp.where(_lanes(a) == 0, 0.0, pltpu.roll(a, 1, 1))


def ay(a):
    n = a.shape[1]
    return jnp.where(_lanes(a) == n - 1, 0.0, pltpu.roll(a, n - 1, 1))


def step_kernel(
    air_ref, bulk_ref, vel_ref, st_ref, mod_ref, b_ref, bh_ref, fl_ref, fr_ref, coef_ref, keep_ref,
    air_out, vel_out, st_out,
):
    width = air_ref.shape[1]
    az_n = air_ref.shape[2]
    gz = vel_ref.shape[2]

    def fl(start, count):
        return fl_ref[pl.ds(start, count), :]

    def fr(start, count):
        return fr_ref[pl.ds(start, count), :]

    def gcol(field_ref, k, left, right):
        cols = [left] + [field_ref[k, c] for c in range(width)] + [right]
        return cols

    sxx = gcol(st_ref, 0, fl(0, gz), fr(0, gz))
    sxy = gcol(st_ref, 3, fl(gz, gz), fr(gz, gz))
    sxz = gcol(st_ref, 4, fl(2 * gz, gz), fr(2 * gz, gz))
    syy = gcol(st_ref, 1, None, fr(3 * gz, gz))
    syz = gcol(st_ref, 5, None, fr(4 * gz, gz))
    szz = gcol(st_ref, 2, None, fr(5 * gz, gz))
    vx = gcol(vel_ref, 0, fl(3 * gz, gz), None)
    vy = gcol(vel_ref, 1, None, fr(6 * gz, gz))
    vz = gcol(vel_ref, 2, None, fr(7 * gz, gz))
    bb = [bh_ref[0]] + [b_ref[c] for c in range(width)] + [bh_ref[1]]
    o = 4 * gz
    pr = fr(8 * gz, az_n)
    u = [fl(o, az_n), fl(o + az_n, az_n)] + [air_ref[1, c] for c in range(width)]
    v = [None, fl(o + 2 * az_n, az_n)] + [air_ref[2, c] for c in range(width)]
    w = [None, fl(o + 3 * az_n, az_n)] + [air_ref[3, c] for c in range(width)]
    p = [None, fl(o + 4 * az_n, az_n)] + [air_ref[0, c] for c in range(width)] + [pr]

    grow = lax.broadcasted_iota(jnp.int32, (gz, sxx[1].shape[1]), 0)
    arow = lax.broadcasted_iota(jnp.int32, (az_n, sxx[1].shape[1]), 0)

    vx1 = [None] * (width + 2)
    vy1 = [None] * (width + 2)
    vz1 = [None] * (width + 2)
    for e in range(width + 2):
        if e <= width:
            force_x = sxx[e + 1] - sxx[e] + sxy[e] - by(sxy[e]) + sxz[e] - bz(sxz[e])
            vx1[e] = vx[e] + bb[e] * force_x
        if e >= 1:
            force_y = sxy[e] - sxy[e - 1] + ay(syy[e]) - syy[e] + syz[e] - bz(syz[e])
            vy1[e] = vy[e] + bb[e] * force_y
            plane = jnp.broadcast_to(p[e + 1][0:1, :], szz[e].shape)
            ghost = jnp.where(grow == gz - 1, -plane, pltpu.roll(szz[e], gz - 1, 0))
            force_z = sxz[e] - sxz[e - 1] + syz[e] - by(syz[e]) + ghost - szz[e]
            vz1[e] = vz[e] + bb[e] * force_z

    for c in range(width):
        e = c + 1
        mx, my, mz = vx1[e], vy1[e], vz1[e]
        lam = mod_ref[0, c]
        mu = mod_ref[1, c]
        longitudinal = lam + 2.0 * mu
        strain_x = mx - vx1[e - 1]
        strain_y = my - by(my)
        strain_z = mz - bz(mz)
        st_out[0, c] = st_ref[0, c] + longitudinal * strain_x + lam * (strain_y + strain_z)
        st_out[1, c] = st_ref[1, c] + longitudinal * strain_y + lam * (strain_x + strain_z)
        st_out[2, c] = st_ref[2, c] + longitudinal * strain_z + lam * (strain_x + strain_y)
        st_out[3, c] = st_ref[3, c] + mu * (ay(mx) - mx + vy1[e + 1] - my)
        sxz1 = st_ref[4, c] + mu * (az(mx) - mx + vz1[e + 1] - mz)
        syz1 = st_ref[5, c] + mu * (az(my) - my + ay(mz) - mz)
        st_out[4, c] = jnp.where(grow == gz - 1, 0.0, sxz1)
        st_out[5, c] = jnp.where(grow == gz - 1, 0.0, syz1)
        vel_out[0, c] = mx
        vel_out[1, c] = my
        vel_out[2, c] = mz

    wind_x = coef_ref[0]
    wind_y = coef_ref[1]
    lift = coef_ref[2]
    u1 = [None] * (width + 2)
    for a in range(1, width + 2):
        u1[a] = (
            u[a]
            - wind_x * (u[a] - u[a - 1])
            - wind_y * (u[a] - by(u[a]))
            - lift * (p[a + 1] - p[a])
        )
    u1[1] = jnp.where(keep_ref[...] > 0.5, u1[1], 0.0)
    for c in range(width):
        a = c + 2
        v1 = v[a] - wind_x * (v[a] - v[a - 1]) - wind_y * (v[a] - by(v[a])) - lift * (ay(p[a]) - p[a])
        w1 = w[a] - wind_x * (w[a] - w[a - 1]) - wind_y * (w[a] - by(w[a])) - lift * (p[a] - bz(p[a]))
        surface = jnp.broadcast_to(vz1[c + 1][gz - 1 : gz, :], w1.shape)
        w1 = jnp.where(arow == 0, surface, w1)
        pm = p[a]
        p1 = (
            pm
            - wind_x * (pm - p[a - 1])
            - wind_y * (pm - by(pm))
            - bulk_ref[c] * ((u1[a] - u1[a - 1]) + (v1 - by(v1)) + (az(w1) - w1))
        )
        air_out[0, c] = p1
        air_out[1, c] = u1[a]
        air_out[2, c] = v1
        air_out[3, c] = w1


def run_step(air, bulk, vel, st, mod, b, bh, from_left, from_right, coef, keep):
    return pl.pallas_call(
        step_kernel,
        out_shape=(
            jax.ShapeDtypeStruct(air.shape, jnp.float32),
            jax.ShapeDtypeStruct(vel.shape, jnp.float32),
            jax.ShapeDtypeStruct(st.shape, jnp.float32),
        ),
        interpret=INTERPRET,
    )(air, bulk, vel, st, mod, b, bh, from_left, from_right, coef, keep)


def body(air_state, air_bulk, air_buoyancy, air_wind, ground_state, ground_moduli, ground_buoyancy):
    west_edge = (lax.axis_index("px") == 0) & (lax.axis_index("py") == 0)
    moved = to_strips(jnp.concatenate([air_state, air_bulk[None]], 0))
    air = moved[:4]
    bulk = moved[4]
    width = air.shape[1]
    az_n = air.shape[2]
    ny = air.shape[3]
    ground = ground_state.transpose(0, 2, 1, 3)
    gz = ground.shape[2]
    vel = ground[:3]
    st = ground[3:]
    top = lax.broadcasted_iota(jnp.int32, st.shape, 2) == gz - 1
    clear = top & (lax.broadcasted_iota(jnp.int32, st.shape, 0) >= 4)
    st = jnp.where(clear, jnp.zeros_like(st), st)
    mod = ground_moduli.transpose(0, 2, 1, 3)
    b = ground_buoyancy.transpose(1, 0, 2)
    b_left, b_right = trade(b[0], b[width - 1])
    bh = jnp.stack([b_left, b_right])
    coef = jnp.broadcast_to(
        jnp.stack([air_wind[0], air_wind[1], air_buoyancy])[:, :, None], (3, az_n, ny)
    )
    keep = jnp.broadcast_to(jnp.where(west_edge, 0.0, 1.0).astype(jnp.float32), (az_n, ny))
    for iteration in range(STEPS):
        to_left = jnp.concatenate(
            [st[jnp.array([0, 3, 4, 1, 5, 2]), 0].reshape(-1, ny), vel[1:, 0].reshape(-1, ny), air[0, 0]],
            0,
        )
        to_right = jnp.concatenate(
            [
                st[jnp.array([0, 3, 4]), width - 1].reshape(-1, ny),
                vel[0, width - 1],
                air[1, width - 2],
                air[1, width - 1],
                air[2, width - 1],
                air[3, width - 1],
                air[0, width - 1],
            ],
            0,
        )
        from_left, from_right = trade(to_left, to_right)
        air, vel, st = run_step(air, bulk, vel, st, mod, b, bh, from_left, from_right, coef, keep)
    ground_after = jnp.concatenate([vel, st], 0).transpose(0, 2, 1, 3)
    return (from_strips(air), ground_after)


def solution(mesh):
    placed = (
        P(None, None, "py", "px"),
        P(None, "py", "px"),
        P(),
        P(),
        P(None, None, ("px", "py"), None),
        P(None, None, ("px", "py"), None),
        P(None, ("px", "py"), None),
    )
    return jax.shard_map(
        body,
        mesh=mesh,
        in_specs=placed,
        out_specs=(P(None, None, "py", "px"), P(None, None, ("px", "py"), None)),
        check_vma=False,
    )
```

```python
import os

import jax
import jax.numpy as jnp
from jax import lax
from jax.experimental import pallas as pl
from jax.experimental.pallas import tpu as pltpu
from jax.sharding import PartitionSpec as P

STEPS = 3
RING = ("px", "py")
INTERPRET = os.environ.get("STENCIL_INTERPRET") == "1"


def trade(to_left, to_right):
    n = lax.axis_size(RING)
    from_right = lax.ppermute(to_left, RING, [(i, i - 1) for i in range(1, n)])
    from_left = lax.ppermute(to_right, RING, [(i, i + 1) for i in range(n - 1)])
    return from_left, from_right


def to_strips(block):
    f, z, ny, nx = block.shape
    parts = lax.axis_size("py")
    split = block.reshape(f, z, ny, parts, nx // parts)
    moved = lax.all_to_all(split, "py", 3, 3, tiled=True)
    return moved.transpose(0, 4, 1, 3, 2).reshape(f, nx // parts, z, parts * ny)


def from_strips(strip):
    f, nx, z, ny_all = strip.shape
    parts = lax.axis_size("py")
    split = strip.reshape(f, nx, z, parts, ny_all // parts)
    moved = lax.all_to_all(split, "py", 3, 3, tiled=True)
    return moved.transpose(0, 2, 4, 3, 1).reshape(f, z, ny_all // parts, parts * nx)


def _rows(a):
    return lax.broadcasted_iota(jnp.int32, a.shape, 0)


def _lanes(a):
    return lax.broadcasted_iota(jnp.int32, a.shape, 1)


def bz(a):
    return jnp.where(_rows(a) == 0, 0.0, pltpu.roll(a, 1, 0))


def az(a):
    n = a.shape[0]
    return jnp.where(_rows(a) == n - 1, 0.0, pltpu.roll(a, n - 1, 0))


def by(a):
    return jnp.where(_lanes(a) == 0, 0.0, pltpu.roll(a, 1, 1))


def ay(a):
    n = a.shape[1]
    return jnp.where(_lanes(a) == n - 1, 0.0, pltpu.roll(a, n - 1, 1))


def step_kernel(
    air_ref, bulk_ref, vel_ref, st_ref, mod_ref, b_ref, bl_ref, br_ref, fl_ref, fr_ref, coef_ref,
    keep_ref, air_out, vel_out, st_out, tl_out, tr_out,
):
    width = air_ref.shape[1]
    az_n = air_ref.shape[2]
    gz = vel_ref.shape[2]

    def fl(start, count):
        return fl_ref[pl.ds(start, count), :]

    def fr(start, count):
        return fr_ref[pl.ds(start, count), :]

    def gcol(field_ref, k, left, right):
        cols = [left] + [field_ref[k, c] for c in range(width)] + [right]
        return cols

    sxx = gcol(st_ref, 0, fl(0, gz), fr(0, gz))
    sxy = gcol(st_ref, 3, fl(gz, gz), fr(gz, gz))
    sxz = gcol(st_ref, 4, fl(2 * gz, gz), fr(2 * gz, gz))
    syy = gcol(st_ref, 1, None, fr(3 * gz, gz))
    syz = gcol(st_ref, 5, None, fr(4 * gz, gz))
    szz = gcol(st_ref, 2, None, fr(5 * gz, gz))
    vx = gcol(vel_ref, 0, fl(3 * gz, gz), None)
    vy = gcol(vel_ref, 1, None, fr(6 * gz, gz))
    vz = gcol(vel_ref, 2, None, fr(7 * gz, gz))
    bb = [bl_ref[...]] + [b_ref[c] for c in range(width)] + [br_ref[...]]
    o = 4 * gz
    pr = fr(8 * gz, az_n)
    u = [fl(o, az_n), fl(o + az_n, az_n)] + [air_ref[1, c] for c in range(width)]
    v = [None, fl(o + 2 * az_n, az_n)] + [air_ref[2, c] for c in range(width)]
    w = [None, fl(o + 3 * az_n, az_n)] + [air_ref[3, c] for c in range(width)]
    p = [None, fl(o + 4 * az_n, az_n)] + [air_ref[0, c] for c in range(width)] + [pr]

    grow = lax.broadcasted_iota(jnp.int32, (gz, sxx[1].shape[1]), 0)
    arow = lax.broadcasted_iota(jnp.int32, (az_n, sxx[1].shape[1]), 0)

    vx1 = [None] * (width + 2)
    vy1 = [None] * (width + 2)
    vz1 = [None] * (width + 2)
    for e in range(width + 2):
        if e <= width:
            force_x = sxx[e + 1] - sxx[e] + sxy[e] - by(sxy[e]) + sxz[e] - bz(sxz[e])
            vx1[e] = vx[e] + bb[e] * force_x
        if e >= 1:
            force_y = sxy[e] - sxy[e - 1] + ay(syy[e]) - syy[e] + syz[e] - bz(syz[e])
            vy1[e] = vy[e] + bb[e] * force_y
            plane = jnp.broadcast_to(p[e + 1][0:1, :], szz[e].shape)
            ghost = jnp.where(grow == gz - 1, -plane, pltpu.roll(szz[e], gz - 1, 0))
            force_z = sxz[e] - sxz[e - 1] + syz[e] - by(syz[e]) + ghost - szz[e]
            vz1[e] = vz[e] + bb[e] * force_z

    for c in range(width):
        e = c + 1
        mx, my, mz = vx1[e], vy1[e], vz1[e]
        lam = mod_ref[0, c]
        mu = mod_ref[1, c]
        longitudinal = lam + 2.0 * mu
        strain_x = mx - vx1[e - 1]
        strain_y = my - by(my)
        strain_z = mz - bz(mz)
        st_out[0, c] = st_ref[0, c] + longitudinal * strain_x + lam * (strain_y + strain_z)
        st_out[1, c] = st_ref[1, c] + longitudinal * strain_y + lam * (strain_x + strain_z)
        st_out[2, c] = st_ref[2, c] + longitudinal * strain_z + lam * (strain_x + strain_y)
        st_out[3, c] = st_ref[3, c] + mu * (ay(mx) - mx + vy1[e + 1] - my)
        sxz1 = st_ref[4, c] + mu * (az(mx) - mx + vz1[e + 1] - mz)
        syz1 = st_ref[5, c] + mu * (az(my) - my + ay(mz) - mz)
        st_out[4, c] = jnp.where(grow == gz - 1, 0.0, sxz1)
        st_out[5, c] = jnp.where(grow == gz - 1, 0.0, syz1)
        vel_out[0, c] = mx
        vel_out[1, c] = my
        vel_out[2, c] = mz
        if c == 0:
            for k, (ref, f) in enumerate(
                [(st_out, 0), (st_out, 3), (st_out, 4), (st_out, 1), (st_out, 5), (st_out, 2),
                 (vel_out, 1), (vel_out, 2)]
            ):
                tl_out[pl.ds(k * gz, gz), :] = ref[f, 0]
        if c == width - 1:
            for k, (ref, f) in enumerate([(st_out, 0), (st_out, 3), (st_out, 4), (vel_out, 0)]):
                tr_out[pl.ds(k * gz, gz), :] = ref[f, c]

    wind_x = coef_ref[0]
    wind_y = coef_ref[1]
    lift = coef_ref[2]
    u1 = [None] * (width + 2)
    for a in range(1, width + 2):
        u1[a] = (
            u[a]
            - wind_x * (u[a] - u[a - 1])
            - wind_y * (u[a] - by(u[a]))
            - lift * (p[a + 1] - p[a])
        )
    u1[1] = jnp.where(keep_ref[...] > 0.5, u1[1], 0.0)
    for c in range(width):
        a = c + 2
        v1 = v[a] - wind_x * (v[a] - v[a - 1]) - wind_y * (v[a] - by(v[a])) - lift * (ay(p[a]) - p[a])
        w1 = w[a] - wind_x * (w[a] - w[a - 1]) - wind_y * (w[a] - by(w[a])) - lift * (p[a] - bz(p[a]))
        surface = jnp.broadcast_to(vz1[c + 1][gz - 1 : gz, :], w1.shape)
        w1 = jnp.where(arow == 0, surface, w1)
        pm = p[a]
        p1 = (
            pm
            - wind_x * (pm - p[a - 1])
            - wind_y * (pm - by(pm))
            - bulk_ref[4, c] * ((u1[a] - u1[a - 1]) + (v1 - by(v1)) + (az(w1) - w1))
        )
        air_out[0, c] = p1
        air_out[1, c] = u1[a]
        air_out[2, c] = v1
        air_out[3, c] = w1
        if c == 0:
            tl_out[pl.ds(8 * gz, az_n), :] = p1
        if c == width - 2:
            tr_out[pl.ds(4 * gz, az_n), :] = u1[a]
        if c == width - 1:
            o = 4 * gz
            tr_out[pl.ds(o + az_n, az_n), :] = u1[a]
            tr_out[pl.ds(o + 2 * az_n, az_n), :] = v1
            tr_out[pl.ds(o + 3 * az_n, az_n), :] = w1
            tr_out[pl.ds(o + 4 * az_n, az_n), :] = p1


def run_step(air, bulk, vel, st, mod, b, b_left, b_right, from_left, from_right, coef, keep):
    return pl.pallas_call(
        step_kernel,
        out_shape=(
            jax.ShapeDtypeStruct((4,) + air.shape[1:], jnp.float32),
            jax.ShapeDtypeStruct(vel.shape, jnp.float32),
            jax.ShapeDtypeStruct(st.shape, jnp.float32),
            jax.ShapeDtypeStruct(from_right.shape, jnp.float32),
            jax.ShapeDtypeStruct(from_left.shape, jnp.float32),
        ),
        interpret=INTERPRET,
    )(air, bulk, vel, st, mod, b, b_left, b_right, from_left, from_right, coef, keep)


def body(air_state, air_bulk, air_buoyancy, air_wind, ground_state, ground_moduli, ground_buoyancy):
    west_edge = (lax.axis_index("px") == 0) & (lax.axis_index("py") == 0)
    moved = to_strips(jnp.concatenate([air_state, air_bulk[None]], 0))
    air = moved
    width = air.shape[1]
    az_n = air.shape[2]
    ny = air.shape[3]
    ground = ground_state.transpose(0, 2, 1, 3)
    gz = ground.shape[2]
    vel = ground[:3]
    st = ground[3:]
    top = lax.broadcasted_iota(jnp.int32, st.shape, 2) == gz - 1
    clear = top & (lax.broadcasted_iota(jnp.int32, st.shape, 0) >= 4)
    st = jnp.where(clear, jnp.zeros_like(st), st)
    mod = ground_moduli.transpose(0, 2, 1, 3)
    b = ground_buoyancy.transpose(1, 0, 2)
    b_left, b_right = trade(b[0], b[width - 1])
    coef = jnp.broadcast_to(
        jnp.stack([air_wind[0], air_wind[1], air_buoyancy])[:, :, None], (3, az_n, ny)
    )
    keep = jnp.broadcast_to(jnp.where(west_edge, 0.0, 1.0).astype(jnp.float32), (az_n, ny))
    to_left = jnp.concatenate(
        [st[i, 0] for i in (0, 3, 4, 1, 5, 2)] + [vel[1, 0], vel[2, 0], air[0, 0]], 0
    )
    to_right = jnp.concatenate(
        [st[i, width - 1] for i in (0, 3, 4)]
        + [vel[0, width - 1], air[1, width - 2]]
        + [air[i, width - 1] for i in (1, 2, 3, 0)],
        0,
    )
    for iteration in range(STEPS):
        from_left, from_right = trade(to_left, to_right)
        air, vel, st, to_left, to_right = run_step(
            air, moved, vel, st, mod, b, b_left, b_right, from_left, from_right, coef, keep
        )
    ground_after = jnp.concatenate([vel, st], 0).transpose(0, 2, 1, 3)
    return (from_strips(air), ground_after)


def solution(mesh):
    placed = (
        P(None, None, "py", "px"),
        P(None, "py", "px"),
        P(),
        P(),
        P(None, None, ("px", "py"), None),
        P(None, None, ("px", "py"), None),
        P(None, ("px", "py"), None),
    )
    return jax.shard_map(
        body,
        mesh=mesh,
        in_specs=placed,
        out_specs=(P(None, None, "py", "px"), P(None, None, ("px", "py"), None)),
        check_vma=False,
    )
```

```python
import os

import jax
import jax.numpy as jnp
from jax import lax
from jax.experimental import pallas as pl
from jax.experimental.pallas import tpu as pltpu
from jax.sharding import PartitionSpec as P

STEPS = 3
RING = ("px", "py")
INTERPRET = os.environ.get("STENCIL_INTERPRET") == "1"


def trade(to_left, to_right):
    n = lax.axis_size(RING)
    from_right = lax.ppermute(to_left, RING, [(i, i - 1) for i in range(1, n)])
    from_left = lax.ppermute(to_right, RING, [(i, i + 1) for i in range(n - 1)])
    return from_left, from_right


def to_strips(block):
    f, z, ny, nx = block.shape
    parts = lax.axis_size("py")
    split = block.reshape(f, z, ny, parts, nx // parts)
    moved = lax.all_to_all(split, "py", 3, 3, tiled=True)
    return moved.transpose(0, 4, 1, 3, 2).reshape(f, nx // parts, z, parts * ny)


def from_strips(strip):
    f, nx, z, ny_all = strip.shape
    parts = lax.axis_size("py")
    split = strip.reshape(f, nx, z, parts, ny_all // parts)
    moved = lax.all_to_all(split, "py", 3, 3, tiled=True)
    return moved.transpose(0, 2, 4, 3, 1).reshape(f, z, ny_all // parts, parts * nx)


def _rows(a):
    return lax.broadcasted_iota(jnp.int32, a.shape, 0)


def _lanes(a):
    return lax.broadcasted_iota(jnp.int32, a.shape, 1)


def bz(a):
    return jnp.where(_rows(a) == 0, 0.0, pltpu.roll(a, 1, 0))


def az(a):
    n = a.shape[0]
    return jnp.where(_rows(a) == n - 1, 0.0, pltpu.roll(a, n - 1, 0))


def by(a):
    return jnp.where(_lanes(a) == 0, 0.0, pltpu.roll(a, 1, 1))


def ay(a):
    n = a.shape[1]
    return jnp.where(_lanes(a) == n - 1, 0.0, pltpu.roll(a, n - 1, 1))


def pack_kernel(air_ref, vel_ref, st_ref, b_ref, tl_out, tr_out):
    width = air_ref.shape[1]
    az_n = air_ref.shape[2]
    gz = vel_ref.shape[2]
    left = [st_ref[f, 0] for f in (0, 3, 4, 1, 5, 2)] + [vel_ref[1, 0], vel_ref[2, 0]]
    for k, value in enumerate(left):
        tl_out[pl.ds(k * gz, gz), :] = value
    tl_out[pl.ds(8 * gz, az_n), :] = air_ref[0, 0]
    tl_out[pl.ds(8 * gz + az_n, gz), :] = b_ref[0]
    right = [st_ref[f, width - 1] for f in (0, 3, 4)] + [vel_ref[0, width - 1]]
    for k, value in enumerate(right):
        tr_out[pl.ds(k * gz, gz), :] = value
    o = 4 * gz
    tr_out[pl.ds(o, az_n), :] = air_ref[1, width - 2]
    for k, f in enumerate((1, 2, 3, 0)):
        tr_out[pl.ds(o + (k + 1) * az_n, az_n), :] = air_ref[f, width - 1]
    tr_out[pl.ds(o + 5 * az_n, gz), :] = b_ref[width - 1]


def run_pack(air, vel, st, b):
    gz = vel.shape[2]
    az_n = air.shape[2]
    ny = air.shape[3]
    return pl.pallas_call(
        pack_kernel,
        out_shape=(
            jax.ShapeDtypeStruct((9 * gz + az_n, ny), jnp.float32),
            jax.ShapeDtypeStruct((5 * gz + 5 * az_n, ny), jnp.float32),
        ),
        interpret=INTERPRET,
    )(air, vel, st, b)


def step_kernel(
    air_ref, bulk_ref, vel_ref, st_ref, mod_ref, b_ref, bl_ref, br_ref, fl_ref, fr_ref, coef_ref,
    keep_ref, air_out, vel_out, st_out, tl_out, tr_out,
):
    width = air_ref.shape[1]
    az_n = air_ref.shape[2]
    gz = vel_ref.shape[2]

    def fl(start, count):
        return fl_ref[pl.ds(start, count), :]

    def fr(start, count):
        return fr_ref[pl.ds(start, count), :]

    def gcol(field_ref, k, left, right):
        cols = [left] + [field_ref[k, c] for c in range(width)] + [right]
        return cols

    sxx = gcol(st_ref, 0, fl(0, gz), fr(0, gz))
    sxy = gcol(st_ref, 3, fl(gz, gz), fr(gz, gz))
    sxz = gcol(st_ref, 4, fl(2 * gz, gz), fr(2 * gz, gz))
    syy = gcol(st_ref, 1, None, fr(3 * gz, gz))
    syz = gcol(st_ref, 5, None, fr(4 * gz, gz))
    szz = gcol(st_ref, 2, None, fr(5 * gz, gz))
    vx = gcol(vel_ref, 0, fl(3 * gz, gz), None)
    vy = gcol(vel_ref, 1, None, fr(6 * gz, gz))
    vz = gcol(vel_ref, 2, None, fr(7 * gz, gz))
    bb = (
        [bl_ref[pl.ds(4 * gz + 5 * az_n, gz), :]]
        + [b_ref[c] for c in range(width)]
        + [br_ref[pl.ds(8 * gz + az_n, gz), :]]
    )
    o = 4 * gz
    pr = fr(8 * gz, az_n)
    u = [fl(o, az_n), fl(o + az_n, az_n)] + [air_ref[1, c] for c in range(width)]
    v = [None, fl(o + 2 * az_n, az_n)] + [air_ref[2, c] for c in range(width)]
    w = [None, fl(o + 3 * az_n, az_n)] + [air_ref[3, c] for c in range(width)]
    p = [None, fl(o + 4 * az_n, az_n)] + [air_ref[0, c] for c in range(width)] + [pr]

    grow = lax.broadcasted_iota(jnp.int32, (gz, sxx[1].shape[1]), 0)
    arow = lax.broadcasted_iota(jnp.int32, (az_n, sxx[1].shape[1]), 0)

    vx1 = [None] * (width + 2)
    vy1 = [None] * (width + 2)
    vz1 = [None] * (width + 2)
    for e in range(width + 2):
        if e <= width:
            force_x = sxx[e + 1] - sxx[e] + sxy[e] - by(sxy[e]) + sxz[e] - bz(sxz[e])
            vx1[e] = vx[e] + bb[e] * force_x
        if e >= 1:
            force_y = sxy[e] - sxy[e - 1] + ay(syy[e]) - syy[e] + syz[e] - bz(syz[e])
            vy1[e] = vy[e] + bb[e] * force_y
            plane = jnp.broadcast_to(p[e + 1][0:1, :], szz[e].shape)
            ghost = jnp.where(grow == gz - 1, -plane, pltpu.roll(szz[e], gz - 1, 0))
            force_z = sxz[e] - sxz[e - 1] + syz[e] - by(syz[e]) + ghost - szz[e]
            vz1[e] = vz[e] + bb[e] * force_z

    for c in range(width):
        e = c + 1
        mx, my, mz = vx1[e], vy1[e], vz1[e]
        lam = mod_ref[0, c]
        mu = mod_ref[1, c]
        longitudinal = lam + 2.0 * mu
        strain_x = mx - vx1[e - 1]
        strain_y = my - by(my)
        strain_z = mz - bz(mz)
        st_out[0, c] = st_ref[0, c] + longitudinal * strain_x + lam * (strain_y + strain_z)
        st_out[1, c] = st_ref[1, c] + longitudinal * strain_y + lam * (strain_x + strain_z)
        st_out[2, c] = st_ref[2, c] + longitudinal * strain_z + lam * (strain_x + strain_y)
        st_out[3, c] = st_ref[3, c] + mu * (ay(mx) - mx + vy1[e + 1] - my)
        sxz1 = st_ref[4, c] + mu * (az(mx) - mx + vz1[e + 1] - mz)
        syz1 = st_ref[5, c] + mu * (az(my) - my + ay(mz) - mz)
        st_out[4, c] = jnp.where(grow == gz - 1, 0.0, sxz1)
        st_out[5, c] = jnp.where(grow == gz - 1, 0.0, syz1)
        vel_out[0, c] = mx
        vel_out[1, c] = my
        vel_out[2, c] = mz
        if c == 0:
            for k, (ref, f) in enumerate(
                [(st_out, 0), (st_out, 3), (st_out, 4), (st_out, 1), (st_out, 5), (st_out, 2),
                 (vel_out, 1), (vel_out, 2)]
            ):
                tl_out[pl.ds(k * gz, gz), :] = ref[f, 0]
        if c == width - 1:
            for k, (ref, f) in enumerate([(st_out, 0), (st_out, 3), (st_out, 4), (vel_out, 0)]):
                tr_out[pl.ds(k * gz, gz), :] = ref[f, c]

    wind_x = coef_ref[0]
    wind_y = coef_ref[1]
    lift = coef_ref[2]
    u1 = [None] * (width + 2)
    for a in range(1, width + 2):
        u1[a] = (
            u[a]
            - wind_x * (u[a] - u[a - 1])
            - wind_y * (u[a] - by(u[a]))
            - lift * (p[a + 1] - p[a])
        )
    u1[1] = jnp.where(keep_ref[...] > 0.5, u1[1], 0.0)
    for c in range(width):
        a = c + 2
        v1 = v[a] - wind_x * (v[a] - v[a - 1]) - wind_y * (v[a] - by(v[a])) - lift * (ay(p[a]) - p[a])
        w1 = w[a] - wind_x * (w[a] - w[a - 1]) - wind_y * (w[a] - by(w[a])) - lift * (p[a] - bz(p[a]))
        surface = jnp.broadcast_to(vz1[c + 1][gz - 1 : gz, :], w1.shape)
        w1 = jnp.where(arow == 0, surface, w1)
        pm = p[a]
        p1 = (
            pm
            - wind_x * (pm - p[a - 1])
            - wind_y * (pm - by(pm))
            - bulk_ref[4, c] * ((u1[a] - u1[a - 1]) + (v1 - by(v1)) + (az(w1) - w1))
        )
        air_out[0, c] = p1
        air_out[1, c] = u1[a]
        air_out[2, c] = v1
        air_out[3, c] = w1
        if c == 0:
            tl_out[pl.ds(8 * gz, az_n), :] = p1
        if c == width - 2:
            tr_out[pl.ds(4 * gz, az_n), :] = u1[a]
        if c == width - 1:
            o = 4 * gz
            tr_out[pl.ds(o + az_n, az_n), :] = u1[a]
            tr_out[pl.ds(o + 2 * az_n, az_n), :] = v1
            tr_out[pl.ds(o + 3 * az_n, az_n), :] = w1
            tr_out[pl.ds(o + 4 * az_n, az_n), :] = p1


def run_step(air, bulk, vel, st, mod, b, b_left, b_right, from_left, from_right, coef, keep):
    return pl.pallas_call(
        step_kernel,
        out_shape=(
            jax.ShapeDtypeStruct((4,) + air.shape[1:], jnp.float32),
            jax.ShapeDtypeStruct(vel.shape, jnp.float32),
            jax.ShapeDtypeStruct(st.shape, jnp.float32),
            jax.ShapeDtypeStruct((8 * st.shape[2] + air.shape[2], air.shape[3]), jnp.float32),
            jax.ShapeDtypeStruct((4 * st.shape[2] + 5 * air.shape[2], air.shape[3]), jnp.float32),
        ),
        interpret=INTERPRET,
    )(air, bulk, vel, st, mod, b, b_left, b_right, from_left, from_right, coef, keep)


def body(air_state, air_bulk, air_buoyancy, air_wind, ground_state, ground_moduli, ground_buoyancy):
    west_edge = (lax.axis_index("px") == 0) & (lax.axis_index("py") == 0)
    moved = to_strips(jnp.concatenate([air_state, air_bulk[None]], 0))
    air = moved
    width = air.shape[1]
    az_n = air.shape[2]
    ny = air.shape[3]
    ground = ground_state.transpose(0, 2, 1, 3)
    gz = ground.shape[2]
    vel = ground[:3]
    st = ground[3:]
    top = lax.broadcasted_iota(jnp.int32, st.shape, 2) == gz - 1
    clear = top & (lax.broadcasted_iota(jnp.int32, st.shape, 0) >= 4)
    st = jnp.where(clear, jnp.zeros_like(st), st)
    mod = ground_moduli.transpose(0, 2, 1, 3)
    b = ground_buoyancy.transpose(1, 0, 2)
    coef = jnp.broadcast_to(
        jnp.stack([air_wind[0], air_wind[1], air_buoyancy])[:, :, None], (3, az_n, ny)
    )
    keep = jnp.broadcast_to(jnp.where(west_edge, 0.0, 1.0).astype(jnp.float32), (az_n, ny))
    to_left, to_right = run_pack(air, vel, st, b)
    for iteration in range(STEPS):
        from_left, from_right = trade(to_left, to_right)
        if iteration == 0:
            b_left, b_right = from_left, from_right
        air, vel, st, to_left, to_right = run_step(
            air, moved, vel, st, mod, b, b_left, b_right, from_left, from_right, coef, keep
        )
    ground_after = jnp.concatenate([vel, st], 0).transpose(0, 2, 1, 3)
    return (from_strips(air), ground_after)


def solution(mesh):
    placed = (
        P(None, None, "py", "px"),
        P(None, "py", "px"),
        P(),
        P(),
        P(None, None, ("px", "py"), None),
        P(None, None, ("px", "py"), None),
        P(None, ("px", "py"), None),
    )
    return jax.shard_map(
        body,
        mesh=mesh,
        in_specs=placed,
        out_specs=(P(None, None, "py", "px"), P(None, None, ("px", "py"), None)),
        check_vma=False,
    )
```

```python
import os

import jax
import jax.numpy as jnp
from jax import lax
from jax.experimental import pallas as pl
from jax.experimental.pallas import tpu as pltpu
from jax.sharding import PartitionSpec as P

STEPS = 3
RING = ("px", "py")
INTERPRET = os.environ.get("STENCIL_INTERPRET") == "1"


def trade(to_left, to_right):
    n = lax.axis_size(RING)
    from_right = lax.ppermute(to_left, RING, [(i, i - 1) for i in range(1, n)])
    from_left = lax.ppermute(to_right, RING, [(i, i + 1) for i in range(n - 1)])
    return from_left, from_right


def to_strips(block):
    f, z, ny, nx = block.shape
    parts = lax.axis_size("py")
    split = block.reshape(f, z, ny, parts, nx // parts)
    moved = lax.all_to_all(split, "py", 3, 3, tiled=True)
    return moved.transpose(0, 4, 1, 3, 2).reshape(f, nx // parts, z, parts * ny)


def from_strips(strip):
    f, nx, z, ny_all = strip.shape
    parts = lax.axis_size("py")
    split = strip.reshape(f, nx, z, parts, ny_all // parts)
    moved = lax.all_to_all(split, "py", 3, 3, tiled=True)
    return moved.transpose(0, 2, 4, 3, 1).reshape(f, z, ny_all // parts, parts * nx)


def _rows(a):
    return lax.broadcasted_iota(jnp.int32, a.shape, 0)


def _lanes(a):
    return lax.broadcasted_iota(jnp.int32, a.shape, 1)


def bz(a):
    return jnp.where(_rows(a) == 0, 0.0, pltpu.roll(a, 1, 0))


def az(a):
    n = a.shape[0]
    return jnp.where(_rows(a) == n - 1, 0.0, pltpu.roll(a, n - 1, 0))


def by(a):
    return jnp.where(_lanes(a) == 0, 0.0, pltpu.roll(a, 1, 1))


def ay(a):
    n = a.shape[1]
    return jnp.where(_lanes(a) == n - 1, 0.0, pltpu.roll(a, n - 1, 1))


def pack_kernel(air_ref, vel_ref, st_ref, b_ref, tl_out, tr_out):
    width = air_ref.shape[1]
    az_n = air_ref.shape[2]
    gz = vel_ref.shape[2]
    left = [st_ref[f, 0] for f in (0, 3, 4, 1, 5, 2)] + [vel_ref[1, 0], vel_ref[2, 0]]
    for k, value in enumerate(left):
        tl_out[pl.ds(k * gz, gz), :] = value
    tl_out[pl.ds(8 * gz, az_n), :] = air_ref[0, 0]
    tl_out[pl.ds(8 * gz + az_n, gz), :] = b_ref[0]
    right = [st_ref[f, width - 1] for f in (0, 3, 4)] + [vel_ref[0, width - 1]]
    for k, value in enumerate(right):
        tr_out[pl.ds(k * gz, gz), :] = value
    o = 4 * gz
    tr_out[pl.ds(o, az_n), :] = air_ref[1, width - 2]
    for k, f in enumerate((1, 2, 3, 0)):
        tr_out[pl.ds(o + (k + 1) * az_n, az_n), :] = air_ref[f, width - 1]
    tr_out[pl.ds(o + 5 * az_n, gz), :] = b_ref[width - 1]


def run_pack(air, vel, st, b):
    gz = vel.shape[2]
    az_n = air.shape[2]
    ny = air.shape[3]
    return pl.pallas_call(
        pack_kernel,
        out_shape=(
            jax.ShapeDtypeStruct((9 * gz + az_n, ny), jnp.float32),
            jax.ShapeDtypeStruct((5 * gz + 5 * az_n, ny), jnp.float32),
        ),
        interpret=INTERPRET,
    )(air, vel, st, b)


def make_step_kernel(edge):
    def kernel(
        air_ref, bulk_ref, vel_ref, st_ref, mod_ref, b_ref, bl_ref, br_ref, fl_ref, fr_ref,
        coef_ref, keep_ref, *outs,
    ):
        width = air_ref.shape[1]
        az_n = air_ref.shape[2]
        gz = vel_ref.shape[2]
        ny = air_ref.shape[3]

        def fl(start, count):
            return fl_ref[pl.ds(start, count), :]

        def fr(start, count):
            return fr_ref[pl.ds(start, count), :]

        grow = lax.broadcasted_iota(jnp.int32, (gz, ny), 0)
        arow = lax.broadcasted_iota(jnp.int32, (az_n, ny), 0)
        cache = {}

        def memo(fn):
            def wrapped(*key):
                full = (fn.__name__,) + key
                if full not in cache:
                    cache[full] = fn(*key)
                return cache[full]

            return wrapped

        halo_l = {0: 0, 3: gz, 4: 2 * gz}
        halo_r = {0: 0, 3: gz, 4: 2 * gz, 1: 3 * gz, 5: 4 * gz, 2: 5 * gz}

        @memo
        def st(f, e):
            if e == 0:
                return fl(halo_l[f], gz)
            if e == width + 1:
                return fr(halo_r[f], gz)
            return st_ref[f, e - 1]

        @memo
        def vel(f, e):
            if e == 0:
                return fl(3 * gz, gz)
            if e == width + 1:
                return fr((6 + f - 1) * gz, gz)
            return vel_ref[f, e - 1]

        @memo
        def bb(e):
            if e == 0:
                return bl_ref[pl.ds(4 * gz + 5 * az_n, gz), :]
            if e == width + 1:
                return br_ref[pl.ds(8 * gz + az_n, gz), :]
            return b_ref[e - 1]

        @memo
        def air(f, a):
            o = 4 * gz
            if a == width + 2:
                return fr(8 * gz, az_n)
            if a < 2:
                if f == 1:
                    return fl(o + a * az_n, az_n)
                return fl(o + {2: 2, 3: 3, 0: 4}[f] * az_n, az_n)
            return air_ref[f, a - 2]

        @memo
        def vx1(e):
            force_x = (
                st(0, e + 1) - st(0, e) + st(3, e) - by(st(3, e)) + st(4, e) - bz(st(4, e))
            )
            return vel(0, e) + bb(e) * force_x

        @memo
        def vy1(e):
            force_y = (
                st(3, e) - st(3, e - 1) + ay(st(1, e)) - st(1, e) + st(5, e) - bz(st(5, e))
            )
            return vel(1, e) + bb(e) * force_y

        @memo
        def vz1(e):
            szz = st(2, e)
            plane = jnp.broadcast_to(air(0, e + 1)[0:1, :], szz.shape)
            ghost = jnp.where(grow == gz - 1, -plane, pltpu.roll(szz, gz - 1, 0))
            force_z = st(4, e) - st(4, e - 1) + st(5, e) - by(st(5, e)) + ghost - szz
            return vel(2, e) + bb(e) * force_z

        @memo
        def stress1(c):
            e = c + 1
            mx, my, mz = vx1(e), vy1(e), vz1(e)
            lam = mod_ref[0, c]
            mu = mod_ref[1, c]
            longitudinal = lam + 2.0 * mu
            strain_x = mx - vx1(e - 1)
            strain_y = my - by(my)
            strain_z = mz - bz(mz)
            sxx = st_ref[0, c] + longitudinal * strain_x + lam * (strain_y + strain_z)
            syy = st_ref[1, c] + longitudinal * strain_y + lam * (strain_x + strain_z)
            szz = st_ref[2, c] + longitudinal * strain_z + lam * (strain_x + strain_y)
            sxy = st_ref[3, c] + mu * (ay(mx) - mx + vy1(e + 1) - my)
            sxz = st_ref[4, c] + mu * (az(mx) - mx + vz1(e + 1) - mz)
            syz = st_ref[5, c] + mu * (az(my) - my + ay(mz) - mz)
            sxz = jnp.where(grow == gz - 1, 0.0, sxz)
            syz = jnp.where(grow == gz - 1, 0.0, syz)
            return (sxx, syy, szz, sxy, sxz, syz)

        wind_x = coef_ref[0]
        wind_y = coef_ref[1]
        lift = coef_ref[2]

        @memo
        def u1(a):
            u = air(1, a)
            value = (
                u
                - wind_x * (u - air(1, a - 1))
                - wind_y * (u - by(u))
                - lift * (air(0, a + 1) - air(0, a))
            )
            if a == 1:
                value = jnp.where(keep_ref[...] > 0.5, value, 0.0)
            return value

        @memo
        def air1(c):
            a = c + 2
            v, w, p = air(2, a), air(3, a), air(0, a)
            v1 = v - wind_x * (v - air(2, a - 1)) - wind_y * (v - by(v)) - lift * (ay(p) - p)
            w1 = w - wind_x * (w - air(3, a - 1)) - wind_y * (w - by(w)) - lift * (p - bz(p))
            surface = jnp.broadcast_to(vz1(c + 1)[gz - 1 : gz, :], w1.shape)
            w1 = jnp.where(arow == 0, surface, w1)
            p1 = (
                p
                - wind_x * (p - air(0, a - 1))
                - wind_y * (p - by(p))
                - bulk_ref[4, c] * ((u1(a) - u1(a - 1)) + (v1 - by(v1)) + (az(w1) - w1))
            )
            return (p1, u1(a), v1, w1)

        if edge:
            tl_out, tr_out = outs
            first = stress1(0)
            left = [first[f] for f in (0, 3, 4, 1, 5, 2)] + [vy1(1), vz1(1)]
            for k, value in enumerate(left):
                tl_out[pl.ds(k * gz, gz), :] = value
            tl_out[pl.ds(8 * gz, az_n), :] = air1(0)[0]
            last = stress1(width - 1)
            right = [last[f] for f in (0, 3, 4)] + [vx1(width)]
            for k, value in enumerate(right):
                tr_out[pl.ds(k * gz, gz), :] = value
            o = 4 * gz
            tr_out[pl.ds(o, az_n), :] = air1(width - 2)[1]
            final = air1(width - 1)
            for k, f in enumerate((1, 2, 3, 0)):
                tr_out[pl.ds(o + (k + 1) * az_n, az_n), :] = final[f]
        else:
            air_out, vel_out, st_out = outs
            for c in range(width):
                new_st = stress1(c)
                for f in range(6):
                    st_out[f, c] = new_st[f]
                vel_out[0, c] = vx1(c + 1)
                vel_out[1, c] = vy1(c + 1)
                vel_out[2, c] = vz1(c + 1)
                new_air = air1(c)
                for f in range(4):
                    air_out[f, c] = new_air[f]

    return kernel


def run_step(air, bulk, vel, st, mod, b, b_left, b_right, from_left, from_right, coef, keep, edge):
    gz = st.shape[2]
    az_n = air.shape[2]
    ny = air.shape[3]
    if edge:
        shapes = (
            jax.ShapeDtypeStruct((8 * gz + az_n, ny), jnp.float32),
            jax.ShapeDtypeStruct((4 * gz + 5 * az_n, ny), jnp.float32),
        )
    else:
        shapes = (
            jax.ShapeDtypeStruct((4,) + air.shape[1:], jnp.float32),
            jax.ShapeDtypeStruct(vel.shape, jnp.float32),
            jax.ShapeDtypeStruct(st.shape, jnp.float32),
        )
    return pl.pallas_call(
        make_step_kernel(edge),
        out_shape=shapes,
        interpret=INTERPRET,
    )(air, bulk, vel, st, mod, b, b_left, b_right, from_left, from_right, coef, keep)


def body(air_state, air_bulk, air_buoyancy, air_wind, ground_state, ground_moduli, ground_buoyancy):
    west_edge = (lax.axis_index("px") == 0) & (lax.axis_index("py") == 0)
    moved = to_strips(jnp.concatenate([air_state, air_bulk[None]], 0))
    air = moved
    width = air.shape[1]
    az_n = air.shape[2]
    ny = air.shape[3]
    ground = ground_state.transpose(0, 2, 1, 3)
    gz = ground.shape[2]
    vel = ground[:3]
    st = ground[3:]
    top = lax.broadcasted_iota(jnp.int32, st.shape, 2) == gz - 1
    clear = top & (lax.broadcasted_iota(jnp.int32, st.shape, 0) >= 4)
    st = jnp.where(clear, jnp.zeros_like(st), st)
    mod = ground_moduli.transpose(0, 2, 1, 3)
    b = ground_buoyancy.transpose(1, 0, 2)
    coef = jnp.broadcast_to(
        jnp.stack([air_wind[0], air_wind[1], air_buoyancy])[:, :, None], (3, az_n, ny)
    )
    keep = jnp.broadcast_to(jnp.where(west_edge, 0.0, 1.0).astype(jnp.float32), (az_n, ny))
    to_left, to_right = run_pack(air, vel, st, b)
    for iteration in range(STEPS):
        from_left, from_right = trade(to_left, to_right)
        if iteration == 0:
            b_left, b_right = from_left, from_right
        operands = (air, moved, vel, st, mod, b, b_left, b_right, from_left, from_right, coef, keep)
        if iteration + 1 < STEPS:
            to_left, to_right = run_step(*operands, edge=True)
        air, vel, st = run_step(*operands, edge=False)
    ground_after = jnp.concatenate([vel, st], 0).transpose(0, 2, 1, 3)
    return (from_strips(air), ground_after)


def solution(mesh):
    placed = (
        P(None, None, "py", "px"),
        P(None, "py", "px"),
        P(),
        P(),
        P(None, None, ("px", "py"), None),
        P(None, None, ("px", "py"), None),
        P(None, ("px", "py"), None),
    )
    return jax.shard_map(
        body,
        mesh=mesh,
        in_specs=placed,
        out_specs=(P(None, None, "py", "px"), P(None, None, ("px", "py"), None)),
        check_vma=False,
    )
```

```python
import os

import jax
import jax.numpy as jnp
from jax import lax
from jax.experimental import pallas as pl
from jax.experimental.pallas import tpu as pltpu
from jax.sharding import PartitionSpec as P

STEPS = 3
RING = ("px", "py")
INTERPRET = os.environ.get("STENCIL_INTERPRET") == "1"


def trade(to_left, to_right):
    n = lax.axis_size(RING)
    from_right = lax.ppermute(to_left, RING, [(i, i - 1) for i in range(1, n)])
    from_left = lax.ppermute(to_right, RING, [(i, i + 1) for i in range(n - 1)])
    return from_left, from_right


def to_strips(block):
    f, z, ny, nx = block.shape
    parts = lax.axis_size("py")
    split = block.reshape(f, z, ny, parts, nx // parts)
    moved = lax.all_to_all(split, "py", 3, 3, tiled=True)
    return moved.transpose(0, 4, 1, 3, 2).reshape(f, nx // parts, z, parts * ny)


def from_strips(strip):
    f, nx, z, ny_all = strip.shape
    parts = lax.axis_size("py")
    split = strip.reshape(f, nx, z, parts, ny_all // parts)
    moved = lax.all_to_all(split, "py", 3, 3, tiled=True)
    return moved.transpose(0, 2, 4, 3, 1).reshape(f, z, ny_all // parts, parts * nx)


def _rows(a):
    return lax.broadcasted_iota(jnp.int32, a.shape, 0)


def _lanes(a):
    return lax.broadcasted_iota(jnp.int32, a.shape, 1)


def bz(a):
    return jnp.where(_rows(a) == 0, 0.0, pltpu.roll(a, 1, 0))


def az(a):
    n = a.shape[0]
    return jnp.where(_rows(a) == n - 1, 0.0, pltpu.roll(a, n - 1, 0))


def by(a):
    return jnp.where(_lanes(a) == 0, 0.0, pltpu.roll(a, 1, 1))


def ay(a):
    n = a.shape[1]
    return jnp.where(_lanes(a) == n - 1, 0.0, pltpu.roll(a, n - 1, 1))


def pack_kernel(air_ref, vel_ref, st_ref, b_ref, tl_out, tr_out):
    width = air_ref.shape[1]
    az_n = air_ref.shape[2]
    gz = vel_ref.shape[2]
    left = [st_ref[f, 0] for f in (0, 3, 4, 1, 5, 2)] + [vel_ref[1, 0], vel_ref[2, 0]]
    for k, value in enumerate(left):
        tl_out[pl.ds(k * gz, gz), :] = value
    tl_out[pl.ds(8 * gz, az_n), :] = air_ref[0, 0]
    tl_out[pl.ds(8 * gz + az_n, gz), :] = b_ref[0]
    right = [st_ref[f, width - 1] for f in (0, 3, 4)] + [vel_ref[0, width - 1]]
    for k, value in enumerate(right):
        tr_out[pl.ds(k * gz, gz), :] = value
    o = 4 * gz
    tr_out[pl.ds(o, az_n), :] = air_ref[1, width - 2]
    for k, f in enumerate((1, 2, 3, 0)):
        tr_out[pl.ds(o + (k + 1) * az_n, az_n), :] = air_ref[f, width - 1]
    tr_out[pl.ds(o + 5 * az_n, gz), :] = b_ref[width - 1]


def run_pack(air, vel, st, b):
    gz = vel.shape[2]
    az_n = air.shape[2]
    ny = air.shape[3]
    return pl.pallas_call(
        pack_kernel,
        out_shape=(
            jax.ShapeDtypeStruct((9 * gz + az_n, ny), jnp.float32),
            jax.ShapeDtypeStruct((5 * gz + 5 * az_n, ny), jnp.float32),
        ),
        interpret=INTERPRET,
    )(air, vel, st, b)


def step_kernel(
    air_ref, bulk_ref, vel_ref, st_ref, mod_ref, b_ref, bl_ref, br_ref, fl_ref, fr_ref, scal_ref,
    air_out, vel_out, st_out, tl_out, tr_out, coef_ref,
):
    width = air_ref.shape[1]
    az_n = air_ref.shape[2]
    gz = vel_ref.shape[2]
    ny = air_ref.shape[3]
    for k in range(3):
        for z in range(az_n):
            coef_ref[k, pl.ds(z, 1), :] = jnp.full((1, ny), scal_ref[k * az_n + z], jnp.float32)

    def fl(start, count):
        return fl_ref[pl.ds(start, count), :]

    def fr(start, count):
        return fr_ref[pl.ds(start, count), :]

    def gcol(field_ref, k, left, right):
        cols = [left] + [field_ref[k, c] for c in range(width)] + [right]
        return cols

    sxx = gcol(st_ref, 0, fl(0, gz), fr(0, gz))
    sxy = gcol(st_ref, 3, fl(gz, gz), fr(gz, gz))
    sxz = gcol(st_ref, 4, fl(2 * gz, gz), fr(2 * gz, gz))
    syy = gcol(st_ref, 1, None, fr(3 * gz, gz))
    syz = gcol(st_ref, 5, None, fr(4 * gz, gz))
    szz = gcol(st_ref, 2, None, fr(5 * gz, gz))
    vx = gcol(vel_ref, 0, fl(3 * gz, gz), None)
    vy = gcol(vel_ref, 1, None, fr(6 * gz, gz))
    vz = gcol(vel_ref, 2, None, fr(7 * gz, gz))
    bb = (
        [bl_ref[pl.ds(4 * gz + 5 * az_n, gz), :]]
        + [b_ref[c] for c in range(width)]
        + [br_ref[pl.ds(8 * gz + az_n, gz), :]]
    )
    o = 4 * gz
    pr = fr(8 * gz, az_n)
    u = [fl(o, az_n), fl(o + az_n, az_n)] + [air_ref[1, c] for c in range(width)]
    v = [None, fl(o + 2 * az_n, az_n)] + [air_ref[2, c] for c in range(width)]
    w = [None, fl(o + 3 * az_n, az_n)] + [air_ref[3, c] for c in range(width)]
    p = [None, fl(o + 4 * az_n, az_n)] + [air_ref[0, c] for c in range(width)] + [pr]

    grow = lax.broadcasted_iota(jnp.int32, (gz, sxx[1].shape[1]), 0)
    arow = lax.broadcasted_iota(jnp.int32, (az_n, sxx[1].shape[1]), 0)

    vx1 = [None] * (width + 2)
    vy1 = [None] * (width + 2)
    vz1 = [None] * (width + 2)
    for e in range(width + 2):
        if e <= width:
            force_x = sxx[e + 1] - sxx[e] + sxy[e] - by(sxy[e]) + sxz[e] - bz(sxz[e])
            vx1[e] = vx[e] + bb[e] * force_x
        if e >= 1:
            force_y = sxy[e] - sxy[e - 1] + ay(syy[e]) - syy[e] + syz[e] - bz(syz[e])
            vy1[e] = vy[e] + bb[e] * force_y
            plane = jnp.broadcast_to(p[e + 1][0:1, :], szz[e].shape)
            ghost = jnp.where(grow == gz - 1, -plane, pltpu.roll(szz[e], gz - 1, 0))
            force_z = sxz[e] - sxz[e - 1] + syz[e] - by(syz[e]) + ghost - szz[e]
            vz1[e] = vz[e] + bb[e] * force_z

    for c in range(width):
        e = c + 1
        mx, my, mz = vx1[e], vy1[e], vz1[e]
        lam = mod_ref[0, c]
        mu = mod_ref[1, c]
        longitudinal = lam + 2.0 * mu
        strain_x = mx - vx1[e - 1]
        strain_y = my - by(my)
        strain_z = mz - bz(mz)
        st_out[0, c] = st_ref[0, c] + longitudinal * strain_x + lam * (strain_y + strain_z)
        st_out[1, c] = st_ref[1, c] + longitudinal * strain_y + lam * (strain_x + strain_z)
        st_out[2, c] = st_ref[2, c] + longitudinal * strain_z + lam * (strain_x + strain_y)
        st_out[3, c] = st_ref[3, c] + mu * (ay(mx) - mx + vy1[e + 1] - my)
        sxz1 = st_ref[4, c] + mu * (az(mx) - mx + vz1[e + 1] - mz)
        syz1 = st_ref[5, c] + mu * (az(my) - my + ay(mz) - mz)
        st_out[4, c] = jnp.where(grow == gz - 1, 0.0, sxz1)
        st_out[5, c] = jnp.where(grow == gz - 1, 0.0, syz1)
        vel_out[0, c] = mx
        vel_out[1, c] = my
        vel_out[2, c] = mz
        if c == 0:
            for k, (ref, f) in enumerate(
                [(st_out, 0), (st_out, 3), (st_out, 4), (st_out, 1), (st_out, 5), (st_out, 2),
                 (vel_out, 1), (vel_out, 2)]
            ):
                tl_out[pl.ds(k * gz, gz), :] = ref[f, 0]
        if c == width - 1:
            for k, (ref, f) in enumerate([(st_out, 0), (st_out, 3), (st_out, 4), (vel_out, 0)]):
                tr_out[pl.ds(k * gz, gz), :] = ref[f, c]

    wind_x = coef_ref[0]
    wind_y = coef_ref[1]
    lift = coef_ref[2]
    u1 = [None] * (width + 2)
    for a in range(1, width + 2):
        u1[a] = (
            u[a]
            - wind_x * (u[a] - u[a - 1])
            - wind_y * (u[a] - by(u[a]))
            - lift * (p[a + 1] - p[a])
        )
    u1[1] = jnp.where(scal_ref[3 * az_n] > 0.5, u1[1], 0.0)
    for c in range(width):
        a = c + 2
        v1 = v[a] - wind_x * (v[a] - v[a - 1]) - wind_y * (v[a] - by(v[a])) - lift * (ay(p[a]) - p[a])
        w1 = w[a] - wind_x * (w[a] - w[a - 1]) - wind_y * (w[a] - by(w[a])) - lift * (p[a] - bz(p[a]))
        surface = jnp.broadcast_to(vz1[c + 1][gz - 1 : gz, :], w1.shape)
        w1 = jnp.where(arow == 0, surface, w1)
        pm = p[a]
        p1 = (
            pm
            - wind_x * (pm - p[a - 1])
            - wind_y * (pm - by(pm))
            - bulk_ref[0, c] * ((u1[a] - u1[a - 1]) + (v1 - by(v1)) + (az(w1) - w1))
        )
        air_out[0, c] = p1
        air_out[1, c] = u1[a]
        air_out[2, c] = v1
        air_out[3, c] = w1
        if c == 0:
            tl_out[pl.ds(8 * gz, az_n), :] = p1
        if c == width - 2:
            tr_out[pl.ds(4 * gz, az_n), :] = u1[a]
        if c == width - 1:
            o = 4 * gz
            tr_out[pl.ds(o + az_n, az_n), :] = u1[a]
            tr_out[pl.ds(o + 2 * az_n, az_n), :] = v1
            tr_out[pl.ds(o + 3 * az_n, az_n), :] = w1
            tr_out[pl.ds(o + 4 * az_n, az_n), :] = p1


def whole(shape):
    return pl.BlockSpec(shape, lambda i: (0,) * len(shape))


def run_step(air, bulk, vel, st, mod, b, b_left, b_right, from_left, from_right, scal):
    fields_in = (4,) + air.shape[1:]
    arrays = (vel, st, mod, b, b_left, b_right, from_left, from_right)
    outs = (
        jax.ShapeDtypeStruct(fields_in, jnp.float32),
        jax.ShapeDtypeStruct(vel.shape, jnp.float32),
        jax.ShapeDtypeStruct(st.shape, jnp.float32),
        jax.ShapeDtypeStruct((8 * st.shape[2] + air.shape[2], air.shape[3]), jnp.float32),
        jax.ShapeDtypeStruct((4 * st.shape[2] + 5 * air.shape[2], air.shape[3]), jnp.float32),
    )
    return pl.pallas_call(
        step_kernel,
        in_specs=[
            whole(fields_in),
            pl.BlockSpec((1,) + bulk.shape[1:], lambda i: (4, 0, 0, 0)),
        ]
        + [whole(a.shape) for a in arrays]
        + [pl.BlockSpec(memory_space=pltpu.SMEM)],
        out_specs=[whole(s.shape) for s in outs],
        scratch_shapes=[pltpu.VMEM((3,) + air.shape[2:], jnp.float32)],
        grid=(1,),
        out_shape=outs,
        interpret=INTERPRET,
    )(air, bulk, vel, st, mod, b, b_left, b_right, from_left, from_right, scal)


def body(air_state, air_bulk, air_buoyancy, air_wind, ground_state, ground_moduli, ground_buoyancy):
    west_edge = (lax.axis_index("px") == 0) & (lax.axis_index("py") == 0)
    moved = to_strips(jnp.concatenate([air_state, air_bulk[None]], 0))
    air = moved
    width = air.shape[1]
    az_n = air.shape[2]
    ny = air.shape[3]
    ground = ground_state.transpose(0, 2, 1, 3)
    gz = ground.shape[2]
    vel = ground[:3]
    st = ground[3:]
    top = lax.broadcasted_iota(jnp.int32, st.shape, 2) == gz - 1
    clear = top & (lax.broadcasted_iota(jnp.int32, st.shape, 0) >= 4)
    st = jnp.where(clear, jnp.zeros_like(st), st)
    mod = ground_moduli.transpose(0, 2, 1, 3)
    b = ground_buoyancy.transpose(1, 0, 2)
    scal = jnp.concatenate(
        [air_wind[0], air_wind[1], air_buoyancy, jnp.where(west_edge, 0.0, 1.0)[None]]
    ).astype(jnp.float32)
    to_left, to_right = run_pack(air, vel, st, b)
    for iteration in range(STEPS):
        from_left, from_right = trade(to_left, to_right)
        if iteration == 0:
            b_left, b_right = from_left, from_right
        air, vel, st, to_left, to_right = run_step(
            air, moved, vel, st, mod, b, b_left, b_right, from_left, from_right, scal
        )
    ground_after = jnp.concatenate([vel, st], 0).transpose(0, 2, 1, 3)
    return (from_strips(air), ground_after)


def solution(mesh):
    placed = (
        P(None, None, "py", "px"),
        P(None, "py", "px"),
        P(),
        P(),
        P(None, None, ("px", "py"), None),
        P(None, None, ("px", "py"), None),
        P(None, ("px", "py"), None),
    )
    return jax.shard_map(
        body,
        mesh=mesh,
        in_specs=placed,
        out_specs=(P(None, None, "py", "px"), P(None, None, ("px", "py"), None)),
        check_vma=False,
    )
```

```python
import functools
import os

import jax
import jax.numpy as jnp
from jax import lax
from jax.experimental import pallas as pl
from jax.experimental.pallas import tpu as pltpu
from jax.sharding import PartitionSpec as P

STEPS = 3
RING = ("px", "py")
INTERPRET = os.environ.get("STENCIL_INTERPRET") == "1"


def trade(to_left, to_right):
    n = lax.axis_size(RING)
    from_right = lax.ppermute(to_left, RING, [(i, i - 1) for i in range(1, n)])
    from_left = lax.ppermute(to_right, RING, [(i, i + 1) for i in range(n - 1)])
    return from_left, from_right


def to_strips(block):
    f, z, ny, nx = block.shape
    parts = lax.axis_size("py")
    split = block.reshape(f, z, ny, parts, nx // parts)
    moved = lax.all_to_all(split, "py", 3, 3, tiled=True)
    return moved.transpose(0, 4, 1, 3, 2).reshape(f, nx // parts, z, parts * ny)


def from_strips(strip):
    f, nx, z, ny_all = strip.shape
    parts = lax.axis_size("py")
    split = strip.reshape(f, nx, z, parts, ny_all // parts)
    moved = lax.all_to_all(split, "py", 3, 3, tiled=True)
    return moved.transpose(0, 2, 4, 3, 1).reshape(f, z, ny_all // parts, parts * nx)


def _rows(a):
    return lax.broadcasted_iota(jnp.int32, a.shape, 0)


def _lanes(a):
    return lax.broadcasted_iota(jnp.int32, a.shape, 1)


def bz(a):
    return jnp.where(_rows(a) == 0, 0.0, pltpu.roll(a, 1, 0))


def az(a):
    n = a.shape[0]
    return jnp.where(_rows(a) == n - 1, 0.0, pltpu.roll(a, n - 1, 0))


def by(a):
    return jnp.where(_lanes(a) == 0, 0.0, pltpu.roll(a, 1, 1))


def ay(a):
    n = a.shape[1]
    return jnp.where(_lanes(a) == n - 1, 0.0, pltpu.roll(a, n - 1, 1))


def one_step(
    air_ref, bulk_ref, vel_ref, st_ref, mod_ref, b_ref, bl_ref, br_ref, fl_ref, fr_ref, scal_ref,
    air_out, vel_out, st_out, tl_out, tr_out, coef_ref,
):
    width = air_ref.shape[1]
    az_n = air_ref.shape[2]
    gz = vel_ref.shape[2]

    def fl(start, count):
        return fl_ref[pl.ds(start, count), :]

    def fr(start, count):
        return fr_ref[pl.ds(start, count), :]

    def gcol(field_ref, k, left, right):
        cols = [left] + [field_ref[k, c] for c in range(width)] + [right]
        return cols

    sxx = gcol(st_ref, 0, fl(0, gz), fr(0, gz))
    sxy = gcol(st_ref, 3, fl(gz, gz), fr(gz, gz))
    sxz = gcol(st_ref, 4, fl(2 * gz, gz), fr(2 * gz, gz))
    syy = gcol(st_ref, 1, None, fr(3 * gz, gz))
    syz = gcol(st_ref, 5, None, fr(4 * gz, gz))
    szz = gcol(st_ref, 2, None, fr(5 * gz, gz))
    vx = gcol(vel_ref, 0, fl(3 * gz, gz), None)
    vy = gcol(vel_ref, 1, None, fr(6 * gz, gz))
    vz = gcol(vel_ref, 2, None, fr(7 * gz, gz))
    bb = (
        [bl_ref[pl.ds(4 * gz + 5 * az_n, gz), :]]
        + [b_ref[c] for c in range(width)]
        + [br_ref[pl.ds(8 * gz + az_n, gz), :]]
    )
    o = 4 * gz
    pr = fr(8 * gz, az_n)
    u = [fl(o, az_n), fl(o + az_n, az_n)] + [air_ref[1, c] for c in range(width)]
    v = [None, fl(o + 2 * az_n, az_n)] + [air_ref[2, c] for c in range(width)]
    w = [None, fl(o + 3 * az_n, az_n)] + [air_ref[3, c] for c in range(width)]
    p = [None, fl(o + 4 * az_n, az_n)] + [air_ref[0, c] for c in range(width)] + [pr]

    grow = lax.broadcasted_iota(jnp.int32, (gz, sxx[1].shape[1]), 0)
    arow = lax.broadcasted_iota(jnp.int32, (az_n, sxx[1].shape[1]), 0)

    vx1 = [None] * (width + 2)
    vy1 = [None] * (width + 2)
    vz1 = [None] * (width + 2)
    for e in range(width + 2):
        if e <= width:
            force_x = sxx[e + 1] - sxx[e] + sxy[e] - by(sxy[e]) + sxz[e] - bz(sxz[e])
            vx1[e] = vx[e] + bb[e] * force_x
        if e >= 1:
            force_y = sxy[e] - sxy[e - 1] + ay(syy[e]) - syy[e] + syz[e] - bz(syz[e])
            vy1[e] = vy[e] + bb[e] * force_y
            plane = jnp.broadcast_to(p[e + 1][0:1, :], szz[e].shape)
            ghost = jnp.where(grow == gz - 1, -plane, pltpu.roll(szz[e], gz - 1, 0))
            force_z = sxz[e] - sxz[e - 1] + syz[e] - by(syz[e]) + ghost - szz[e]
            vz1[e] = vz[e] + bb[e] * force_z

    for c in range(width):
        e = c + 1
        mx, my, mz = vx1[e], vy1[e], vz1[e]
        lam = mod_ref[0, c]
        mu = mod_ref[1, c]
        longitudinal = lam + 2.0 * mu
        strain_x = mx - vx1[e - 1]
        strain_y = my - by(my)
        strain_z = mz - bz(mz)
        st_out[0, c] = st_ref[0, c] + longitudinal * strain_x + lam * (strain_y + strain_z)
        st_out[1, c] = st_ref[1, c] + longitudinal * strain_y + lam * (strain_x + strain_z)
        st_out[2, c] = st_ref[2, c] + longitudinal * strain_z + lam * (strain_x + strain_y)
        st_out[3, c] = st_ref[3, c] + mu * (ay(mx) - mx + vy1[e + 1] - my)
        sxz1 = st_ref[4, c] + mu * (az(mx) - mx + vz1[e + 1] - mz)
        syz1 = st_ref[5, c] + mu * (az(my) - my + ay(mz) - mz)
        st_out[4, c] = jnp.where(grow == gz - 1, 0.0, sxz1)
        st_out[5, c] = jnp.where(grow == gz - 1, 0.0, syz1)
        vel_out[0, c] = mx
        vel_out[1, c] = my
        vel_out[2, c] = mz
        if c == 0 and tl_out is not None:
            for k, (ref, f) in enumerate(
                [(st_out, 0), (st_out, 3), (st_out, 4), (st_out, 1), (st_out, 5), (st_out, 2),
                 (vel_out, 1), (vel_out, 2)]
            ):
                tl_out[pl.ds(k * gz, gz), :] = ref[f, 0]
        if c == width - 1 and tr_out is not None:
            for k, (ref, f) in enumerate([(st_out, 0), (st_out, 3), (st_out, 4), (vel_out, 0)]):
                tr_out[pl.ds(k * gz, gz), :] = ref[f, c]

    wind_x = coef_ref[0]
    wind_y = coef_ref[1]
    lift = coef_ref[2]
    u1 = [None] * (width + 2)
    for a in range(1, width + 2):
        u1[a] = (
            u[a]
            - wind_x * (u[a] - u[a - 1])
            - wind_y * (u[a] - by(u[a]))
            - lift * (p[a + 1] - p[a])
        )
    u1[1] = jnp.where(scal_ref[3 * az_n] > 0.5, u1[1], 0.0)
    for c in range(width):
        a = c + 2
        v1 = v[a] - wind_x * (v[a] - v[a - 1]) - wind_y * (v[a] - by(v[a])) - lift * (ay(p[a]) - p[a])
        w1 = w[a] - wind_x * (w[a] - w[a - 1]) - wind_y * (w[a] - by(w[a])) - lift * (p[a] - bz(p[a]))
        surface = jnp.broadcast_to(vz1[c + 1][gz - 1 : gz, :], w1.shape)
        w1 = jnp.where(arow == 0, surface, w1)
        pm = p[a]
        p1 = (
            pm
            - wind_x * (pm - p[a - 1])
            - wind_y * (pm - by(pm))
            - bulk_ref[c] * ((u1[a] - u1[a - 1]) + (v1 - by(v1)) + (az(w1) - w1))
        )
        air_out[0, c] = p1
        air_out[1, c] = u1[a]
        air_out[2, c] = v1
        air_out[3, c] = w1
        if c == 0 and tl_out is not None:
            tl_out[pl.ds(8 * gz, az_n), :] = p1
        if c == width - 2 and tr_out is not None:
            tr_out[pl.ds(4 * gz, az_n), :] = u1[a]
        if c == width - 1 and tr_out is not None:
            o = 4 * gz
            tr_out[pl.ds(o + az_n, az_n), :] = u1[a]
            tr_out[pl.ds(o + 2 * az_n, az_n), :] = v1
            tr_out[pl.ds(o + 3 * az_n, az_n), :] = w1
            tr_out[pl.ds(o + 4 * az_n, az_n), :] = p1


MESH = pl.DeviceIdType.MESH


def fused_kernel(
    n_py, n_ring, air_ref, vel_ref, st_ref, mod_ref, b_ref, scal_ref,
    air_out, vel_out, st_out,
    air_a, vel_a, st_a, air_b, vel_b, st_b, coef_ref, send_l, send_r, recv_l, recv_r,
    send_sem, recv_sem,
):
    width = air_ref.shape[1]
    az_n = air_ref.shape[2]
    gz = vel_ref.shape[2]
    ny = air_ref.shape[3]
    me = lax.axis_index("px") * n_py + lax.axis_index("py")
    has_left = me > 0
    has_right = me < n_ring - 1
    left = ((me - 1) // n_py, (me - 1) % n_py)
    right = ((me + 1) // n_py, (me + 1) % n_py)
    rows_l = send_l.shape[1]
    rows_r = send_r.shape[1]

    @pl.when(jnp.logical_not(has_left))
    def _():
        recv_l[...] = jnp.zeros_like(recv_l)

    @pl.when(jnp.logical_not(has_right))
    def _():
        recv_r[...] = jnp.zeros_like(recv_r)

    barrier = pltpu.get_barrier_semaphore()

    @pl.when(has_left)
    def _():
        pl.semaphore_signal(barrier, inc=1, device_id=left, device_id_type=MESH)

    @pl.when(has_right)
    def _():
        pl.semaphore_signal(barrier, inc=1, device_id=right, device_id_type=MESH)

    @pl.when(has_left & has_right)
    def _():
        pl.semaphore_wait(barrier, 2)

    @pl.when(jnp.logical_not(has_left & has_right))
    def _():
        pl.semaphore_wait(barrier, 1)

    for k in range(3):
        for z in range(az_n):
            coef_ref[k, pl.ds(z, 1), :] = jnp.full((1, ny), scal_ref[k * az_n + z], jnp.float32)

    tl = send_l.at[0]
    tr = send_r.at[0]
    left_rows = [st_ref[f, 0] for f in (0, 3, 4, 1, 5, 2)] + [vel_ref[1, 0], vel_ref[2, 0]]
    for k, value in enumerate(left_rows):
        tl[pl.ds(k * gz, gz), :] = value
    tl[pl.ds(8 * gz, az_n), :] = air_ref[0, 0]
    tl[pl.ds(8 * gz + az_n, gz), :] = b_ref[0]
    right_rows = [st_ref[f, width - 1] for f in (0, 3, 4)] + [vel_ref[0, width - 1]]
    for k, value in enumerate(right_rows):
        tr[pl.ds(k * gz, gz), :] = value
    o = 4 * gz
    tr[pl.ds(o, az_n), :] = air_ref[1, width - 2]
    for k, f in enumerate((1, 2, 3, 0)):
        tr[pl.ds(o + (k + 1) * az_n, az_n), :] = air_ref[f, width - 1]
    tr[pl.ds(o + 5 * az_n, gz), :] = b_ref[width - 1]

    def exchange(n, count_l, count_r):
        to_left = pltpu.make_async_remote_copy(
            src_ref=send_l.at[n, pl.ds(0, count_l)],
            dst_ref=recv_r.at[n, pl.ds(0, count_l)],
            send_sem=send_sem.at[n, 0],
            recv_sem=recv_sem.at[n, 1],
            device_id=left,
            device_id_type=MESH,
        )
        to_right = pltpu.make_async_remote_copy(
            src_ref=send_r.at[n, pl.ds(0, count_r)],
            dst_ref=recv_l.at[n, pl.ds(0, count_r)],
            send_sem=send_sem.at[n, 1],
            recv_sem=recv_sem.at[n, 0],
            device_id=right,
            device_id_type=MESH,
        )

        @pl.when(has_left)
        def _():
            to_left.start()

        @pl.when(has_right)
        def _():
            to_right.start()

        @pl.when(has_left)
        def _():
            to_left.wait_send()
            to_right.wait_recv()

        @pl.when(has_right)
        def _():
            to_right.wait_send()
            to_left.wait_recv()

    full_l = 8 * gz + az_n
    full_r = 4 * gz + 5 * az_n
    exchange(0, rows_l, rows_r)
    states = [
        (air_ref, vel_ref, st_ref),
        (air_a, vel_a, st_a),
        (air_b, vel_b, st_b),
        (air_out, vel_out, st_out),
    ]
    for n in range(STEPS):
        src = states[n] if n < len(states) - 1 else states[-2]
        dst = states[n + 1] if n + 1 < STEPS else states[-1]
        last = n + 1 == STEPS
        one_step(
            src[0], air_ref.at[4], src[1], src[2], mod_ref, b_ref, recv_l.at[0], recv_r.at[0],
            recv_l.at[n], recv_r.at[n], scal_ref, dst[0], dst[1], dst[2],
            None if last else send_l.at[n + 1], None if last else send_r.at[n + 1], coef_ref,
        )
        if not last:
            exchange(n + 1, full_l, full_r)


def fused(air, vel, st, mod, b, scal):
    n_py = lax.axis_size("py")
    n_ring = lax.axis_size(RING)
    gz = st.shape[2]
    az_n = air.shape[2]
    ny = air.shape[3]
    fields = (4,) + air.shape[1:]
    rows_l = 9 * gz + az_n
    rows_r = 5 * gz + 5 * az_n
    vmem = pl.BlockSpec(memory_space=pltpu.VMEM)
    return pl.pallas_call(
        functools.partial(fused_kernel, n_py, n_ring),
        out_shape=(
            jax.ShapeDtypeStruct(fields, jnp.float32),
            jax.ShapeDtypeStruct(vel.shape, jnp.float32),
            jax.ShapeDtypeStruct(st.shape, jnp.float32),
        ),
        in_specs=[vmem] * 5 + [pl.BlockSpec(memory_space=pltpu.SMEM)],
        out_specs=(vmem, vmem, vmem),
        scratch_shapes=[
            pltpu.VMEM(fields, jnp.float32),
            pltpu.VMEM(vel.shape, jnp.float32),
            pltpu.VMEM(st.shape, jnp.float32),
            pltpu.VMEM(fields, jnp.float32),
            pltpu.VMEM(vel.shape, jnp.float32),
            pltpu.VMEM(st.shape, jnp.float32),
            pltpu.VMEM((3, az_n, ny), jnp.float32),
            pltpu.VMEM((STEPS, rows_l, ny), jnp.float32),
            pltpu.VMEM((STEPS, rows_r, ny), jnp.float32),
            pltpu.VMEM((STEPS, rows_r, ny), jnp.float32),
            pltpu.VMEM((STEPS, rows_l, ny), jnp.float32),
            pltpu.SemaphoreType.DMA((STEPS, 2)),
            pltpu.SemaphoreType.DMA((STEPS, 2)),
        ],
        compiler_params=pltpu.CompilerParams(collective_id=0, has_side_effects=True),
        interpret=INTERPRET,
    )(air, vel, st, mod, b, scal)


def body(air_state, air_bulk, air_buoyancy, air_wind, ground_state, ground_moduli, ground_buoyancy):
    west_edge = (lax.axis_index("px") == 0) & (lax.axis_index("py") == 0)
    moved = to_strips(jnp.concatenate([air_state, air_bulk[None]], 0))
    ground = ground_state.transpose(0, 2, 1, 3)
    gz = ground.shape[2]
    vel = ground[:3]
    st = ground[3:]
    top = lax.broadcasted_iota(jnp.int32, st.shape, 2) == gz - 1
    clear = top & (lax.broadcasted_iota(jnp.int32, st.shape, 0) >= 4)
    st = jnp.where(clear, jnp.zeros_like(st), st)
    mod = ground_moduli.transpose(0, 2, 1, 3)
    b = ground_buoyancy.transpose(1, 0, 2)
    scal = jnp.concatenate(
        [air_wind[0], air_wind[1], air_buoyancy, jnp.where(west_edge, 0.0, 1.0)[None]]
    ).astype(jnp.float32)
    air, vel, st = fused(moved, vel, st, mod, b, scal)
    ground_after = jnp.concatenate([vel, st], 0).transpose(0, 2, 1, 3)
    return (from_strips(air), ground_after)


def solution(mesh):
    placed = (
        P(None, None, "py", "px"),
        P(None, "py", "px"),
        P(),
        P(),
        P(None, None, ("px", "py"), None),
        P(None, None, ("px", "py"), None),
        P(None, ("px", "py"), None),
    )
    return jax.shard_map(
        body,
        mesh=mesh,
        in_specs=placed,
        out_specs=(P(None, None, "py", "px"), P(None, None, ("px", "py"), None)),
        check_vma=False,
    )
```

```python
import functools
import os

import jax
import jax.numpy as jnp
from jax import lax
from jax.experimental import pallas as pl
from jax.experimental.pallas import tpu as pltpu
from jax.sharding import PartitionSpec as P

STEPS = 3
RING = ("px", "py")
INTERPRET = os.environ.get("STENCIL_INTERPRET") == "1"


def trade(to_left, to_right):
    n = lax.axis_size(RING)
    from_right = lax.ppermute(to_left, RING, [(i, i - 1) for i in range(1, n)])
    from_left = lax.ppermute(to_right, RING, [(i, i + 1) for i in range(n - 1)])
    return from_left, from_right


def to_strips(block):
    f, z, ny, nx = block.shape
    parts = lax.axis_size("py")
    split = block.reshape(f, z, ny, parts, nx // parts)
    moved = lax.all_to_all(split, "py", 3, 3, tiled=True)
    return moved.transpose(0, 4, 1, 3, 2).reshape(f, nx // parts, z, parts * ny)


def from_strips(strip):
    f, nx, z, ny_all = strip.shape
    parts = lax.axis_size("py")
    split = strip.reshape(f, nx, z, parts, ny_all // parts)
    moved = lax.all_to_all(split, "py", 3, 3, tiled=True)
    return moved.transpose(0, 2, 4, 3, 1).reshape(f, z, ny_all // parts, parts * nx)


def _rows(a):
    return lax.broadcasted_iota(jnp.int32, a.shape, 0)


def _lanes(a):
    return lax.broadcasted_iota(jnp.int32, a.shape, 1)


def bz(a):
    return jnp.where(_rows(a) == 0, 0.0, pltpu.roll(a, 1, 0))


def az(a):
    n = a.shape[0]
    return jnp.where(_rows(a) == n - 1, 0.0, pltpu.roll(a, n - 1, 0))


def by(a):
    return jnp.where(_lanes(a) == 0, 0.0, pltpu.roll(a, 1, 1))


def ay(a):
    n = a.shape[1]
    return jnp.where(_lanes(a) == n - 1, 0.0, pltpu.roll(a, n - 1, 1))


def one_step(
    air_ref, bulk_ref, vel_ref, st_ref, mod_ref, b_ref, bl_ref, br_ref, fl_ref, fr_ref, scal_ref,
    air_out, vel_out, st_out, tl_out, tr_out, coef_ref, after_edges=None,
):
    width = air_ref.shape[1]
    az_n = air_ref.shape[2]
    gz = vel_ref.shape[2]

    def fl(start, count):
        return fl_ref[pl.ds(start, count), :]

    def fr(start, count):
        return fr_ref[pl.ds(start, count), :]

    def gcol(field_ref, k, left, right):
        cols = [left] + [field_ref[k, c] for c in range(width)] + [right]
        return cols

    sxx = gcol(st_ref, 0, fl(0, gz), fr(0, gz))
    sxy = gcol(st_ref, 3, fl(gz, gz), fr(gz, gz))
    sxz = gcol(st_ref, 4, fl(2 * gz, gz), fr(2 * gz, gz))
    syy = gcol(st_ref, 1, None, fr(3 * gz, gz))
    syz = gcol(st_ref, 5, None, fr(4 * gz, gz))
    szz = gcol(st_ref, 2, None, fr(5 * gz, gz))
    vx = gcol(vel_ref, 0, fl(3 * gz, gz), None)
    vy = gcol(vel_ref, 1, None, fr(6 * gz, gz))
    vz = gcol(vel_ref, 2, None, fr(7 * gz, gz))
    bb = (
        [bl_ref[pl.ds(4 * gz + 5 * az_n, gz), :]]
        + [b_ref[c] for c in range(width)]
        + [br_ref[pl.ds(8 * gz + az_n, gz), :]]
    )
    o = 4 * gz
    pr = fr(8 * gz, az_n)
    u = [fl(o, az_n), fl(o + az_n, az_n)] + [air_ref[1, c] for c in range(width)]
    v = [None, fl(o + 2 * az_n, az_n)] + [air_ref[2, c] for c in range(width)]
    w = [None, fl(o + 3 * az_n, az_n)] + [air_ref[3, c] for c in range(width)]
    p = [None, fl(o + 4 * az_n, az_n)] + [air_ref[0, c] for c in range(width)] + [pr]

    grow = lax.broadcasted_iota(jnp.int32, (gz, sxx[1].shape[1]), 0)
    arow = lax.broadcasted_iota(jnp.int32, (az_n, sxx[1].shape[1]), 0)

    vx1 = [None] * (width + 2)
    vy1 = [None] * (width + 2)
    vz1 = [None] * (width + 2)
    for e in range(width + 2):
        if e <= width:
            force_x = sxx[e + 1] - sxx[e] + sxy[e] - by(sxy[e]) + sxz[e] - bz(sxz[e])
            vx1[e] = vx[e] + bb[e] * force_x
        if e >= 1:
            force_y = sxy[e] - sxy[e - 1] + ay(syy[e]) - syy[e] + syz[e] - bz(syz[e])
            vy1[e] = vy[e] + bb[e] * force_y
            plane = jnp.broadcast_to(p[e + 1][0:1, :], szz[e].shape)
            ghost = jnp.where(grow == gz - 1, -plane, pltpu.roll(szz[e], gz - 1, 0))
            force_z = sxz[e] - sxz[e - 1] + syz[e] - by(syz[e]) + ghost - szz[e]
            vz1[e] = vz[e] + bb[e] * force_z

    def ground_col(c):
        e = c + 1
        mx, my, mz = vx1[e], vy1[e], vz1[e]
        lam = mod_ref[0, c]
        mu = mod_ref[1, c]
        longitudinal = lam + 2.0 * mu
        strain_x = mx - vx1[e - 1]
        strain_y = my - by(my)
        strain_z = mz - bz(mz)
        st_out[0, c] = st_ref[0, c] + longitudinal * strain_x + lam * (strain_y + strain_z)
        st_out[1, c] = st_ref[1, c] + longitudinal * strain_y + lam * (strain_x + strain_z)
        st_out[2, c] = st_ref[2, c] + longitudinal * strain_z + lam * (strain_x + strain_y)
        st_out[3, c] = st_ref[3, c] + mu * (ay(mx) - mx + vy1[e + 1] - my)
        sxz1 = st_ref[4, c] + mu * (az(mx) - mx + vz1[e + 1] - mz)
        syz1 = st_ref[5, c] + mu * (az(my) - my + ay(mz) - mz)
        st_out[4, c] = jnp.where(grow == gz - 1, 0.0, sxz1)
        st_out[5, c] = jnp.where(grow == gz - 1, 0.0, syz1)
        vel_out[0, c] = mx
        vel_out[1, c] = my
        vel_out[2, c] = mz
        if c == 0 and tl_out is not None:
            for k, (ref, f) in enumerate(
                [(st_out, 0), (st_out, 3), (st_out, 4), (st_out, 1), (st_out, 5), (st_out, 2),
                 (vel_out, 1), (vel_out, 2)]
            ):
                tl_out[pl.ds(k * gz, gz), :] = ref[f, 0]
        if c == width - 1 and tr_out is not None:
            for k, (ref, f) in enumerate([(st_out, 0), (st_out, 3), (st_out, 4), (vel_out, 0)]):
                tr_out[pl.ds(k * gz, gz), :] = ref[f, c]

    wind_x = coef_ref[0]
    wind_y = coef_ref[1]
    lift = coef_ref[2]
    u1 = [None] * (width + 2)
    for a in range(1, width + 2):
        u1[a] = (
            u[a]
            - wind_x * (u[a] - u[a - 1])
            - wind_y * (u[a] - by(u[a]))
            - lift * (p[a + 1] - p[a])
        )
    u1[1] = jnp.where(scal_ref[3 * az_n] > 0.5, u1[1], 0.0)

    def air_col(c):
        a = c + 2
        v1 = v[a] - wind_x * (v[a] - v[a - 1]) - wind_y * (v[a] - by(v[a])) - lift * (ay(p[a]) - p[a])
        w1 = w[a] - wind_x * (w[a] - w[a - 1]) - wind_y * (w[a] - by(w[a])) - lift * (p[a] - bz(p[a]))
        surface = jnp.broadcast_to(vz1[c + 1][gz - 1 : gz, :], w1.shape)
        w1 = jnp.where(arow == 0, surface, w1)
        pm = p[a]
        p1 = (
            pm
            - wind_x * (pm - p[a - 1])
            - wind_y * (pm - by(pm))
            - bulk_ref[c] * ((u1[a] - u1[a - 1]) + (v1 - by(v1)) + (az(w1) - w1))
        )
        air_out[0, c] = p1
        air_out[1, c] = u1[a]
        air_out[2, c] = v1
        air_out[3, c] = w1
        if c == 0 and tl_out is not None:
            tl_out[pl.ds(8 * gz, az_n), :] = p1
        if c == width - 2 and tr_out is not None:
            tr_out[pl.ds(4 * gz, az_n), :] = u1[a]
        if c == width - 1 and tr_out is not None:
            o = 4 * gz
            tr_out[pl.ds(o + az_n, az_n), :] = u1[a]
            tr_out[pl.ds(o + 2 * az_n, az_n), :] = v1
            tr_out[pl.ds(o + 3 * az_n, az_n), :] = w1
            tr_out[pl.ds(o + 4 * az_n, az_n), :] = p1

    ground_edges = [0, width - 1]
    air_edges = [0, width - 2, width - 1]
    for c in ground_edges:
        ground_col(c)
    for c in air_edges:
        air_col(c)
    if after_edges is not None:
        after_edges()
    for c in range(width):
        if c not in ground_edges:
            ground_col(c)
    for c in range(width):
        if c not in air_edges:
            air_col(c)


MESH = pl.DeviceIdType.MESH


def fused_kernel(
    n_py, n_ring, air_ref, vel_ref, st_ref, mod_ref, b_ref, scal_ref,
    air_out, vel_out, st_out,
    air_a, vel_a, st_a, air_b, vel_b, st_b, coef_ref, send_l, send_r, recv_l, recv_r,
    send_sem, recv_sem,
):
    width = air_ref.shape[1]
    az_n = air_ref.shape[2]
    gz = vel_ref.shape[2]
    ny = air_ref.shape[3]
    me = lax.axis_index("px") * n_py + lax.axis_index("py")
    has_left = me > 0
    has_right = me < n_ring - 1
    left = ((me - 1) // n_py, (me - 1) % n_py)
    right = ((me + 1) // n_py, (me + 1) % n_py)
    rows_l = send_l.shape[1]
    rows_r = send_r.shape[1]

    @pl.when(jnp.logical_not(has_left))
    def _():
        recv_l[...] = jnp.zeros_like(recv_l)

    @pl.when(jnp.logical_not(has_right))
    def _():
        recv_r[...] = jnp.zeros_like(recv_r)

    barrier = pltpu.get_barrier_semaphore()

    @pl.when(has_left)
    def _():
        pl.semaphore_signal(barrier, inc=1, device_id=left, device_id_type=MESH)

    @pl.when(has_right)
    def _():
        pl.semaphore_signal(barrier, inc=1, device_id=right, device_id_type=MESH)

    @pl.when(has_left & has_right)
    def _():
        pl.semaphore_wait(barrier, 2)

    @pl.when(jnp.logical_not(has_left & has_right))
    def _():
        pl.semaphore_wait(barrier, 1)

    for k in range(3):
        for z in range(az_n):
            coef_ref[k, pl.ds(z, 1), :] = jnp.full((1, ny), scal_ref[k * az_n + z], jnp.float32)

    tl = send_l.at[0]
    tr = send_r.at[0]
    left_rows = [st_ref[f, 0] for f in (0, 3, 4, 1, 5, 2)] + [vel_ref[1, 0], vel_ref[2, 0]]
    for k, value in enumerate(left_rows):
        tl[pl.ds(k * gz, gz), :] = value
    tl[pl.ds(8 * gz, az_n), :] = air_ref[0, 0]
    tl[pl.ds(8 * gz + az_n, gz), :] = b_ref[0]
    right_rows = [st_ref[f, width - 1] for f in (0, 3, 4)] + [vel_ref[0, width - 1]]
    for k, value in enumerate(right_rows):
        tr[pl.ds(k * gz, gz), :] = value
    o = 4 * gz
    tr[pl.ds(o, az_n), :] = air_ref[1, width - 2]
    for k, f in enumerate((1, 2, 3, 0)):
        tr[pl.ds(o + (k + 1) * az_n, az_n), :] = air_ref[f, width - 1]
    tr[pl.ds(o + 5 * az_n, gz), :] = b_ref[width - 1]

    def copies(n, count_l, count_r):
        to_left = pltpu.make_async_remote_copy(
            src_ref=send_l.at[n, pl.ds(0, count_l)],
            dst_ref=recv_r.at[n, pl.ds(0, count_l)],
            send_sem=send_sem.at[n, 0],
            recv_sem=recv_sem.at[n, 1],
            device_id=left,
            device_id_type=MESH,
        )
        to_right = pltpu.make_async_remote_copy(
            src_ref=send_r.at[n, pl.ds(0, count_r)],
            dst_ref=recv_l.at[n, pl.ds(0, count_r)],
            send_sem=send_sem.at[n, 1],
            recv_sem=recv_sem.at[n, 0],
            device_id=right,
            device_id_type=MESH,
        )

        return to_left, to_right

    def start(n, count_l, count_r):
        to_left, to_right = copies(n, count_l, count_r)

        @pl.when(has_left)
        def _():
            to_left.start()

        @pl.when(has_right)
        def _():
            to_right.start()

    def wait_recv(n, count_l, count_r):
        to_left, to_right = copies(n, count_l, count_r)

        @pl.when(has_left)
        def _():
            to_right.wait_recv()

        @pl.when(has_right)
        def _():
            to_left.wait_recv()

    def wait_send(n, count_l, count_r):
        to_left, to_right = copies(n, count_l, count_r)

        @pl.when(has_left)
        def _():
            to_left.wait_send()

        @pl.when(has_right)
        def _():
            to_right.wait_send()

    full_l = 8 * gz + az_n
    full_r = 4 * gz + 5 * az_n
    counts = [(rows_l, rows_r)] + [(full_l, full_r)] * (STEPS - 1)
    start(0, *counts[0])
    wait_recv(0, *counts[0])
    states = [
        (air_ref, vel_ref, st_ref),
        (air_a, vel_a, st_a),
        (air_b, vel_b, st_b),
        (air_out, vel_out, st_out),
    ]
    for n in range(STEPS):
        src = states[n] if n < len(states) - 1 else states[-2]
        dst = states[n + 1] if n + 1 < STEPS else states[-1]
        last = n + 1 == STEPS
        one_step(
            src[0], air_ref.at[4], src[1], src[2], mod_ref, b_ref, recv_l.at[0], recv_r.at[0],
            recv_l.at[n], recv_r.at[n], scal_ref, dst[0], dst[1], dst[2],
            None if last else send_l.at[n + 1], None if last else send_r.at[n + 1], coef_ref,
            None if last else functools.partial(start, n + 1, *counts[n + 1]),
        )
        if not last:
            wait_recv(n + 1, *counts[n + 1])
    for n in range(STEPS):
        wait_send(n, *counts[n])


def fused(air, vel, st, mod, b, scal):
    n_py = lax.axis_size("py")
    n_ring = lax.axis_size(RING)
    gz = st.shape[2]
    az_n = air.shape[2]
    ny = air.shape[3]
    fields = (4,) + air.shape[1:]
    rows_l = 9 * gz + az_n
    rows_r = 5 * gz + 5 * az_n
    vmem = pl.BlockSpec(memory_space=pltpu.VMEM)
    return pl.pallas_call(
        functools.partial(fused_kernel, n_py, n_ring),
        out_shape=(
            jax.ShapeDtypeStruct(fields, jnp.float32),
            jax.ShapeDtypeStruct(vel.shape, jnp.float32),
            jax.ShapeDtypeStruct(st.shape, jnp.float32),
        ),
        in_specs=[vmem] * 5 + [pl.BlockSpec(memory_space=pltpu.SMEM)],
        out_specs=(vmem, vmem, vmem),
        scratch_shapes=[
            pltpu.VMEM(fields, jnp.float32),
            pltpu.VMEM(vel.shape, jnp.float32),
            pltpu.VMEM(st.shape, jnp.float32),
            pltpu.VMEM(fields, jnp.float32),
            pltpu.VMEM(vel.shape, jnp.float32),
            pltpu.VMEM(st.shape, jnp.float32),
            pltpu.VMEM((3, az_n, ny), jnp.float32),
            pltpu.VMEM((STEPS, rows_l, ny), jnp.float32),
            pltpu.VMEM((STEPS, rows_r, ny), jnp.float32),
            pltpu.VMEM((STEPS, rows_r, ny), jnp.float32),
            pltpu.VMEM((STEPS, rows_l, ny), jnp.float32),
            pltpu.SemaphoreType.DMA((STEPS, 2)),
            pltpu.SemaphoreType.DMA((STEPS, 2)),
        ],
        compiler_params=pltpu.CompilerParams(collective_id=0, has_side_effects=True),
        interpret=INTERPRET,
    )(air, vel, st, mod, b, scal)


def body(air_state, air_bulk, air_buoyancy, air_wind, ground_state, ground_moduli, ground_buoyancy):
    west_edge = (lax.axis_index("px") == 0) & (lax.axis_index("py") == 0)
    moved = to_strips(jnp.concatenate([air_state, air_bulk[None]], 0))
    ground = ground_state.transpose(0, 2, 1, 3)
    gz = ground.shape[2]
    vel = ground[:3]
    st = ground[3:]
    top = lax.broadcasted_iota(jnp.int32, st.shape, 2) == gz - 1
    clear = top & (lax.broadcasted_iota(jnp.int32, st.shape, 0) >= 4)
    st = jnp.where(clear, jnp.zeros_like(st), st)
    mod = ground_moduli.transpose(0, 2, 1, 3)
    b = ground_buoyancy.transpose(1, 0, 2)
    scal = jnp.concatenate(
        [air_wind[0], air_wind[1], air_buoyancy, jnp.where(west_edge, 0.0, 1.0)[None]]
    ).astype(jnp.float32)
    air, vel, st = fused(moved, vel, st, mod, b, scal)
    ground_after = jnp.concatenate([vel, st], 0).transpose(0, 2, 1, 3)
    return (from_strips(air), ground_after)


def solution(mesh):
    placed = (
        P(None, None, "py", "px"),
        P(None, "py", "px"),
        P(),
        P(),
        P(None, None, ("px", "py"), None),
        P(None, None, ("px", "py"), None),
        P(None, ("px", "py"), None),
    )
    return jax.shard_map(
        body,
        mesh=mesh,
        in_specs=placed,
        out_specs=(P(None, None, "py", "px"), P(None, None, ("px", "py"), None)),
        check_vma=False,
    )
```

```python
import functools
import os

import jax
import jax.numpy as jnp
from jax import lax
from jax.experimental import pallas as pl
from jax.experimental.pallas import tpu as pltpu
from jax.sharding import PartitionSpec as P

STEPS = 3
RING = ("px", "py")
INTERPRET = os.environ.get("STENCIL_INTERPRET") == "1"


def trade(to_left, to_right):
    n = lax.axis_size(RING)
    from_right = lax.ppermute(to_left, RING, [(i, i - 1) for i in range(1, n)])
    from_left = lax.ppermute(to_right, RING, [(i, i + 1) for i in range(n - 1)])
    return from_left, from_right


def to_strips(block):
    f, z, ny, nx = block.shape
    parts = lax.axis_size("py")
    split = block.reshape(f, z, ny, parts, nx // parts)
    moved = lax.all_to_all(split, "py", 3, 3, tiled=True)
    return moved.transpose(0, 4, 1, 3, 2).reshape(f, nx // parts, z, parts * ny)


def from_strips(strip):
    f, nx, z, ny_all = strip.shape
    parts = lax.axis_size("py")
    split = strip.reshape(f, nx, z, parts, ny_all // parts)
    moved = lax.all_to_all(split, "py", 3, 3, tiled=True)
    return moved.transpose(0, 2, 4, 3, 1).reshape(f, z, ny_all // parts, parts * nx)


def _rows(a):
    return lax.broadcasted_iota(jnp.int32, a.shape, 0)


def _lanes(a):
    return lax.broadcasted_iota(jnp.int32, a.shape, 1)


def bz(a):
    return jnp.where(_rows(a) == 0, 0.0, pltpu.roll(a, 1, 0))


def az(a):
    n = a.shape[0]
    return jnp.where(_rows(a) == n - 1, 0.0, pltpu.roll(a, n - 1, 0))


def by(a):
    return jnp.where(_lanes(a) == 0, 0.0, pltpu.roll(a, 1, 1))


def ay(a):
    n = a.shape[1]
    return jnp.where(_lanes(a) == n - 1, 0.0, pltpu.roll(a, n - 1, 1))


def one_step(
    air_ref, bulk_ref, vel_ref, st_ref, mod_ref, b_ref, bl_ref, br_ref, fl_ref, fr_ref, scal_ref,
    air_out, vel_out, st_out, tl_out, tr_out, coef_ref, after_edges=None,
):
    width = air_ref.shape[1]
    az_n = air_ref.shape[2]
    gz = vel_ref.shape[2]

    def fl(start, count):
        return fl_ref[pl.ds(start, count), :]

    def fr(start, count):
        return fr_ref[pl.ds(start, count), :]

    def gcol(field_ref, k, left, right):
        cols = [left] + [field_ref[k, c] for c in range(width)] + [right]
        return cols

    sxx = gcol(st_ref, 0, fl(0, gz), fr(0, gz))
    sxy = gcol(st_ref, 3, fl(gz, gz), fr(gz, gz))
    sxz = gcol(st_ref, 4, fl(2 * gz, gz), fr(2 * gz, gz))
    syy = gcol(st_ref, 1, None, fr(3 * gz, gz))
    syz = gcol(st_ref, 5, None, fr(4 * gz, gz))
    szz = gcol(st_ref, 2, None, fr(5 * gz, gz))
    vx = gcol(vel_ref, 0, fl(3 * gz, gz), None)
    vy = gcol(vel_ref, 1, None, fr(6 * gz, gz))
    vz = gcol(vel_ref, 2, None, fr(7 * gz, gz))
    bb = (
        [bl_ref[pl.ds(4 * gz + 5 * az_n, gz), :]]
        + [b_ref[c] for c in range(width)]
        + [br_ref[pl.ds(8 * gz + az_n, gz), :]]
    )
    o = 4 * gz
    pr = fr(8 * gz, az_n)
    u = [fl(o, az_n), fl(o + az_n, az_n)] + [air_ref[1, c] for c in range(width)]
    v = [None, fl(o + 2 * az_n, az_n)] + [air_ref[2, c] for c in range(width)]
    w = [None, fl(o + 3 * az_n, az_n)] + [air_ref[3, c] for c in range(width)]
    p = [None, fl(o + 4 * az_n, az_n)] + [air_ref[0, c] for c in range(width)] + [pr]

    grow = lax.broadcasted_iota(jnp.int32, (gz, sxx[1].shape[1]), 0)
    arow = lax.broadcasted_iota(jnp.int32, (az_n, sxx[1].shape[1]), 0)

    vx1 = [None] * (width + 2)
    vy1 = [None] * (width + 2)
    vz1 = [None] * (width + 2)
    for e in range(width + 2):
        if e <= width:
            force_x = sxx[e + 1] - sxx[e] + sxy[e] - by(sxy[e]) + sxz[e] - bz(sxz[e])
            vx1[e] = vx[e] + bb[e] * force_x
        if e >= 1:
            force_y = sxy[e] - sxy[e - 1] + ay(syy[e]) - syy[e] + syz[e] - bz(syz[e])
            vy1[e] = vy[e] + bb[e] * force_y
            plane = jnp.broadcast_to(p[e + 1][0:1, :], szz[e].shape)
            ghost = jnp.where(grow == gz - 1, -plane, pltpu.roll(szz[e], gz - 1, 0))
            force_z = sxz[e] - sxz[e - 1] + syz[e] - by(syz[e]) + ghost - szz[e]
            vz1[e] = vz[e] + bb[e] * force_z

    def ground_col(c):
        e = c + 1
        mx, my, mz = vx1[e], vy1[e], vz1[e]
        lam = mod_ref[0, c]
        mu = mod_ref[1, c]
        longitudinal = lam + 2.0 * mu
        strain_x = mx - vx1[e - 1]
        strain_y = my - by(my)
        strain_z = mz - bz(mz)
        st_out[0, c] = st_ref[0, c] + longitudinal * strain_x + lam * (strain_y + strain_z)
        st_out[1, c] = st_ref[1, c] + longitudinal * strain_y + lam * (strain_x + strain_z)
        st_out[2, c] = st_ref[2, c] + longitudinal * strain_z + lam * (strain_x + strain_y)
        st_out[3, c] = st_ref[3, c] + mu * (ay(mx) - mx + vy1[e + 1] - my)
        sxz1 = st_ref[4, c] + mu * (az(mx) - mx + vz1[e + 1] - mz)
        syz1 = st_ref[5, c] + mu * (az(my) - my + ay(mz) - mz)
        st_out[4, c] = jnp.where(grow == gz - 1, 0.0, sxz1)
        st_out[5, c] = jnp.where(grow == gz - 1, 0.0, syz1)
        vel_out[0, c] = mx
        vel_out[1, c] = my
        vel_out[2, c] = mz
        if c == 0 and tl_out is not None:
            for k, (ref, f) in enumerate(
                [(st_out, 0), (st_out, 3), (st_out, 4), (st_out, 1), (st_out, 5), (st_out, 2),
                 (vel_out, 1), (vel_out, 2)]
            ):
                tl_out[pl.ds(k * gz, gz), :] = ref[f, 0]
        if c == width - 1 and tr_out is not None:
            for k, (ref, f) in enumerate([(st_out, 0), (st_out, 3), (st_out, 4), (vel_out, 0)]):
                tr_out[pl.ds(k * gz, gz), :] = ref[f, c]

    wind_x = coef_ref[0]
    wind_y = coef_ref[1]
    lift = coef_ref[2]
    u1 = [None] * (width + 2)
    for a in range(1, width + 2):
        u1[a] = (
            u[a]
            - wind_x * (u[a] - u[a - 1])
            - wind_y * (u[a] - by(u[a]))
            - lift * (p[a + 1] - p[a])
        )
    u1[1] = jnp.where(scal_ref[3 * az_n] > 0.5, u1[1], 0.0)

    def air_col(c):
        a = c + 2
        v1 = v[a] - wind_x * (v[a] - v[a - 1]) - wind_y * (v[a] - by(v[a])) - lift * (ay(p[a]) - p[a])
        w1 = w[a] - wind_x * (w[a] - w[a - 1]) - wind_y * (w[a] - by(w[a])) - lift * (p[a] - bz(p[a]))
        surface = jnp.broadcast_to(vz1[c + 1][gz - 1 : gz, :], w1.shape)
        w1 = jnp.where(arow == 0, surface, w1)
        pm = p[a]
        p1 = (
            pm
            - wind_x * (pm - p[a - 1])
            - wind_y * (pm - by(pm))
            - bulk_ref[c] * ((u1[a] - u1[a - 1]) + (v1 - by(v1)) + (az(w1) - w1))
        )
        air_out[0, c] = p1
        air_out[1, c] = u1[a]
        air_out[2, c] = v1
        air_out[3, c] = w1
        if c == 0 and tl_out is not None:
            tl_out[pl.ds(8 * gz, az_n), :] = p1
        if c == width - 2 and tr_out is not None:
            tr_out[pl.ds(4 * gz, az_n), :] = u1[a]
        if c == width - 1 and tr_out is not None:
            o = 4 * gz
            tr_out[pl.ds(o + az_n, az_n), :] = u1[a]
            tr_out[pl.ds(o + 2 * az_n, az_n), :] = v1
            tr_out[pl.ds(o + 3 * az_n, az_n), :] = w1
            tr_out[pl.ds(o + 4 * az_n, az_n), :] = p1

    ground_edges = [0, width - 1]
    air_edges = [0, width - 2, width - 1]
    for c in ground_edges:
        ground_col(c)
    for c in air_edges:
        air_col(c)
    if after_edges is not None:
        after_edges()
    for c in range(width):
        if c not in ground_edges:
            ground_col(c)
    for c in range(width):
        if c not in air_edges:
            air_col(c)


MESH = pl.DeviceIdType.MESH


class Fields:
    def __init__(self, refs):
        self.refs = refs
        self.shape = (len(refs),) + tuple(refs[0].shape)

    def __getitem__(self, index):
        return self.refs[index[0]][index[1:]]


def fused_kernel(
    n_py, n_ring, air_pu, air_vwb, vel_ref, st_ref, mod_ref, b_ref, scal_ref,
    air_out, vel_out, st_out,
    air_a, vel_a, st_a, air_b, vel_b, st_b, coef_ref, send_l, send_r, recv_l, recv_r,
    send_sem, recv_sem,
):
    air_ref = Fields([air_pu.at[0], air_pu.at[1], air_vwb.at[0], air_vwb.at[1]])
    width = air_ref.shape[1]
    az_n = air_ref.shape[2]
    gz = vel_ref.shape[2]
    ny = air_ref.shape[3]
    me = lax.axis_index("px") * n_py + lax.axis_index("py")
    has_left = me > 0
    has_right = me < n_ring - 1
    left = ((me - 1) // n_py, (me - 1) % n_py)
    right = ((me + 1) // n_py, (me + 1) % n_py)
    rows_l = send_l.shape[1]
    rows_r = send_r.shape[1]

    @pl.when(jnp.logical_not(has_left))
    def _():
        recv_l[...] = jnp.zeros_like(recv_l)

    @pl.when(jnp.logical_not(has_right))
    def _():
        recv_r[...] = jnp.zeros_like(recv_r)

    barrier = pltpu.get_barrier_semaphore()

    @pl.when(has_left)
    def _():
        pl.semaphore_signal(barrier, inc=1, device_id=left, device_id_type=MESH)

    @pl.when(has_right)
    def _():
        pl.semaphore_signal(barrier, inc=1, device_id=right, device_id_type=MESH)

    @pl.when(has_left & has_right)
    def _():
        pl.semaphore_wait(barrier, 2)

    @pl.when(jnp.logical_not(has_left & has_right))
    def _():
        pl.semaphore_wait(barrier, 1)

    for k in range(3):
        for z in range(az_n):
            coef_ref[k, pl.ds(z, 1), :] = jnp.full((1, ny), scal_ref[k * az_n + z], jnp.float32)

    tl = send_l.at[0]
    tr = send_r.at[0]
    left_rows = [st_ref[f, 0] for f in (0, 3, 4, 1, 5, 2)] + [vel_ref[1, 0], vel_ref[2, 0]]
    for k, value in enumerate(left_rows):
        tl[pl.ds(k * gz, gz), :] = value
    tl[pl.ds(8 * gz, az_n), :] = air_ref[0, 0]
    tl[pl.ds(8 * gz + az_n, gz), :] = b_ref[0]
    right_rows = [st_ref[f, width - 1] for f in (0, 3, 4)] + [vel_ref[0, width - 1]]
    for k, value in enumerate(right_rows):
        tr[pl.ds(k * gz, gz), :] = value
    o = 4 * gz
    tr[pl.ds(o, az_n), :] = air_ref[1, width - 2]
    for k, f in enumerate((1, 2, 3, 0)):
        tr[pl.ds(o + (k + 1) * az_n, az_n), :] = air_ref[f, width - 1]
    tr[pl.ds(o + 5 * az_n, gz), :] = b_ref[width - 1]

    def copies(n, count_l, count_r):
        to_left = pltpu.make_async_remote_copy(
            src_ref=send_l.at[n, pl.ds(0, count_l)],
            dst_ref=recv_r.at[n, pl.ds(0, count_l)],
            send_sem=send_sem.at[n, 0],
            recv_sem=recv_sem.at[n, 1],
            device_id=left,
            device_id_type=MESH,
        )
        to_right = pltpu.make_async_remote_copy(
            src_ref=send_r.at[n, pl.ds(0, count_r)],
            dst_ref=recv_l.at[n, pl.ds(0, count_r)],
            send_sem=send_sem.at[n, 1],
            recv_sem=recv_sem.at[n, 0],
            device_id=right,
            device_id_type=MESH,
        )

        return to_left, to_right

    def start(n, count_l, count_r):
        to_left, to_right = copies(n, count_l, count_r)

        @pl.when(has_left)
        def _():
            to_left.start()

        @pl.when(has_right)
        def _():
            to_right.start()

    def wait_recv(n, count_l, count_r):
        to_left, to_right = copies(n, count_l, count_r)

        @pl.when(has_left)
        def _():
            to_right.wait_recv()

        @pl.when(has_right)
        def _():
            to_left.wait_recv()

    def wait_send(n, count_l, count_r):
        to_left, to_right = copies(n, count_l, count_r)

        @pl.when(has_left)
        def _():
            to_left.wait_send()

        @pl.when(has_right)
        def _():
            to_right.wait_send()

    full_l = 8 * gz + az_n
    full_r = 4 * gz + 5 * az_n
    counts = [(rows_l, rows_r)] + [(full_l, full_r)] * (STEPS - 1)
    start(0, *counts[0])
    wait_recv(0, *counts[0])
    states = [
        (air_ref, vel_ref, st_ref),
        (air_a, vel_a, st_a),
        (air_b, vel_b, st_b),
        (air_out, vel_out, st_out),
    ]
    for n in range(STEPS):
        src = states[n] if n < len(states) - 1 else states[-2]
        dst = states[n + 1] if n + 1 < STEPS else states[-1]
        last = n + 1 == STEPS
        one_step(
            src[0], air_vwb.at[2], src[1], src[2], mod_ref, b_ref, recv_l.at[0], recv_r.at[0],
            recv_l.at[n], recv_r.at[n], scal_ref, dst[0], dst[1], dst[2],
            None if last else send_l.at[n + 1], None if last else send_r.at[n + 1], coef_ref,
            None if last else functools.partial(start, n + 1, *counts[n + 1]),
        )
        if not last:
            wait_recv(n + 1, *counts[n + 1])
    for n in range(STEPS):
        wait_send(n, *counts[n])


def fused(air, air_vwb, vel, st, mod, b, scal):
    n_py = lax.axis_size("py")
    n_ring = lax.axis_size(RING)
    gz = st.shape[2]
    az_n = air.shape[2]
    ny = air.shape[3]
    fields = (4,) + air.shape[1:]
    rows_l = 9 * gz + az_n
    rows_r = 5 * gz + 5 * az_n
    vmem = pl.BlockSpec(memory_space=pltpu.VMEM)
    return pl.pallas_call(
        functools.partial(fused_kernel, n_py, n_ring),
        out_shape=(
            jax.ShapeDtypeStruct(fields, jnp.float32),
            jax.ShapeDtypeStruct(vel.shape, jnp.float32),
            jax.ShapeDtypeStruct(st.shape, jnp.float32),
        ),
        in_specs=[vmem] * 6 + [pl.BlockSpec(memory_space=pltpu.SMEM)],
        out_specs=(vmem, vmem, vmem),
        scratch_shapes=[
            pltpu.VMEM(fields, jnp.float32),
            pltpu.VMEM(vel.shape, jnp.float32),
            pltpu.VMEM(st.shape, jnp.float32),
            pltpu.VMEM(fields, jnp.float32),
            pltpu.VMEM(vel.shape, jnp.float32),
            pltpu.VMEM(st.shape, jnp.float32),
            pltpu.VMEM((3, az_n, ny), jnp.float32),
            pltpu.VMEM((STEPS, rows_l, ny), jnp.float32),
            pltpu.VMEM((STEPS, rows_r, ny), jnp.float32),
            pltpu.VMEM((STEPS, rows_r, ny), jnp.float32),
            pltpu.VMEM((STEPS, rows_l, ny), jnp.float32),
            pltpu.SemaphoreType.DMA((STEPS, 2)),
            pltpu.SemaphoreType.DMA((STEPS, 2)),
        ],
        compiler_params=pltpu.CompilerParams(collective_id=0, has_side_effects=True),
        interpret=INTERPRET,
    )(air, air_vwb, vel, st, mod, b, scal)


def body(air_state, air_bulk, air_buoyancy, air_wind, ground_state, ground_moduli, ground_buoyancy):
    west_edge = (lax.axis_index("px") == 0) & (lax.axis_index("py") == 0)
    air_pu = to_strips(air_state[:2])
    air_vwb = to_strips(jnp.concatenate([air_state[2:], air_bulk[None]], 0))
    ground = ground_state.transpose(0, 2, 1, 3)
    gz = ground.shape[2]
    vel = ground[:3]
    st = ground[3:]
    top = lax.broadcasted_iota(jnp.int32, st.shape, 2) == gz - 1
    clear = top & (lax.broadcasted_iota(jnp.int32, st.shape, 0) >= 4)
    st = jnp.where(clear, jnp.zeros_like(st), st)
    mod = ground_moduli.transpose(0, 2, 1, 3)
    b = ground_buoyancy.transpose(1, 0, 2)
    scal = jnp.concatenate(
        [air_wind[0], air_wind[1], air_buoyancy, jnp.where(west_edge, 0.0, 1.0)[None]]
    ).astype(jnp.float32)
    air, vel, st = fused(air_pu, air_vwb, vel, st, mod, b, scal)
    ground_after = jnp.concatenate([vel, st], 0).transpose(0, 2, 1, 3)
    return (from_strips(air), ground_after)


def solution(mesh):
    placed = (
        P(None, None, "py", "px"),
        P(None, "py", "px"),
        P(),
        P(),
        P(None, None, ("px", "py"), None),
        P(None, None, ("px", "py"), None),
        P(None, ("px", "py"), None),
    )
    return jax.shard_map(
        body,
        mesh=mesh,
        in_specs=placed,
        out_specs=(P(None, None, "py", "px"), P(None, None, ("px", "py"), None)),
        check_vma=False,
    )
```

```python
import functools
import os

import jax
import jax.numpy as jnp
from jax import lax
from jax.experimental import pallas as pl
from jax.experimental.pallas import tpu as pltpu
from jax.sharding import PartitionSpec as P

STEPS = 3
RING = ("px", "py")
INTERPRET = os.environ.get("STENCIL_INTERPRET") == "1"


def trade(to_left, to_right):
    n = lax.axis_size(RING)
    from_right = lax.ppermute(to_left, RING, [(i, i - 1) for i in range(1, n)])
    from_left = lax.ppermute(to_right, RING, [(i, i + 1) for i in range(n - 1)])
    return from_left, from_right


def to_strips(block):
    f, z, ny, nx = block.shape
    parts = lax.axis_size("py")
    split = block.reshape(f, z, ny, parts, nx // parts)
    moved = lax.all_to_all(split, "py", 3, 3, tiled=True)
    return moved.transpose(0, 4, 1, 3, 2).reshape(f, nx // parts, z, parts * ny)


def from_strips(strip):
    f, nx, z, ny_all = strip.shape
    parts = lax.axis_size("py")
    split = strip.reshape(f, nx, z, parts, ny_all // parts)
    moved = lax.all_to_all(split, "py", 3, 3, tiled=True)
    return moved.transpose(0, 2, 4, 3, 1).reshape(f, z, ny_all // parts, parts * nx)


def _rows(a):
    return lax.broadcasted_iota(jnp.int32, a.shape, 0)


def _lanes(a):
    return lax.broadcasted_iota(jnp.int32, a.shape, 1)


def bz(a):
    return jnp.where(_rows(a) == 0, 0.0, pltpu.roll(a, 1, 0))


def az(a):
    n = a.shape[0]
    return jnp.where(_rows(a) == n - 1, 0.0, pltpu.roll(a, n - 1, 0))


def by(a):
    return jnp.where(_lanes(a) == 0, 0.0, pltpu.roll(a, 1, 1))


def ay(a):
    n = a.shape[1]
    return jnp.where(_lanes(a) == n - 1, 0.0, pltpu.roll(a, n - 1, 1))


def one_step(
    air_ref, bulk_ref, vel_ref, st_ref, mod_ref, b_ref, bl_ref, br_ref, fl_ref, fr_ref, scal_ref,
    air_out, vel_out, st_out, tl_out, tr_out, coef_ref, after_edges=None,
):
    width = air_ref.shape[1]
    az_n = air_ref.shape[2]
    gz = vel_ref.shape[2]

    def fl(start, count):
        return fl_ref[pl.ds(start, count), :]

    def fr(start, count):
        return fr_ref[pl.ds(start, count), :]

    def gcol(field_ref, k, left, right):
        cols = [left] + [field_ref[k, c] for c in range(width)] + [right]
        return cols

    sxx = gcol(st_ref, 0, fl(0, gz), fr(0, gz))
    sxy = gcol(st_ref, 3, fl(gz, gz), fr(gz, gz))
    sxz = gcol(st_ref, 4, fl(2 * gz, gz), fr(2 * gz, gz))
    syy = gcol(st_ref, 1, None, fr(3 * gz, gz))
    syz = gcol(st_ref, 5, None, fr(4 * gz, gz))
    szz = gcol(st_ref, 2, None, fr(5 * gz, gz))
    vx = gcol(vel_ref, 0, fl(3 * gz, gz), None)
    vy = gcol(vel_ref, 1, None, fr(6 * gz, gz))
    vz = gcol(vel_ref, 2, None, fr(7 * gz, gz))
    bb = (
        [bl_ref[pl.ds(4 * gz + 5 * az_n, gz), :]]
        + [b_ref[c] for c in range(width)]
        + [br_ref[pl.ds(8 * gz + az_n, gz), :]]
    )
    o = 4 * gz
    pr = fr(8 * gz, az_n)
    u = [fl(o, az_n), fl(o + az_n, az_n)] + [air_ref[1, c] for c in range(width)]
    v = [None, fl(o + 2 * az_n, az_n)] + [air_ref[2, c] for c in range(width)]
    w = [None, fl(o + 3 * az_n, az_n)] + [air_ref[3, c] for c in range(width)]
    p = [None, fl(o + 4 * az_n, az_n)] + [air_ref[0, c] for c in range(width)] + [pr]

    grow = lax.broadcasted_iota(jnp.int32, (gz, sxx[1].shape[1]), 0)
    arow = lax.broadcasted_iota(jnp.int32, (az_n, sxx[1].shape[1]), 0)

    vx1 = [None] * (width + 2)
    vy1 = [None] * (width + 2)
    vz1 = [None] * (width + 2)
    for e in range(width + 2):
        if e <= width:
            force_x = sxx[e + 1] - sxx[e] + sxy[e] - by(sxy[e]) + sxz[e] - bz(sxz[e])
            vx1[e] = vx[e] + bb[e] * force_x
        if e >= 1:
            force_y = sxy[e] - sxy[e - 1] + ay(syy[e]) - syy[e] + syz[e] - bz(syz[e])
            vy1[e] = vy[e] + bb[e] * force_y
            plane = jnp.broadcast_to(p[e + 1][0:1, :], szz[e].shape)
            ghost = jnp.where(grow == gz - 1, -plane, pltpu.roll(szz[e], gz - 1, 0))
            force_z = sxz[e] - sxz[e - 1] + syz[e] - by(syz[e]) + ghost - szz[e]
            vz1[e] = vz[e] + bb[e] * force_z

    def ground_col(c):
        e = c + 1
        mx, my, mz = vx1[e], vy1[e], vz1[e]
        lam = mod_ref[0, c]
        mu = mod_ref[1, c]
        longitudinal = lam + 2.0 * mu
        strain_x = mx - vx1[e - 1]
        strain_y = my - by(my)
        strain_z = mz - bz(mz)
        st_out[0, c] = st_ref[0, c] + longitudinal * strain_x + lam * (strain_y + strain_z)
        st_out[1, c] = st_ref[1, c] + longitudinal * strain_y + lam * (strain_x + strain_z)
        st_out[2, c] = st_ref[2, c] + longitudinal * strain_z + lam * (strain_x + strain_y)
        st_out[3, c] = st_ref[3, c] + mu * (ay(mx) - mx + vy1[e + 1] - my)
        sxz1 = st_ref[4, c] + mu * (az(mx) - mx + vz1[e + 1] - mz)
        syz1 = st_ref[5, c] + mu * (az(my) - my + ay(mz) - mz)
        st_out[4, c] = jnp.where(grow == gz - 1, 0.0, sxz1)
        st_out[5, c] = jnp.where(grow == gz - 1, 0.0, syz1)
        vel_out[0, c] = mx
        vel_out[1, c] = my
        vel_out[2, c] = mz
        if c == 0 and tl_out is not None:
            for k, (ref, f) in enumerate(
                [(st_out, 0), (st_out, 3), (st_out, 4), (st_out, 1), (st_out, 5), (st_out, 2),
                 (vel_out, 1), (vel_out, 2)]
            ):
                tl_out[pl.ds(k * gz, gz), :] = ref[f, 0]
        if c == width - 1 and tr_out is not None:
            for k, (ref, f) in enumerate([(st_out, 0), (st_out, 3), (st_out, 4), (vel_out, 0)]):
                tr_out[pl.ds(k * gz, gz), :] = ref[f, c]

    wind_x = coef_ref[0]
    wind_y = coef_ref[1]
    lift = coef_ref[2]
    u1 = [None] * (width + 2)
    for a in range(1, width + 2):
        u1[a] = (
            u[a]
            - wind_x * (u[a] - u[a - 1])
            - wind_y * (u[a] - by(u[a]))
            - lift * (p[a + 1] - p[a])
        )
    u1[1] = jnp.where(scal_ref[3 * az_n] > 0.5, u1[1], 0.0)

    def air_col(c):
        a = c + 2
        v1 = v[a] - wind_x * (v[a] - v[a - 1]) - wind_y * (v[a] - by(v[a])) - lift * (ay(p[a]) - p[a])
        w1 = w[a] - wind_x * (w[a] - w[a - 1]) - wind_y * (w[a] - by(w[a])) - lift * (p[a] - bz(p[a]))
        surface = jnp.broadcast_to(vz1[c + 1][gz - 1 : gz, :], w1.shape)
        w1 = jnp.where(arow == 0, surface, w1)
        pm = p[a]
        p1 = (
            pm
            - wind_x * (pm - p[a - 1])
            - wind_y * (pm - by(pm))
            - bulk_ref[c] * ((u1[a] - u1[a - 1]) + (v1 - by(v1)) + (az(w1) - w1))
        )
        air_out[0, c] = p1
        air_out[1, c] = u1[a]
        air_out[2, c] = v1
        air_out[3, c] = w1
        if c == 0 and tl_out is not None:
            tl_out[pl.ds(8 * gz, az_n), :] = p1
        if c == width - 2 and tr_out is not None:
            tr_out[pl.ds(4 * gz, az_n), :] = u1[a]
        if c == width - 1 and tr_out is not None:
            o = 4 * gz
            tr_out[pl.ds(o + az_n, az_n), :] = u1[a]
            tr_out[pl.ds(o + 2 * az_n, az_n), :] = v1
            tr_out[pl.ds(o + 3 * az_n, az_n), :] = w1
            tr_out[pl.ds(o + 4 * az_n, az_n), :] = p1

    ground_edges = [0, width - 1]
    air_edges = [0, width - 2, width - 1]
    for c in ground_edges:
        ground_col(c)
    for c in air_edges:
        air_col(c)
    if after_edges is not None:
        after_edges()
    for c in range(width):
        if c not in ground_edges:
            ground_col(c)
    for c in range(width):
        if c not in air_edges:
            air_col(c)


MESH = pl.DeviceIdType.MESH


def send_layout_kernel(air_ref, bulk_ref, out_ref):
    fields = air_ref.shape[0]
    rows = air_ref.shape[1]
    nyl = out_ref.shape[1] // 16
    nz = rows // nyl
    parts = out_ref.shape[0]
    width = air_ref.shape[2] // parts
    for yl in range(nyl):
        m = jnp.concatenate(
            [air_ref[f, pl.ds(yl, nz, stride=nyl), :] for f in range(fields)], 0
        )
        t = m.T.reshape(parts, width, m.shape[0])
        out_ref[:, pl.ds(yl * width, width), :] = t
        mb = jnp.concatenate(
            [bulk_ref[pl.ds(yl, nz, stride=nyl), :], jnp.zeros((m.shape[0] - nz, m.shape[1]), jnp.float32)], 0
        )
        tb = mb.T.reshape(parts, width, m.shape[0])
        out_ref[:, pl.ds(nyl * width + yl * width, width), :] = tb


def to_strips_fast(air_state, air_bulk):
    f, z, ny, nx = air_state.shape
    parts = lax.axis_size("py")
    width = nx // parts
    flat = air_state.reshape(f, z * ny, nx)
    bulk = air_bulk.reshape(z * ny, nx)
    payload = pl.pallas_call(
        send_layout_kernel,
        out_shape=jax.ShapeDtypeStruct((parts, 2 * ny * width, f * z), jnp.float32),
        interpret=INTERPRET,
    )(flat, bulk)
    return lax.all_to_all(payload, "py", 0, 0, tiled=True)


def fused_kernel(
    n_py, n_ring, pay_ref, vel_ref, st_ref, mod_ref, b_ref, scal_ref,
    air_out, vel_out, st_out, air_ref,
    air_a, vel_a, st_a, air_b, vel_b, st_b, coef_ref, send_l, send_r, recv_l, recv_r,
    send_sem, recv_sem,
):
    width = air_ref.shape[1]
    az_n = air_ref.shape[2]
    gz = vel_ref.shape[2]
    ny = air_ref.shape[3]
    me = lax.axis_index("px") * n_py + lax.axis_index("py")
    has_left = me > 0
    has_right = me < n_ring - 1
    left = ((me - 1) // n_py, (me - 1) % n_py)
    right = ((me + 1) // n_py, (me + 1) % n_py)
    rows_l = send_l.shape[1]
    rows_r = send_r.shape[1]

    nyl = ny // n_py
    for xl in range(width):
        n_air = pay_ref[:, pl.ds(xl, nyl, stride=width), :].reshape(ny, ny)
        t = n_air.T
        for f in range(4):
            air_ref[f, xl] = t[f * az_n : (f + 1) * az_n]
        n_bulk = pay_ref[:, pl.ds(nyl * width + xl, nyl, stride=width), :].reshape(ny, ny)
        air_ref[4, xl] = n_bulk.T[0:az_n]

    @pl.when(jnp.logical_not(has_left))
    def _():
        recv_l[...] = jnp.zeros_like(recv_l)

    @pl.when(jnp.logical_not(has_right))
    def _():
        recv_r[...] = jnp.zeros_like(recv_r)

    barrier = pltpu.get_barrier_semaphore()

    @pl.when(has_left)
    def _():
        pl.semaphore_signal(barrier, inc=1, device_id=left, device_id_type=MESH)

    @pl.when(has_right)
    def _():
        pl.semaphore_signal(barrier, inc=1, device_id=right, device_id_type=MESH)

    @pl.when(has_left & has_right)
    def _():
        pl.semaphore_wait(barrier, 2)

    @pl.when(jnp.logical_not(has_left & has_right))
    def _():
        pl.semaphore_wait(barrier, 1)

    for k in range(3):
        for z in range(az_n):
            coef_ref[k, pl.ds(z, 1), :] = jnp.full((1, ny), scal_ref[k * az_n + z], jnp.float32)

    tl = send_l.at[0]
    tr = send_r.at[0]
    left_rows = [st_ref[f, 0] for f in (0, 3, 4, 1, 5, 2)] + [vel_ref[1, 0], vel_ref[2, 0]]
    for k, value in enumerate(left_rows):
        tl[pl.ds(k * gz, gz), :] = value
    tl[pl.ds(8 * gz, az_n), :] = air_ref[0, 0]
    tl[pl.ds(8 * gz + az_n, gz), :] = b_ref[0]
    right_rows = [st_ref[f, width - 1] for f in (0, 3, 4)] + [vel_ref[0, width - 1]]
    for k, value in enumerate(right_rows):
        tr[pl.ds(k * gz, gz), :] = value
    o = 4 * gz
    tr[pl.ds(o, az_n), :] = air_ref[1, width - 2]
    for k, f in enumerate((1, 2, 3, 0)):
        tr[pl.ds(o + (k + 1) * az_n, az_n), :] = air_ref[f, width - 1]
    tr[pl.ds(o + 5 * az_n, gz), :] = b_ref[width - 1]

    def copies(n, count_l, count_r):
        to_left = pltpu.make_async_remote_copy(
            src_ref=send_l.at[n, pl.ds(0, count_l)],
            dst_ref=recv_r.at[n, pl.ds(0, count_l)],
            send_sem=send_sem.at[n, 0],
            recv_sem=recv_sem.at[n, 1],
            device_id=left,
            device_id_type=MESH,
        )
        to_right = pltpu.make_async_remote_copy(
            src_ref=send_r.at[n, pl.ds(0, count_r)],
            dst_ref=recv_l.at[n, pl.ds(0, count_r)],
            send_sem=send_sem.at[n, 1],
            recv_sem=recv_sem.at[n, 0],
            device_id=right,
            device_id_type=MESH,
        )

        return to_left, to_right

    def start(n, count_l, count_r):
        to_left, to_right = copies(n, count_l, count_r)

        @pl.when(has_left)
        def _():
            to_left.start()

        @pl.when(has_right)
        def _():
            to_right.start()

    def wait_recv(n, count_l, count_r):
        to_left, to_right = copies(n, count_l, count_r)

        @pl.when(has_left)
        def _():
            to_right.wait_recv()

        @pl.when(has_right)
        def _():
            to_left.wait_recv()

    def wait_send(n, count_l, count_r):
        to_left, to_right = copies(n, count_l, count_r)

        @pl.when(has_left)
        def _():
            to_left.wait_send()

        @pl.when(has_right)
        def _():
            to_right.wait_send()

    full_l = 8 * gz + az_n
    full_r = 4 * gz + 5 * az_n
    counts = [(rows_l, rows_r)] + [(full_l, full_r)] * (STEPS - 1)
    start(0, *counts[0])
    wait_recv(0, *counts[0])
    states = [
        (air_ref, vel_ref, st_ref),
        (air_a, vel_a, st_a),
        (air_b, vel_b, st_b),
        (air_out, vel_out, st_out),
    ]
    for n in range(STEPS):
        src = states[n] if n < len(states) - 1 else states[-2]
        dst = states[n + 1] if n + 1 < STEPS else states[-1]
        last = n + 1 == STEPS
        one_step(
            src[0], air_ref.at[4], src[1], src[2], mod_ref, b_ref, recv_l.at[0], recv_r.at[0],
            recv_l.at[n], recv_r.at[n], scal_ref, dst[0], dst[1], dst[2],
            None if last else send_l.at[n + 1], None if last else send_r.at[n + 1], coef_ref,
            None if last else functools.partial(start, n + 1, *counts[n + 1]),
        )
        if not last:
            wait_recv(n + 1, *counts[n + 1])
    for n in range(STEPS):
        wait_send(n, *counts[n])


def fused(payload, vel, st, mod, b, scal, az_n):
    n_py = lax.axis_size("py")
    n_ring = lax.axis_size(RING)
    gz = st.shape[2]
    ny = payload.shape[2]
    width = vel.shape[1]
    fields = (4, width, az_n, ny)
    rows_l = 9 * gz + az_n
    rows_r = 5 * gz + 5 * az_n
    vmem = pl.BlockSpec(memory_space=pltpu.VMEM)
    return pl.pallas_call(
        functools.partial(fused_kernel, n_py, n_ring),
        out_shape=(
            jax.ShapeDtypeStruct(fields, jnp.float32),
            jax.ShapeDtypeStruct(vel.shape, jnp.float32),
            jax.ShapeDtypeStruct(st.shape, jnp.float32),
        ),
        in_specs=[vmem] * 5 + [pl.BlockSpec(memory_space=pltpu.SMEM)],
        out_specs=(vmem, vmem, vmem),
        scratch_shapes=[
            pltpu.VMEM((5, width, az_n, ny), jnp.float32),
            pltpu.VMEM(fields, jnp.float32),
            pltpu.VMEM(vel.shape, jnp.float32),
            pltpu.VMEM(st.shape, jnp.float32),
            pltpu.VMEM(fields, jnp.float32),
            pltpu.VMEM(vel.shape, jnp.float32),
            pltpu.VMEM(st.shape, jnp.float32),
            pltpu.VMEM((3, az_n, ny), jnp.float32),
            pltpu.VMEM((STEPS, rows_l, ny), jnp.float32),
            pltpu.VMEM((STEPS, rows_r, ny), jnp.float32),
            pltpu.VMEM((STEPS, rows_r, ny), jnp.float32),
            pltpu.VMEM((STEPS, rows_l, ny), jnp.float32),
            pltpu.SemaphoreType.DMA((STEPS, 2)),
            pltpu.SemaphoreType.DMA((STEPS, 2)),
        ],
        compiler_params=pltpu.CompilerParams(collective_id=0, has_side_effects=True),
        interpret=INTERPRET,
    )(payload, vel, st, mod, b, scal)


def body(air_state, air_bulk, air_buoyancy, air_wind, ground_state, ground_moduli, ground_buoyancy):
    west_edge = (lax.axis_index("px") == 0) & (lax.axis_index("py") == 0)
    payload = to_strips_fast(air_state, air_bulk)
    ground = ground_state.transpose(0, 2, 1, 3)
    gz = ground.shape[2]
    vel = ground[:3]
    st = ground[3:]
    top = lax.broadcasted_iota(jnp.int32, st.shape, 2) == gz - 1
    clear = top & (lax.broadcasted_iota(jnp.int32, st.shape, 0) >= 4)
    st = jnp.where(clear, jnp.zeros_like(st), st)
    mod = ground_moduli.transpose(0, 2, 1, 3)
    b = ground_buoyancy.transpose(1, 0, 2)
    scal = jnp.concatenate(
        [air_wind[0], air_wind[1], air_buoyancy, jnp.where(west_edge, 0.0, 1.0)[None]]
    ).astype(jnp.float32)
    air, vel, st = fused(payload, vel, st, mod, b, scal, air_state.shape[1])
    ground_after = jnp.concatenate([vel, st], 0).transpose(0, 2, 1, 3)
    return (from_strips(air), ground_after)


def solution(mesh):
    placed = (
        P(None, None, "py", "px"),
        P(None, "py", "px"),
        P(),
        P(),
        P(None, None, ("px", "py"), None),
        P(None, None, ("px", "py"), None),
        P(None, ("px", "py"), None),
    )
    return jax.shard_map(
        body,
        mesh=mesh,
        in_specs=placed,
        out_specs=(P(None, None, "py", "px"), P(None, None, ("px", "py"), None)),
        check_vma=False,
    )
```

```python
import functools
import os

import jax
import jax.numpy as jnp
from jax import lax
from jax.experimental import pallas as pl
from jax.experimental.pallas import tpu as pltpu
from jax.sharding import PartitionSpec as P

STEPS = 3
RING = ("px", "py")
INTERPRET = os.environ.get("STENCIL_INTERPRET") == "1"


def trade(to_left, to_right):
    n = lax.axis_size(RING)
    from_right = lax.ppermute(to_left, RING, [(i, i - 1) for i in range(1, n)])
    from_left = lax.ppermute(to_right, RING, [(i, i + 1) for i in range(n - 1)])
    return from_left, from_right


def to_strips(block):
    f, z, ny, nx = block.shape
    parts = lax.axis_size("py")
    split = block.reshape(f, z, ny, parts, nx // parts)
    moved = lax.all_to_all(split, "py", 3, 3, tiled=True)
    return moved.transpose(0, 4, 1, 3, 2).reshape(f, nx // parts, z, parts * ny)


def from_strips(strip):
    f, nx, z, ny_all = strip.shape
    parts = lax.axis_size("py")
    split = strip.reshape(f, nx, z, parts, ny_all // parts)
    moved = lax.all_to_all(split, "py", 3, 3, tiled=True)
    return moved.transpose(0, 2, 4, 3, 1).reshape(f, z, ny_all // parts, parts * nx)


def _rows(a):
    return lax.broadcasted_iota(jnp.int32, a.shape, 0)


def _lanes(a):
    return lax.broadcasted_iota(jnp.int32, a.shape, 1)


def bz(a):
    return jnp.where(_rows(a) == 0, 0.0, pltpu.roll(a, 1, 0))


def az(a):
    n = a.shape[0]
    return jnp.where(_rows(a) == n - 1, 0.0, pltpu.roll(a, n - 1, 0))


def by(a):
    return jnp.where(_lanes(a) == 0, 0.0, pltpu.roll(a, 1, 1))


def ay(a):
    n = a.shape[1]
    return jnp.where(_lanes(a) == n - 1, 0.0, pltpu.roll(a, n - 1, 1))


def one_step(
    air_ref, bulk_ref, vel_ref, st_ref, mod_ref, b_ref, bl_ref, br_ref, fl_ref, fr_ref, scal_ref,
    air_out, vel_out, st_out, tl_out, tr_out, coef_ref, after_edges=None,
):
    width = air_ref.shape[1]
    az_n = air_ref.shape[2]
    gz = vel_ref.shape[2]

    def fl(start, count):
        return fl_ref[pl.ds(start, count), :]

    def fr(start, count):
        return fr_ref[pl.ds(start, count), :]

    def gcol(field_ref, k, left, right):
        cols = [left] + [field_ref[k, c] for c in range(width)] + [right]
        return cols

    sxx = gcol(st_ref, 0, fl(0, gz), fr(0, gz))
    sxy = gcol(st_ref, 3, fl(gz, gz), fr(gz, gz))
    sxz = gcol(st_ref, 4, fl(2 * gz, gz), fr(2 * gz, gz))
    syy = gcol(st_ref, 1, None, fr(3 * gz, gz))
    syz = gcol(st_ref, 5, None, fr(4 * gz, gz))
    szz = gcol(st_ref, 2, None, fr(5 * gz, gz))
    vx = gcol(vel_ref, 0, fl(3 * gz, gz), None)
    vy = gcol(vel_ref, 1, None, fr(6 * gz, gz))
    vz = gcol(vel_ref, 2, None, fr(7 * gz, gz))
    bb = (
        [bl_ref[pl.ds(4 * gz + 5 * az_n, gz), :]]
        + [b_ref[c] for c in range(width)]
        + [br_ref[pl.ds(8 * gz + az_n, gz), :]]
    )
    o = 4 * gz
    pr = fr(8 * gz, az_n)
    u = [fl(o, az_n), fl(o + az_n, az_n)] + [air_ref[1, c] for c in range(width)]
    v = [None, fl(o + 2 * az_n, az_n)] + [air_ref[2, c] for c in range(width)]
    w = [None, fl(o + 3 * az_n, az_n)] + [air_ref[3, c] for c in range(width)]
    p = [None, fl(o + 4 * az_n, az_n)] + [air_ref[0, c] for c in range(width)] + [pr]

    grow = lax.broadcasted_iota(jnp.int32, (gz, sxx[1].shape[1]), 0)
    arow = lax.broadcasted_iota(jnp.int32, (az_n, sxx[1].shape[1]), 0)

    vx1 = [None] * (width + 2)
    vy1 = [None] * (width + 2)
    vz1 = [None] * (width + 2)
    for e in range(width + 2):
        if e <= width:
            force_x = sxx[e + 1] - sxx[e] + sxy[e] - by(sxy[e]) + sxz[e] - bz(sxz[e])
            vx1[e] = vx[e] + bb[e] * force_x
        if e >= 1:
            force_y = sxy[e] - sxy[e - 1] + ay(syy[e]) - syy[e] + syz[e] - bz(syz[e])
            vy1[e] = vy[e] + bb[e] * force_y
            plane = jnp.broadcast_to(p[e + 1][0:1, :], szz[e].shape)
            ghost = jnp.where(grow == gz - 1, -plane, pltpu.roll(szz[e], gz - 1, 0))
            force_z = sxz[e] - sxz[e - 1] + syz[e] - by(syz[e]) + ghost - szz[e]
            vz1[e] = vz[e] + bb[e] * force_z

    def ground_col(c):
        e = c + 1
        mx, my, mz = vx1[e], vy1[e], vz1[e]
        lam = mod_ref[0, c]
        mu = mod_ref[1, c]
        longitudinal = lam + 2.0 * mu
        strain_x = mx - vx1[e - 1]
        strain_y = my - by(my)
        strain_z = mz - bz(mz)
        st_out[0, c] = st_ref[0, c] + longitudinal * strain_x + lam * (strain_y + strain_z)
        st_out[1, c] = st_ref[1, c] + longitudinal * strain_y + lam * (strain_x + strain_z)
        st_out[2, c] = st_ref[2, c] + longitudinal * strain_z + lam * (strain_x + strain_y)
        st_out[3, c] = st_ref[3, c] + mu * (ay(mx) - mx + vy1[e + 1] - my)
        sxz1 = st_ref[4, c] + mu * (az(mx) - mx + vz1[e + 1] - mz)
        syz1 = st_ref[5, c] + mu * (az(my) - my + ay(mz) - mz)
        st_out[4, c] = jnp.where(grow == gz - 1, 0.0, sxz1)
        st_out[5, c] = jnp.where(grow == gz - 1, 0.0, syz1)
        vel_out[0, c] = mx
        vel_out[1, c] = my
        vel_out[2, c] = mz
        if c == 0 and tl_out is not None:
            for k, (ref, f) in enumerate(
                [(st_out, 0), (st_out, 3), (st_out, 4), (st_out, 1), (st_out, 5), (st_out, 2),
                 (vel_out, 1), (vel_out, 2)]
            ):
                tl_out[pl.ds(k * gz, gz), :] = ref[f, 0]
        if c == width - 1 and tr_out is not None:
            for k, (ref, f) in enumerate([(st_out, 0), (st_out, 3), (st_out, 4), (vel_out, 0)]):
                tr_out[pl.ds(k * gz, gz), :] = ref[f, c]

    wind_x = coef_ref[0]
    wind_y = coef_ref[1]
    lift = coef_ref[2]
    u1 = [None] * (width + 2)
    for a in range(1, width + 2):
        u1[a] = (
            u[a]
            - wind_x * (u[a] - u[a - 1])
            - wind_y * (u[a] - by(u[a]))
            - lift * (p[a + 1] - p[a])
        )
    u1[1] = jnp.where(scal_ref[3 * az_n] > 0.5, u1[1], 0.0)

    def air_col(c):
        a = c + 2
        v1 = v[a] - wind_x * (v[a] - v[a - 1]) - wind_y * (v[a] - by(v[a])) - lift * (ay(p[a]) - p[a])
        w1 = w[a] - wind_x * (w[a] - w[a - 1]) - wind_y * (w[a] - by(w[a])) - lift * (p[a] - bz(p[a]))
        surface = jnp.broadcast_to(vz1[c + 1][gz - 1 : gz, :], w1.shape)
        w1 = jnp.where(arow == 0, surface, w1)
        pm = p[a]
        p1 = (
            pm
            - wind_x * (pm - p[a - 1])
            - wind_y * (pm - by(pm))
            - bulk_ref[c] * ((u1[a] - u1[a - 1]) + (v1 - by(v1)) + (az(w1) - w1))
        )
        air_out[0, c] = p1
        air_out[1, c] = u1[a]
        air_out[2, c] = v1
        air_out[3, c] = w1
        if c == 0 and tl_out is not None:
            tl_out[pl.ds(8 * gz, az_n), :] = p1
        if c == width - 2 and tr_out is not None:
            tr_out[pl.ds(4 * gz, az_n), :] = u1[a]
        if c == width - 1 and tr_out is not None:
            o = 4 * gz
            tr_out[pl.ds(o + az_n, az_n), :] = u1[a]
            tr_out[pl.ds(o + 2 * az_n, az_n), :] = v1
            tr_out[pl.ds(o + 3 * az_n, az_n), :] = w1
            tr_out[pl.ds(o + 4 * az_n, az_n), :] = p1

    ground_edges = [0, width - 1]
    air_edges = [0, width - 2, width - 1]
    for c in ground_edges:
        ground_col(c)
    for c in air_edges:
        air_col(c)
    if after_edges is not None:
        after_edges()
    for c in range(width):
        if c not in ground_edges:
            ground_col(c)
    for c in range(width):
        if c not in air_edges:
            air_col(c)


MESH = pl.DeviceIdType.MESH


def send_layout_kernel(air_ref, bulk_ref, out_ref):
    fields = air_ref.shape[0]
    rows = air_ref.shape[1]
    nyl = out_ref.shape[1] // 16
    nz = rows // nyl
    parts = out_ref.shape[0]
    width = air_ref.shape[2] // parts
    for yl in range(nyl):
        m = jnp.concatenate(
            [air_ref[f, pl.ds(yl, nz, stride=nyl), :] for f in range(fields)], 0
        )
        t = m.T.reshape(parts, width, m.shape[0])
        out_ref[:, pl.ds(yl * width, width), :] = t
        mb = jnp.concatenate(
            [bulk_ref[pl.ds(yl, nz, stride=nyl), :], jnp.zeros((m.shape[0] - nz, m.shape[1]), jnp.float32)], 0
        )
        tb = mb.T.reshape(parts, width, m.shape[0])
        out_ref[:, pl.ds(nyl * width + yl * width, width), :] = tb


def recv_layout_kernel(width, nyl, pay_ref, out_ref):
    fields = out_ref.shape[0]
    parts = pay_ref.shape[0]
    nz = pay_ref.shape[2] // fields
    for yl in range(nyl):
        n = pay_ref[:, pl.ds(yl, width, stride=nyl), :].reshape(parts * width, fields * nz)
        t = n.T
        for f in range(fields):
            out_ref[f, pl.ds(yl, nz, stride=nyl), :] = t[f * nz : (f + 1) * nz]


def from_strips_fast(payload, fields, az_n, width):
    parts = payload.shape[0]
    nyl = payload.shape[1] // width
    got = lax.all_to_all(payload, "py", 0, 0, tiled=True)
    out = pl.pallas_call(
        functools.partial(recv_layout_kernel, width, nyl),
        out_shape=jax.ShapeDtypeStruct((fields, az_n * nyl, width * parts), jnp.float32),
        interpret=INTERPRET,
    )(got)
    return out.reshape(fields, az_n, nyl, width * parts)


def to_strips_fast(air_state, air_bulk):
    f, z, ny, nx = air_state.shape
    parts = lax.axis_size("py")
    width = nx // parts
    flat = air_state.reshape(f, z * ny, nx)
    bulk = air_bulk.reshape(z * ny, nx)
    payload = pl.pallas_call(
        send_layout_kernel,
        out_shape=jax.ShapeDtypeStruct((parts, 2 * ny * width, f * z), jnp.float32),
        interpret=INTERPRET,
    )(flat, bulk)
    return lax.all_to_all(payload, "py", 0, 0, tiled=True)


def fused_kernel(
    n_py, n_ring, pay_ref, vel_ref, st_ref, mod_ref, b_ref, scal_ref,
    pay_out, vel_out, st_out, air_ref, air_out,
    air_a, vel_a, st_a, air_b, vel_b, st_b, coef_ref, send_l, send_r, recv_l, recv_r,
    send_sem, recv_sem,
):
    width = air_ref.shape[1]
    az_n = air_ref.shape[2]
    gz = vel_ref.shape[2]
    ny = air_ref.shape[3]
    me = lax.axis_index("px") * n_py + lax.axis_index("py")
    has_left = me > 0
    has_right = me < n_ring - 1
    left = ((me - 1) // n_py, (me - 1) % n_py)
    right = ((me + 1) // n_py, (me + 1) % n_py)
    rows_l = send_l.shape[1]
    rows_r = send_r.shape[1]

    nyl = ny // n_py
    for xl in range(width):
        n_air = pay_ref[:, pl.ds(xl, nyl, stride=width), :].reshape(ny, ny)
        t = n_air.T
        for f in range(4):
            air_ref[f, xl] = t[f * az_n : (f + 1) * az_n]
        n_bulk = pay_ref[:, pl.ds(nyl * width + xl, nyl, stride=width), :].reshape(ny, ny)
        air_ref[4, xl] = n_bulk.T[0:az_n]

    @pl.when(jnp.logical_not(has_left))
    def _():
        recv_l[...] = jnp.zeros_like(recv_l)

    @pl.when(jnp.logical_not(has_right))
    def _():
        recv_r[...] = jnp.zeros_like(recv_r)

    barrier = pltpu.get_barrier_semaphore()

    @pl.when(has_left)
    def _():
        pl.semaphore_signal(barrier, inc=1, device_id=left, device_id_type=MESH)

    @pl.when(has_right)
    def _():
        pl.semaphore_signal(barrier, inc=1, device_id=right, device_id_type=MESH)

    @pl.when(has_left & has_right)
    def _():
        pl.semaphore_wait(barrier, 2)

    @pl.when(jnp.logical_not(has_left & has_right))
    def _():
        pl.semaphore_wait(barrier, 1)

    for k in range(3):
        for z in range(az_n):
            coef_ref[k, pl.ds(z, 1), :] = jnp.full((1, ny), scal_ref[k * az_n + z], jnp.float32)

    tl = send_l.at[0]
    tr = send_r.at[0]
    left_rows = [st_ref[f, 0] for f in (0, 3, 4, 1, 5, 2)] + [vel_ref[1, 0], vel_ref[2, 0]]
    for k, value in enumerate(left_rows):
        tl[pl.ds(k * gz, gz), :] = value
    tl[pl.ds(8 * gz, az_n), :] = air_ref[0, 0]
    tl[pl.ds(8 * gz + az_n, gz), :] = b_ref[0]
    right_rows = [st_ref[f, width - 1] for f in (0, 3, 4)] + [vel_ref[0, width - 1]]
    for k, value in enumerate(right_rows):
        tr[pl.ds(k * gz, gz), :] = value
    o = 4 * gz
    tr[pl.ds(o, az_n), :] = air_ref[1, width - 2]
    for k, f in enumerate((1, 2, 3, 0)):
        tr[pl.ds(o + (k + 1) * az_n, az_n), :] = air_ref[f, width - 1]
    tr[pl.ds(o + 5 * az_n, gz), :] = b_ref[width - 1]

    def copies(n, count_l, count_r):
        to_left = pltpu.make_async_remote_copy(
            src_ref=send_l.at[n, pl.ds(0, count_l)],
            dst_ref=recv_r.at[n, pl.ds(0, count_l)],
            send_sem=send_sem.at[n, 0],
            recv_sem=recv_sem.at[n, 1],
            device_id=left,
            device_id_type=MESH,
        )
        to_right = pltpu.make_async_remote_copy(
            src_ref=send_r.at[n, pl.ds(0, count_r)],
            dst_ref=recv_l.at[n, pl.ds(0, count_r)],
            send_sem=send_sem.at[n, 1],
            recv_sem=recv_sem.at[n, 0],
            device_id=right,
            device_id_type=MESH,
        )

        return to_left, to_right

    def start(n, count_l, count_r):
        to_left, to_right = copies(n, count_l, count_r)

        @pl.when(has_left)
        def _():
            to_left.start()

        @pl.when(has_right)
        def _():
            to_right.start()

    def wait_recv(n, count_l, count_r):
        to_left, to_right = copies(n, count_l, count_r)

        @pl.when(has_left)
        def _():
            to_right.wait_recv()

        @pl.when(has_right)
        def _():
            to_left.wait_recv()

    def wait_send(n, count_l, count_r):
        to_left, to_right = copies(n, count_l, count_r)

        @pl.when(has_left)
        def _():
            to_left.wait_send()

        @pl.when(has_right)
        def _():
            to_right.wait_send()

    full_l = 8 * gz + az_n
    full_r = 4 * gz + 5 * az_n
    counts = [(rows_l, rows_r)] + [(full_l, full_r)] * (STEPS - 1)
    start(0, *counts[0])
    wait_recv(0, *counts[0])
    states = [
        (air_ref, vel_ref, st_ref),
        (air_a, vel_a, st_a),
        (air_b, vel_b, st_b),
        (air_out, vel_out, st_out),
    ]
    for n in range(STEPS):
        src = states[n] if n < len(states) - 1 else states[-2]
        dst = states[n + 1] if n + 1 < STEPS else states[-1]
        last = n + 1 == STEPS
        one_step(
            src[0], air_ref.at[4], src[1], src[2], mod_ref, b_ref, recv_l.at[0], recv_r.at[0],
            recv_l.at[n], recv_r.at[n], scal_ref, dst[0], dst[1], dst[2],
            None if last else send_l.at[n + 1], None if last else send_r.at[n + 1], coef_ref,
            None if last else functools.partial(start, n + 1, *counts[n + 1]),
        )
        if not last:
            wait_recv(n + 1, *counts[n + 1])
    for xl in range(width):
        m = jnp.concatenate([air_out[f, xl] for f in range(4)], 0)
        t = m.T.reshape(n_py, nyl, 4 * az_n)
        pay_out[:, pl.ds(xl * nyl, nyl), :] = t
    for n in range(STEPS):
        wait_send(n, *counts[n])


def fused(payload, vel, st, mod, b, scal, az_n):
    n_py = lax.axis_size("py")
    n_ring = lax.axis_size(RING)
    gz = st.shape[2]
    ny = payload.shape[2]
    width = vel.shape[1]
    fields = (4, width, az_n, ny)
    rows_l = 9 * gz + az_n
    rows_r = 5 * gz + 5 * az_n
    vmem = pl.BlockSpec(memory_space=pltpu.VMEM)
    return pl.pallas_call(
        functools.partial(fused_kernel, n_py, n_ring),
        out_shape=(
            jax.ShapeDtypeStruct((n_py, width * (ny // n_py), 4 * az_n), jnp.float32),
            jax.ShapeDtypeStruct(vel.shape, jnp.float32),
            jax.ShapeDtypeStruct(st.shape, jnp.float32),
        ),
        in_specs=[vmem] * 5 + [pl.BlockSpec(memory_space=pltpu.SMEM)],
        out_specs=(vmem, vmem, vmem),
        scratch_shapes=[
            pltpu.VMEM((5, width, az_n, ny), jnp.float32),
            pltpu.VMEM(fields, jnp.float32),
            pltpu.VMEM(fields, jnp.float32),
            pltpu.VMEM(vel.shape, jnp.float32),
            pltpu.VMEM(st.shape, jnp.float32),
            pltpu.VMEM(fields, jnp.float32),
            pltpu.VMEM(vel.shape, jnp.float32),
            pltpu.VMEM(st.shape, jnp.float32),
            pltpu.VMEM((3, az_n, ny), jnp.float32),
            pltpu.VMEM((STEPS, rows_l, ny), jnp.float32),
            pltpu.VMEM((STEPS, rows_r, ny), jnp.float32),
            pltpu.VMEM((STEPS, rows_r, ny), jnp.float32),
            pltpu.VMEM((STEPS, rows_l, ny), jnp.float32),
            pltpu.SemaphoreType.DMA((STEPS, 2)),
            pltpu.SemaphoreType.DMA((STEPS, 2)),
        ],
        compiler_params=pltpu.CompilerParams(collective_id=0, has_side_effects=True),
        interpret=INTERPRET,
    )(payload, vel, st, mod, b, scal)


def body(air_state, air_bulk, air_buoyancy, air_wind, ground_state, ground_moduli, ground_buoyancy):
    west_edge = (lax.axis_index("px") == 0) & (lax.axis_index("py") == 0)
    payload = to_strips_fast(air_state, air_bulk)
    ground = ground_state.transpose(0, 2, 1, 3)
    gz = ground.shape[2]
    vel = ground[:3]
    st = ground[3:]
    top = lax.broadcasted_iota(jnp.int32, st.shape, 2) == gz - 1
    clear = top & (lax.broadcasted_iota(jnp.int32, st.shape, 0) >= 4)
    st = jnp.where(clear, jnp.zeros_like(st), st)
    mod = ground_moduli.transpose(0, 2, 1, 3)
    b = ground_buoyancy.transpose(1, 0, 2)
    scal = jnp.concatenate(
        [air_wind[0], air_wind[1], air_buoyancy, jnp.where(west_edge, 0.0, 1.0)[None]]
    ).astype(jnp.float32)
    air, vel, st = fused(payload, vel, st, mod, b, scal, air_state.shape[1])
    ground_after = jnp.concatenate([vel, st], 0).transpose(0, 2, 1, 3)
    return (from_strips_fast(air, 4, air_state.shape[1], vel.shape[1]), ground_after)


def solution(mesh):
    placed = (
        P(None, None, "py", "px"),
        P(None, "py", "px"),
        P(),
        P(),
        P(None, None, ("px", "py"), None),
        P(None, None, ("px", "py"), None),
        P(None, ("px", "py"), None),
    )
    return jax.shard_map(
        body,
        mesh=mesh,
        in_specs=placed,
        out_specs=(P(None, None, "py", "px"), P(None, None, ("px", "py"), None)),
        check_vma=False,
    )
```

```python
import functools
import os

import jax
import jax.numpy as jnp
from jax import lax
from jax.experimental import pallas as pl
from jax.experimental.pallas import tpu as pltpu
from jax.sharding import PartitionSpec as P

STEPS = 3
RING = ("px", "py")
INTERPRET = os.environ.get("STENCIL_INTERPRET") == "1"


def trade(to_left, to_right):
    n = lax.axis_size(RING)
    from_right = lax.ppermute(to_left, RING, [(i, i - 1) for i in range(1, n)])
    from_left = lax.ppermute(to_right, RING, [(i, i + 1) for i in range(n - 1)])
    return from_left, from_right


def to_strips(block):
    f, z, ny, nx = block.shape
    parts = lax.axis_size("py")
    split = block.reshape(f, z, ny, parts, nx // parts)
    moved = lax.all_to_all(split, "py", 3, 3, tiled=True)
    return moved.transpose(0, 4, 1, 3, 2).reshape(f, nx // parts, z, parts * ny)


def from_strips(strip):
    f, nx, z, ny_all = strip.shape
    parts = lax.axis_size("py")
    split = strip.reshape(f, nx, z, parts, ny_all // parts)
    moved = lax.all_to_all(split, "py", 3, 3, tiled=True)
    return moved.transpose(0, 2, 4, 3, 1).reshape(f, z, ny_all // parts, parts * nx)


def _rows(a):
    return lax.broadcasted_iota(jnp.int32, a.shape, 0)


def _lanes(a):
    return lax.broadcasted_iota(jnp.int32, a.shape, 1)


def bz(a):
    return jnp.where(_rows(a) == 0, 0.0, pltpu.roll(a, 1, 0))


def az(a):
    n = a.shape[0]
    return jnp.where(_rows(a) == n - 1, 0.0, pltpu.roll(a, n - 1, 0))


def by(a):
    return jnp.where(_lanes(a) == 0, 0.0, pltpu.roll(a, 1, 1))


def ay(a):
    n = a.shape[1]
    return jnp.where(_lanes(a) == n - 1, 0.0, pltpu.roll(a, n - 1, 1))


def one_step(
    air_ref, bulk_ref, vel_ref, st_ref, mod_ref, b_ref, bl_ref, br_ref, fl_ref, fr_ref, scal_ref,
    air_out, vel_out, st_out, tl_out, tr_out, coef_ref, after_edges=None,
):
    width = air_ref.shape[1]
    az_n = air_ref.shape[2]
    gz = vel_ref.shape[2]

    def fl(start, count):
        return fl_ref[pl.ds(start, count), :]

    def fr(start, count):
        return fr_ref[pl.ds(start, count), :]

    def gcol(field_ref, k, left, right):
        cols = [left] + [field_ref[k, c] for c in range(width)] + [right]
        return cols

    sxx = gcol(st_ref, 0, fl(0, gz), fr(0, gz))
    sxy = gcol(st_ref, 3, fl(gz, gz), fr(gz, gz))
    sxz = gcol(st_ref, 4, fl(2 * gz, gz), fr(2 * gz, gz))
    syy = gcol(st_ref, 1, None, fr(3 * gz, gz))
    syz = gcol(st_ref, 5, None, fr(4 * gz, gz))
    szz = gcol(st_ref, 2, None, fr(5 * gz, gz))
    vx = gcol(vel_ref, 0, fl(3 * gz, gz), None)
    vy = gcol(vel_ref, 1, None, fr(6 * gz, gz))
    vz = gcol(vel_ref, 2, None, fr(7 * gz, gz))
    bb = (
        [bl_ref[pl.ds(4 * gz + 5 * az_n, gz), :]]
        + [b_ref[c] for c in range(width)]
        + [br_ref[pl.ds(8 * gz + az_n, gz), :]]
    )
    o = 4 * gz
    pr = fr(8 * gz, az_n)
    u = [fl(o, az_n), fl(o + az_n, az_n)] + [air_ref[1, c] for c in range(width)]
    v = [None, fl(o + 2 * az_n, az_n)] + [air_ref[2, c] for c in range(width)]
    w = [None, fl(o + 3 * az_n, az_n)] + [air_ref[3, c] for c in range(width)]
    p = [None, fl(o + 4 * az_n, az_n)] + [air_ref[0, c] for c in range(width)] + [pr]

    grow = lax.broadcasted_iota(jnp.int32, (gz, sxx[1].shape[1]), 0)
    arow = lax.broadcasted_iota(jnp.int32, (az_n, sxx[1].shape[1]), 0)

    vx1 = [None] * (width + 2)
    vy1 = [None] * (width + 2)
    vz1 = [None] * (width + 2)
    for e in range(width + 2):
        if e <= width:
            force_x = sxx[e + 1] - sxx[e] + sxy[e] - by(sxy[e]) + sxz[e] - bz(sxz[e])
            vx1[e] = vx[e] + bb[e] * force_x
        if e >= 1:
            force_y = sxy[e] - sxy[e - 1] + ay(syy[e]) - syy[e] + syz[e] - bz(syz[e])
            vy1[e] = vy[e] + bb[e] * force_y
            plane = jnp.broadcast_to(p[e + 1][0:1, :], szz[e].shape)
            ghost = jnp.where(grow == gz - 1, -plane, pltpu.roll(szz[e], gz - 1, 0))
            force_z = sxz[e] - sxz[e - 1] + syz[e] - by(syz[e]) + ghost - szz[e]
            vz1[e] = vz[e] + bb[e] * force_z

    def ground_col(c):
        e = c + 1
        mx, my, mz = vx1[e], vy1[e], vz1[e]
        lam = mod_ref[0, c]
        mu = mod_ref[1, c]
        longitudinal = lam + 2.0 * mu
        strain_x = mx - vx1[e - 1]
        strain_y = my - by(my)
        strain_z = mz - bz(mz)
        st_out[0, c] = st_ref[0, c] + longitudinal * strain_x + lam * (strain_y + strain_z)
        st_out[1, c] = st_ref[1, c] + longitudinal * strain_y + lam * (strain_x + strain_z)
        st_out[2, c] = st_ref[2, c] + longitudinal * strain_z + lam * (strain_x + strain_y)
        st_out[3, c] = st_ref[3, c] + mu * (ay(mx) - mx + vy1[e + 1] - my)
        sxz1 = st_ref[4, c] + mu * (az(mx) - mx + vz1[e + 1] - mz)
        syz1 = st_ref[5, c] + mu * (az(my) - my + ay(mz) - mz)
        st_out[4, c] = jnp.where(grow == gz - 1, 0.0, sxz1)
        st_out[5, c] = jnp.where(grow == gz - 1, 0.0, syz1)
        vel_out[0, c] = mx
        vel_out[1, c] = my
        vel_out[2, c] = mz
        if c == 0 and tl_out is not None:
            for k, (ref, f) in enumerate(
                [(st_out, 0), (st_out, 3), (st_out, 4), (st_out, 1), (st_out, 5), (st_out, 2),
                 (vel_out, 1), (vel_out, 2)]
            ):
                tl_out[pl.ds(k * gz, gz), :] = ref[f, 0]
        if c == width - 1 and tr_out is not None:
            for k, (ref, f) in enumerate([(st_out, 0), (st_out, 3), (st_out, 4), (vel_out, 0)]):
                tr_out[pl.ds(k * gz, gz), :] = ref[f, c]

    wind_x = coef_ref[0]
    wind_y = coef_ref[1]
    lift = coef_ref[2]
    u1 = [None] * (width + 2)
    for a in range(1, width + 2):
        u1[a] = (
            u[a]
            - wind_x * (u[a] - u[a - 1])
            - wind_y * (u[a] - by(u[a]))
            - lift * (p[a + 1] - p[a])
        )
    u1[1] = jnp.where(scal_ref[3 * az_n] > 0.5, u1[1], 0.0)

    def air_col(c):
        a = c + 2
        v1 = v[a] - wind_x * (v[a] - v[a - 1]) - wind_y * (v[a] - by(v[a])) - lift * (ay(p[a]) - p[a])
        w1 = w[a] - wind_x * (w[a] - w[a - 1]) - wind_y * (w[a] - by(w[a])) - lift * (p[a] - bz(p[a]))
        surface = jnp.broadcast_to(vz1[c + 1][gz - 1 : gz, :], w1.shape)
        w1 = jnp.where(arow == 0, surface, w1)
        pm = p[a]
        p1 = (
            pm
            - wind_x * (pm - p[a - 1])
            - wind_y * (pm - by(pm))
            - bulk_ref[c] * ((u1[a] - u1[a - 1]) + (v1 - by(v1)) + (az(w1) - w1))
        )
        air_out[0, c] = p1
        air_out[1, c] = u1[a]
        air_out[2, c] = v1
        air_out[3, c] = w1
        if c == 0 and tl_out is not None:
            tl_out[pl.ds(8 * gz, az_n), :] = p1
        if c == width - 2 and tr_out is not None:
            tr_out[pl.ds(4 * gz, az_n), :] = u1[a]
        if c == width - 1 and tr_out is not None:
            o = 4 * gz
            tr_out[pl.ds(o + az_n, az_n), :] = u1[a]
            tr_out[pl.ds(o + 2 * az_n, az_n), :] = v1
            tr_out[pl.ds(o + 3 * az_n, az_n), :] = w1
            tr_out[pl.ds(o + 4 * az_n, az_n), :] = p1

    ground_edges = [0, width - 1]
    air_edges = [0, width - 2, width - 1]
    for c in ground_edges:
        ground_col(c)
    for c in air_edges:
        air_col(c)
    if after_edges is not None:
        after_edges()
    for c in range(width):
        if c not in ground_edges:
            ground_col(c)
    for c in range(width):
        if c not in air_edges:
            air_col(c)


MESH = pl.DeviceIdType.MESH


def send_layout_kernel(air_ref, bulk_ref, out_ref):
    fields = air_ref.shape[0]
    rows = air_ref.shape[1]
    nyl = out_ref.shape[1] // 16
    nz = rows // nyl
    parts = out_ref.shape[0]
    width = air_ref.shape[2] // parts
    for yl in range(nyl):
        m = jnp.concatenate(
            [air_ref[f, pl.ds(yl, nz, stride=nyl), :] for f in range(fields)], 0
        )
        t = m.T.reshape(parts, width, m.shape[0])
        out_ref[:, pl.ds(yl * width, width), :] = t
        mb = jnp.concatenate(
            [bulk_ref[pl.ds(yl, nz, stride=nyl), :], jnp.zeros((m.shape[0] - nz, m.shape[1]), jnp.float32)], 0
        )
        tb = mb.T.reshape(parts, width, m.shape[0])
        out_ref[:, pl.ds(nyl * width + yl * width, width), :] = tb


def recv_layout_kernel(width, nyl, pay_ref, out_ref):
    fields = out_ref.shape[0]
    parts = pay_ref.shape[0]
    nz = pay_ref.shape[2] // fields
    for yl in range(nyl):
        n = pay_ref[:, pl.ds(yl, width, stride=nyl), :].reshape(parts * width, fields * nz)
        t = n.T
        for f in range(fields):
            out_ref[f, pl.ds(yl, nz, stride=nyl), :] = t[f * nz : (f + 1) * nz]


def from_strips_fast(payload, fields, az_n, width):
    parts = payload.shape[0]
    nyl = payload.shape[1] // width
    got = lax.all_to_all(payload, "py", 0, 0, tiled=True)
    out = pl.pallas_call(
        functools.partial(recv_layout_kernel, width, nyl),
        out_shape=jax.ShapeDtypeStruct((fields, az_n * nyl, width * parts), jnp.float32),
        interpret=INTERPRET,
    )(got)
    return out.reshape(fields, az_n, nyl, width * parts)


def to_strips_fast(air_state, air_bulk):
    f, z, ny, nx = air_state.shape
    parts = lax.axis_size("py")
    width = nx // parts
    flat = air_state.reshape(f, z * ny, nx)
    bulk = air_bulk.reshape(z * ny, nx)
    payload = pl.pallas_call(
        send_layout_kernel,
        out_shape=jax.ShapeDtypeStruct((parts, 2 * ny * width, f * z), jnp.float32),
        interpret=INTERPRET,
    )(flat, bulk)
    return lax.all_to_all(payload, "py", 0, 0, tiled=True)


def fused_kernel(
    n_py, n_ring, blk_ref, bulkblk_ref, vel_ref, st_ref, mod_ref, b_ref, scal_ref,
    airblk_out, vel_out, st_out, pay_ref, pay_send, pay_out, pay_back, a2a_sem, air_ref, air_out,
    air_a, vel_a, st_a, air_b, vel_b, st_b, coef_ref, send_l, send_r, recv_l, recv_r,
    send_sem, recv_sem,
):
    width = air_ref.shape[1]
    az_n = air_ref.shape[2]
    gz = vel_ref.shape[2]
    ny = air_ref.shape[3]
    me = lax.axis_index("px") * n_py + lax.axis_index("py")
    has_left = me > 0
    has_right = me < n_ring - 1
    left = ((me - 1) // n_py, (me - 1) % n_py)
    right = ((me + 1) // n_py, (me + 1) % n_py)
    rows_l = send_l.shape[1]
    rows_r = send_r.shape[1]

    nyl = ny // n_py
    my_py = lax.axis_index("py")
    my_px = lax.axis_index("px")
    n_px = n_ring // n_py
    extra_l = (my_py == 0) & (my_px > 0)
    extra_r = (my_py == n_py - 1) & (my_px < n_px - 1)
    nz = az_n
    for yl in range(nyl):
        m = jnp.concatenate([blk_ref[f, pl.ds(yl, nz, stride=nyl), :] for f in range(4)], 0)
        pay_send[:, pl.ds(yl * width, width), :] = m.T.reshape(n_py, width, 4 * nz)
        mb = jnp.concatenate(
            [bulkblk_ref[pl.ds(yl, nz, stride=nyl), :], jnp.zeros((3 * nz, n_py * width), jnp.float32)], 0
        )
        pay_send[:, pl.ds(nyl * width + yl * width, width), :] = mb.T.reshape(n_py, width, 4 * nz)

    @pl.when(jnp.logical_not(has_left))
    def _():
        recv_l[...] = jnp.zeros_like(recv_l)

    @pl.when(jnp.logical_not(has_right))
    def _():
        recv_r[...] = jnp.zeros_like(recv_r)

    barrier = pltpu.get_barrier_semaphore()

    for q in range(n_py):

        @pl.when(my_py != q)
        def _():
            pl.semaphore_signal(barrier, inc=1, device_id=(my_px, q), device_id_type=MESH)

    @pl.when(extra_l)
    def _():
        pl.semaphore_signal(barrier, inc=1, device_id=left, device_id_type=MESH)

    @pl.when(extra_r)
    def _():
        pl.semaphore_signal(barrier, inc=1, device_id=right, device_id_type=MESH)

    for count in range(3):

        @pl.when(extra_l.astype(jnp.int32) + extra_r.astype(jnp.int32) == count)
        def _():
            pl.semaphore_wait(barrier, n_py - 1 + count)

    def group_copy(src, dst, k, q, slot):
        return pltpu.make_async_remote_copy(
            src_ref=src.at[q],
            dst_ref=dst.at[slot],
            send_sem=a2a_sem.at[k, q],
            recv_sem=a2a_sem.at[k + 1, slot],
            device_id=(my_px, q),
            device_id_type=MESH,
        )

    def group_send(src, dst, k):
        for q in range(n_py):

            @pl.when(my_py != q)
            def _():
                group_copy(src, dst, k, q, my_py).start()

        dst[my_py] = src[my_py]

    def group_wait(src, dst, k):
        for q in range(n_py):

            @pl.when(my_py != q)
            def _():
                group_copy(src, dst, k, q, q).wait_recv()

    def group_send_wait(src, dst, k):
        for q in range(n_py):

            @pl.when(my_py != q)
            def _():
                group_copy(src, dst, k, q, my_py).wait_send()

    group_send(pay_send, pay_ref, 0)
    group_wait(pay_send, pay_ref, 0)
    for xl in range(width):
        n_air = pay_ref[:, pl.ds(xl, nyl, stride=width), :].reshape(ny, 4 * az_n)
        t = n_air.T
        for f in range(4):
            air_ref[f, xl] = t[f * az_n : (f + 1) * az_n]
        n_bulk = pay_ref[:, pl.ds(nyl * width + xl, nyl, stride=width), :].reshape(ny, 4 * az_n)
        air_ref[4, xl] = n_bulk.T[0:az_n]


    for k in range(3):
        for z in range(az_n):
            coef_ref[k, pl.ds(z, 1), :] = jnp.full((1, ny), scal_ref[k * az_n + z], jnp.float32)

    tl = send_l.at[0]
    tr = send_r.at[0]
    left_rows = [st_ref[f, 0] for f in (0, 3, 4, 1, 5, 2)] + [vel_ref[1, 0], vel_ref[2, 0]]
    for k, value in enumerate(left_rows):
        tl[pl.ds(k * gz, gz), :] = value
    tl[pl.ds(8 * gz, az_n), :] = air_ref[0, 0]
    tl[pl.ds(8 * gz + az_n, gz), :] = b_ref[0]
    right_rows = [st_ref[f, width - 1] for f in (0, 3, 4)] + [vel_ref[0, width - 1]]
    for k, value in enumerate(right_rows):
        tr[pl.ds(k * gz, gz), :] = value
    o = 4 * gz
    tr[pl.ds(o, az_n), :] = air_ref[1, width - 2]
    for k, f in enumerate((1, 2, 3, 0)):
        tr[pl.ds(o + (k + 1) * az_n, az_n), :] = air_ref[f, width - 1]
    tr[pl.ds(o + 5 * az_n, gz), :] = b_ref[width - 1]

    def copies(n, count_l, count_r):
        to_left = pltpu.make_async_remote_copy(
            src_ref=send_l.at[n, pl.ds(0, count_l)],
            dst_ref=recv_r.at[n, pl.ds(0, count_l)],
            send_sem=send_sem.at[n, 0],
            recv_sem=recv_sem.at[n, 1],
            device_id=left,
            device_id_type=MESH,
        )
        to_right = pltpu.make_async_remote_copy(
            src_ref=send_r.at[n, pl.ds(0, count_r)],
            dst_ref=recv_l.at[n, pl.ds(0, count_r)],
            send_sem=send_sem.at[n, 1],
            recv_sem=recv_sem.at[n, 0],
            device_id=right,
            device_id_type=MESH,
        )

        return to_left, to_right

    def start(n, count_l, count_r):
        to_left, to_right = copies(n, count_l, count_r)

        @pl.when(has_left)
        def _():
            to_left.start()

        @pl.when(has_right)
        def _():
            to_right.start()

    def wait_recv(n, count_l, count_r):
        to_left, to_right = copies(n, count_l, count_r)

        @pl.when(has_left)
        def _():
            to_right.wait_recv()

        @pl.when(has_right)
        def _():
            to_left.wait_recv()

    def wait_send(n, count_l, count_r):
        to_left, to_right = copies(n, count_l, count_r)

        @pl.when(has_left)
        def _():
            to_left.wait_send()

        @pl.when(has_right)
        def _():
            to_right.wait_send()

    full_l = 8 * gz + az_n
    full_r = 4 * gz + 5 * az_n
    counts = [(rows_l, rows_r)] + [(full_l, full_r)] * (STEPS - 1)
    start(0, *counts[0])
    wait_recv(0, *counts[0])
    states = [
        (air_ref, vel_ref, st_ref),
        (air_a, vel_a, st_a),
        (air_b, vel_b, st_b),
        (air_out, vel_out, st_out),
    ]
    for n in range(STEPS):
        src = states[n] if n < len(states) - 1 else states[-2]
        dst = states[n + 1] if n + 1 < STEPS else states[-1]
        last = n + 1 == STEPS
        one_step(
            src[0], air_ref.at[4], src[1], src[2], mod_ref, b_ref, recv_l.at[0], recv_r.at[0],
            recv_l.at[n], recv_r.at[n], scal_ref, dst[0], dst[1], dst[2],
            None if last else send_l.at[n + 1], None if last else send_r.at[n + 1], coef_ref,
            None if last else functools.partial(start, n + 1, *counts[n + 1]),
        )
        if not last:
            wait_recv(n + 1, *counts[n + 1])
    for xl in range(width):
        m = jnp.concatenate([air_out[f, xl] for f in range(4)], 0)
        t = m.T.reshape(n_py, nyl, 4 * az_n)
        pay_out[:, pl.ds(xl * nyl, nyl), :] = t
    group_send(pay_out, pay_back, 2)
    group_wait(pay_out, pay_back, 2)
    for yl in range(nyl):
        nb = pay_back[:, pl.ds(yl, width, stride=nyl), :].reshape(n_py * width, 4 * nz)
        tb = nb.T
        for f in range(4):
            airblk_out[f, pl.ds(yl, nz, stride=nyl), :] = tb[f * nz : (f + 1) * nz]
    for n in range(STEPS):
        wait_send(n, *counts[n])
    group_send_wait(pay_send, pay_ref, 0)
    group_send_wait(pay_out, pay_back, 2)


def fused(blk, bulkblk, vel, st, mod, b, scal, az_n):
    n_py = lax.axis_size("py")
    n_ring = lax.axis_size(RING)
    gz = st.shape[2]
    nyl = blk.shape[1] // az_n
    ny = nyl * n_py
    width = vel.shape[1]
    fields = (4, width, az_n, ny)
    rows_l = 9 * gz + az_n
    rows_r = 5 * gz + 5 * az_n
    vmem = pl.BlockSpec(memory_space=pltpu.VMEM)
    return pl.pallas_call(
        functools.partial(fused_kernel, n_py, n_ring),
        out_shape=(
            jax.ShapeDtypeStruct(blk.shape, jnp.float32),
            jax.ShapeDtypeStruct(vel.shape, jnp.float32),
            jax.ShapeDtypeStruct(st.shape, jnp.float32),
        ),
        in_specs=[vmem] * 6 + [pl.BlockSpec(memory_space=pltpu.SMEM)],
        out_specs=(vmem, vmem, vmem),
        scratch_shapes=[
            pltpu.VMEM((n_py, 2 * nyl * width, 4 * az_n), jnp.float32),
            pltpu.VMEM((n_py, 2 * nyl * width, 4 * az_n), jnp.float32),
            pltpu.VMEM((n_py, nyl * width, 4 * az_n), jnp.float32),
            pltpu.VMEM((n_py, nyl * width, 4 * az_n), jnp.float32),
            pltpu.SemaphoreType.DMA((4, n_py)),
            pltpu.VMEM((5, width, az_n, ny), jnp.float32),
            pltpu.VMEM(fields, jnp.float32),
            pltpu.VMEM(fields, jnp.float32),
            pltpu.VMEM(vel.shape, jnp.float32),
            pltpu.VMEM(st.shape, jnp.float32),
            pltpu.VMEM(fields, jnp.float32),
            pltpu.VMEM(vel.shape, jnp.float32),
            pltpu.VMEM(st.shape, jnp.float32),
            pltpu.VMEM((3, az_n, ny), jnp.float32),
            pltpu.VMEM((STEPS, rows_l, ny), jnp.float32),
            pltpu.VMEM((STEPS, rows_r, ny), jnp.float32),
            pltpu.VMEM((STEPS, rows_r, ny), jnp.float32),
            pltpu.VMEM((STEPS, rows_l, ny), jnp.float32),
            pltpu.SemaphoreType.DMA((STEPS, 2)),
            pltpu.SemaphoreType.DMA((STEPS, 2)),
        ],
        compiler_params=pltpu.CompilerParams(collective_id=0, has_side_effects=True),
        interpret=INTERPRET,
    )(blk, bulkblk, vel, st, mod, b, scal)


def body(air_state, air_bulk, air_buoyancy, air_wind, ground_state, ground_moduli, ground_buoyancy):
    west_edge = (lax.axis_index("px") == 0) & (lax.axis_index("py") == 0)
    f_n, az_n, ny_l, nx_l = air_state.shape
    blk = air_state.reshape(f_n, az_n * ny_l, nx_l)
    bulkblk = air_bulk.reshape(az_n * ny_l, nx_l)
    ground = ground_state.transpose(0, 2, 1, 3)
    gz = ground.shape[2]
    vel = ground[:3]
    st = ground[3:]
    top = lax.broadcasted_iota(jnp.int32, st.shape, 2) == gz - 1
    clear = top & (lax.broadcasted_iota(jnp.int32, st.shape, 0) >= 4)
    st = jnp.where(clear, jnp.zeros_like(st), st)
    mod = ground_moduli.transpose(0, 2, 1, 3)
    b = ground_buoyancy.transpose(1, 0, 2)
    scal = jnp.concatenate(
        [air_wind[0], air_wind[1], air_buoyancy, jnp.where(west_edge, 0.0, 1.0)[None]]
    ).astype(jnp.float32)
    air, vel, st = fused(blk, bulkblk, vel, st, mod, b, scal, az_n)
    ground_after = jnp.concatenate([vel, st], 0).transpose(0, 2, 1, 3)
    return (air.reshape(air_state.shape), ground_after)


def solution(mesh):
    placed = (
        P(None, None, "py", "px"),
        P(None, "py", "px"),
        P(),
        P(),
        P(None, None, ("px", "py"), None),
        P(None, None, ("px", "py"), None),
        P(None, ("px", "py"), None),
    )
    return jax.shard_map(
        body,
        mesh=mesh,
        in_specs=placed,
        out_specs=(P(None, None, "py", "px"), P(None, None, ("px", "py"), None)),
        check_vma=False,
    )
```

```python
import functools
import os

import jax
import jax.numpy as jnp
from jax import lax
from jax.experimental import pallas as pl
from jax.experimental.pallas import tpu as pltpu
from jax.sharding import PartitionSpec as P

STEPS = 3
RING = ("px", "py")
INTERPRET = os.environ.get("STENCIL_INTERPRET") == "1"


def trade(to_left, to_right):
    n = lax.axis_size(RING)
    from_right = lax.ppermute(to_left, RING, [(i, i - 1) for i in range(1, n)])
    from_left = lax.ppermute(to_right, RING, [(i, i + 1) for i in range(n - 1)])
    return from_left, from_right


def to_strips(block):
    f, z, ny, nx = block.shape
    parts = lax.axis_size("py")
    split = block.reshape(f, z, ny, parts, nx // parts)
    moved = lax.all_to_all(split, "py", 3, 3, tiled=True)
    return moved.transpose(0, 4, 1, 3, 2).reshape(f, nx // parts, z, parts * ny)


def from_strips(strip):
    f, nx, z, ny_all = strip.shape
    parts = lax.axis_size("py")
    split = strip.reshape(f, nx, z, parts, ny_all // parts)
    moved = lax.all_to_all(split, "py", 3, 3, tiled=True)
    return moved.transpose(0, 2, 4, 3, 1).reshape(f, z, ny_all // parts, parts * nx)


def _rows(a):
    return lax.broadcasted_iota(jnp.int32, a.shape, 0)


def _lanes(a):
    return lax.broadcasted_iota(jnp.int32, a.shape, 1)


def bz(a):
    return jnp.where(_rows(a) == 0, 0.0, pltpu.roll(a, 1, 0))


def az(a):
    n = a.shape[0]
    return jnp.where(_rows(a) == n - 1, 0.0, pltpu.roll(a, n - 1, 0))


def by(a):
    return jnp.where(_lanes(a) == 0, 0.0, pltpu.roll(a, 1, 1))


def ay(a):
    n = a.shape[1]
    return jnp.where(_lanes(a) == n - 1, 0.0, pltpu.roll(a, n - 1, 1))


def one_step(
    air_ref, bulk_ref, vel_ref, st_ref, mod_ref, b_ref, bl_ref, br_ref, fl_ref, fr_ref, scal_ref,
    air_out, vel_out, st_out, tl_out, tr_out, coef_ref, after_edges=None,
):
    width = air_ref.shape[1]
    az_n = air_ref.shape[2]
    gz = vel_ref.shape[2]

    def fl(start, count):
        return fl_ref[pl.ds(start, count), :]

    def fr(start, count):
        return fr_ref[pl.ds(start, count), :]

    def gcol(field_ref, k, left, right):
        cols = [left] + [field_ref[k, c] for c in range(width)] + [right]
        return cols

    sxx = gcol(st_ref, 0, fl(0, gz), fr(0, gz))
    sxy = gcol(st_ref, 3, fl(gz, gz), fr(gz, gz))
    sxz = gcol(st_ref, 4, fl(2 * gz, gz), fr(2 * gz, gz))
    syy = gcol(st_ref, 1, None, fr(3 * gz, gz))
    syz = gcol(st_ref, 5, None, fr(4 * gz, gz))
    szz = gcol(st_ref, 2, None, fr(5 * gz, gz))
    vx = gcol(vel_ref, 0, fl(3 * gz, gz), None)
    vy = gcol(vel_ref, 1, None, fr(6 * gz, gz))
    vz = gcol(vel_ref, 2, None, fr(7 * gz, gz))
    bb = (
        [bl_ref[pl.ds(4 * gz + 5 * az_n, gz), :]]
        + [b_ref[c] for c in range(width)]
        + [br_ref[pl.ds(8 * gz + az_n, gz), :]]
    )
    o = 4 * gz
    pr = fr(8 * gz, az_n)
    u = [fl(o, az_n), fl(o + az_n, az_n)] + [air_ref[1, c] for c in range(width)]
    v = [None, fl(o + 2 * az_n, az_n)] + [air_ref[2, c] for c in range(width)]
    w = [None, fl(o + 3 * az_n, az_n)] + [air_ref[3, c] for c in range(width)]
    p = [None, fl(o + 4 * az_n, az_n)] + [air_ref[0, c] for c in range(width)] + [pr]

    grow = lax.broadcasted_iota(jnp.int32, (gz, sxx[1].shape[1]), 0)
    arow = lax.broadcasted_iota(jnp.int32, (az_n, sxx[1].shape[1]), 0)

    vx1 = [None] * (width + 2)
    vy1 = [None] * (width + 2)
    vz1 = [None] * (width + 2)
    for e in range(width + 2):
        if e <= width:
            force_x = sxx[e + 1] - sxx[e] + sxy[e] - by(sxy[e]) + sxz[e] - bz(sxz[e])
            vx1[e] = vx[e] + bb[e] * force_x
        if e >= 1:
            force_y = sxy[e] - sxy[e - 1] + ay(syy[e]) - syy[e] + syz[e] - bz(syz[e])
            vy1[e] = vy[e] + bb[e] * force_y
            plane = jnp.broadcast_to(p[e + 1][0:1, :], szz[e].shape)
            ghost = jnp.where(grow == gz - 1, -plane, pltpu.roll(szz[e], gz - 1, 0))
            force_z = sxz[e] - sxz[e - 1] + syz[e] - by(syz[e]) + ghost - szz[e]
            vz1[e] = vz[e] + bb[e] * force_z

    def ground_col(c):
        e = c + 1
        mx, my, mz = vx1[e], vy1[e], vz1[e]
        lam = mod_ref[0, c]
        mu = mod_ref[1, c]
        longitudinal = lam + 2.0 * mu
        strain_x = mx - vx1[e - 1]
        strain_y = my - by(my)
        strain_z = mz - bz(mz)
        st_out[0, c] = st_ref[0, c] + longitudinal * strain_x + lam * (strain_y + strain_z)
        st_out[1, c] = st_ref[1, c] + longitudinal * strain_y + lam * (strain_x + strain_z)
        st_out[2, c] = st_ref[2, c] + longitudinal * strain_z + lam * (strain_x + strain_y)
        st_out[3, c] = st_ref[3, c] + mu * (ay(mx) - mx + vy1[e + 1] - my)
        sxz1 = st_ref[4, c] + mu * (az(mx) - mx + vz1[e + 1] - mz)
        syz1 = st_ref[5, c] + mu * (az(my) - my + ay(mz) - mz)
        st_out[4, c] = jnp.where(grow == gz - 1, 0.0, sxz1)
        st_out[5, c] = jnp.where(grow == gz - 1, 0.0, syz1)
        vel_out[0, c] = mx
        vel_out[1, c] = my
        vel_out[2, c] = mz
        if c == 0 and tl_out is not None:
            for k, (ref, f) in enumerate(
                [(st_out, 0), (st_out, 3), (st_out, 4), (st_out, 1), (st_out, 5), (st_out, 2),
                 (vel_out, 1), (vel_out, 2)]
            ):
                tl_out[pl.ds(k * gz, gz), :] = ref[f, 0]
        if c == width - 1 and tr_out is not None:
            for k, (ref, f) in enumerate([(st_out, 0), (st_out, 3), (st_out, 4), (vel_out, 0)]):
                tr_out[pl.ds(k * gz, gz), :] = ref[f, c]

    wind_x = coef_ref[0]
    wind_y = coef_ref[1]
    lift = coef_ref[2]
    u1 = [None] * (width + 2)
    for a in range(1, width + 2):
        u1[a] = (
            u[a]
            - wind_x * (u[a] - u[a - 1])
            - wind_y * (u[a] - by(u[a]))
            - lift * (p[a + 1] - p[a])
        )
    u1[1] = jnp.where(scal_ref[3 * az_n] > 0.5, u1[1], 0.0)

    def air_col(c):
        a = c + 2
        v1 = v[a] - wind_x * (v[a] - v[a - 1]) - wind_y * (v[a] - by(v[a])) - lift * (ay(p[a]) - p[a])
        w1 = w[a] - wind_x * (w[a] - w[a - 1]) - wind_y * (w[a] - by(w[a])) - lift * (p[a] - bz(p[a]))
        surface = jnp.broadcast_to(vz1[c + 1][gz - 1 : gz, :], w1.shape)
        w1 = jnp.where(arow == 0, surface, w1)
        pm = p[a]
        p1 = (
            pm
            - wind_x * (pm - p[a - 1])
            - wind_y * (pm - by(pm))
            - bulk_ref[c] * ((u1[a] - u1[a - 1]) + (v1 - by(v1)) + (az(w1) - w1))
        )
        air_out[0, c] = p1
        air_out[1, c] = u1[a]
        air_out[2, c] = v1
        air_out[3, c] = w1
        if c == 0 and tl_out is not None:
            tl_out[pl.ds(8 * gz, az_n), :] = p1
        if c == width - 2 and tr_out is not None:
            tr_out[pl.ds(4 * gz, az_n), :] = u1[a]
        if c == width - 1 and tr_out is not None:
            o = 4 * gz
            tr_out[pl.ds(o + az_n, az_n), :] = u1[a]
            tr_out[pl.ds(o + 2 * az_n, az_n), :] = v1
            tr_out[pl.ds(o + 3 * az_n, az_n), :] = w1
            tr_out[pl.ds(o + 4 * az_n, az_n), :] = p1

    ground_edges = [0, width - 1]
    air_edges = [0, width - 2, width - 1]
    for c in ground_edges:
        ground_col(c)
    for c in air_edges:
        air_col(c)
    if after_edges is not None:
        after_edges()
    for c in range(width):
        if c not in ground_edges:
            ground_col(c)
    for c in range(width):
        if c not in air_edges:
            air_col(c)


MESH = pl.DeviceIdType.MESH


def send_layout_kernel(air_ref, bulk_ref, out_ref):
    fields = air_ref.shape[0]
    rows = air_ref.shape[1]
    nyl = out_ref.shape[1] // 16
    nz = rows // nyl
    parts = out_ref.shape[0]
    width = air_ref.shape[2] // parts
    for yl in range(nyl):
        m = jnp.concatenate(
            [air_ref[f, pl.ds(yl, nz, stride=nyl), :] for f in range(fields)], 0
        )
        t = m.T.reshape(parts, width, m.shape[0])
        out_ref[:, pl.ds(yl * width, width), :] = t
        mb = jnp.concatenate(
            [bulk_ref[pl.ds(yl, nz, stride=nyl), :], jnp.zeros((m.shape[0] - nz, m.shape[1]), jnp.float32)], 0
        )
        tb = mb.T.reshape(parts, width, m.shape[0])
        out_ref[:, pl.ds(nyl * width + yl * width, width), :] = tb


def recv_layout_kernel(width, nyl, pay_ref, out_ref):
    fields = out_ref.shape[0]
    parts = pay_ref.shape[0]
    nz = pay_ref.shape[2] // fields
    for yl in range(nyl):
        n = pay_ref[:, pl.ds(yl, width, stride=nyl), :].reshape(parts * width, fields * nz)
        t = n.T
        for f in range(fields):
            out_ref[f, pl.ds(yl, nz, stride=nyl), :] = t[f * nz : (f + 1) * nz]


def from_strips_fast(payload, fields, az_n, width):
    parts = payload.shape[0]
    nyl = payload.shape[1] // width
    got = lax.all_to_all(payload, "py", 0, 0, tiled=True)
    out = pl.pallas_call(
        functools.partial(recv_layout_kernel, width, nyl),
        out_shape=jax.ShapeDtypeStruct((fields, az_n * nyl, width * parts), jnp.float32),
        interpret=INTERPRET,
    )(got)
    return out.reshape(fields, az_n, nyl, width * parts)


def to_strips_fast(air_state, air_bulk):
    f, z, ny, nx = air_state.shape
    parts = lax.axis_size("py")
    width = nx // parts
    flat = air_state.reshape(f, z * ny, nx)
    bulk = air_bulk.reshape(z * ny, nx)
    payload = pl.pallas_call(
        send_layout_kernel,
        out_shape=jax.ShapeDtypeStruct((parts, 2 * ny * width, f * z), jnp.float32),
        interpret=INTERPRET,
    )(flat, bulk)
    return lax.all_to_all(payload, "py", 0, 0, tiled=True)


class Strided:
    def __init__(self, ref, layers, width, offset=0, fields=None, clear=()):
        self.ref = ref
        self.layers = layers
        self.width = width
        self.offset = offset
        self.clear = clear
        n = ref.shape[0] - offset if fields is None else fields
        self.shape = (n, width, layers, ref.shape[-1])

    def _rows(self, c):
        return pl.ds(c, self.layers, stride=self.width)

    def __getitem__(self, index):
        f, c = index
        value = self.ref[self.offset + f, self._rows(c), :]
        if f in self.clear:
            top = lax.broadcasted_iota(jnp.int32, value.shape, 0) == self.layers - 1
            value = jnp.where(top, 0.0, value)
        return value

    def __setitem__(self, index, value):
        f, c = index
        self.ref[self.offset + f, self._rows(c), :] = value


class Plane:
    def __init__(self, ref, layers, width):
        self.ref = ref
        self.layers = layers
        self.width = width

    def __getitem__(self, c):
        return self.ref[pl.ds(c, self.layers, stride=self.width), :]


class Scalars:
    def __init__(self, wind_ref, lift_ref, keep):
        self.wind_ref = wind_ref
        self.lift_ref = lift_ref
        self.keep = keep
        self.levels = lift_ref.shape[0]

    def __getitem__(self, i):
        n = self.levels
        if i < 2 * n:
            return self.wind_ref[i // n, i % n]
        if i < 3 * n:
            return self.lift_ref[i - 2 * n]
        return self.keep


def fused_kernel(
    n_py, n_ring, gz, width, blk_ref, bulkblk_ref, gin_ref, modin_ref, bin_ref, wind_ref, lift_ref,
    airblk_out, gout_ref, pay_ref, pay_send, pay_out, pay_back, a2a_sem, air_ref, air_out,
    air_a, vel_a, st_a, air_b, vel_b, st_b, coef_ref, send_l, send_r, recv_l, recv_r,
    send_sem, recv_sem,
):
    az_n = air_ref.shape[2]
    ny = air_ref.shape[3]
    me = lax.axis_index("px") * n_py + lax.axis_index("py")
    vel_ref = Strided(gin_ref, gz, width, 0, 3)
    st_ref = Strided(gin_ref, gz, width, 3, 6, clear=(4, 5))
    mod_ref = Strided(modin_ref, gz, width)
    b_ref = Plane(bin_ref, gz, width)
    vel_out = Strided(gout_ref, gz, width, 0, 3)
    st_out = Strided(gout_ref, gz, width, 3, 6)
    scal_ref = Scalars(wind_ref, lift_ref, jnp.where(me > 0, 1.0, 0.0))
    has_left = me > 0
    has_right = me < n_ring - 1
    left = ((me - 1) // n_py, (me - 1) % n_py)
    right = ((me + 1) // n_py, (me + 1) % n_py)
    rows_l = send_l.shape[1]
    rows_r = send_r.shape[1]

    nyl = ny // n_py
    my_py = lax.axis_index("py")
    my_px = lax.axis_index("px")
    n_px = n_ring // n_py
    extra_l = (my_py == 0) & (my_px > 0)
    extra_r = (my_py == n_py - 1) & (my_px < n_px - 1)
    nz = az_n
    for yl in range(nyl):
        m = jnp.concatenate([blk_ref[f, pl.ds(yl, nz, stride=nyl), :] for f in range(4)], 0)
        pay_send[:, pl.ds(yl * width, width), :] = m.T.reshape(n_py, width, 4 * nz)
        mb = jnp.concatenate(
            [bulkblk_ref[pl.ds(yl, nz, stride=nyl), :], jnp.zeros((3 * nz, n_py * width), jnp.float32)], 0
        )
        pay_send[:, pl.ds(nyl * width + yl * width, width), :] = mb.T.reshape(n_py, width, 4 * nz)

    @pl.when(jnp.logical_not(has_left))
    def _():
        recv_l[...] = jnp.zeros_like(recv_l)

    @pl.when(jnp.logical_not(has_right))
    def _():
        recv_r[...] = jnp.zeros_like(recv_r)

    barrier = pltpu.get_barrier_semaphore()

    for q in range(n_py):

        @pl.when(my_py != q)
        def _():
            pl.semaphore_signal(barrier, inc=1, device_id=(my_px, q), device_id_type=MESH)

    @pl.when(extra_l)
    def _():
        pl.semaphore_signal(barrier, inc=1, device_id=left, device_id_type=MESH)

    @pl.when(extra_r)
    def _():
        pl.semaphore_signal(barrier, inc=1, device_id=right, device_id_type=MESH)

    for count in range(3):

        @pl.when(extra_l.astype(jnp.int32) + extra_r.astype(jnp.int32) == count)
        def _():
            pl.semaphore_wait(barrier, n_py - 1 + count)

    def group_copy(src, dst, k, q, slot):
        return pltpu.make_async_remote_copy(
            src_ref=src.at[q],
            dst_ref=dst.at[slot],
            send_sem=a2a_sem.at[k, q],
            recv_sem=a2a_sem.at[k + 1, slot],
            device_id=(my_px, q),
            device_id_type=MESH,
        )

    def group_send(src, dst, k):
        for q in range(n_py):

            @pl.when(my_py != q)
            def _():
                group_copy(src, dst, k, q, my_py).start()

        dst[my_py] = src[my_py]

    def group_wait(src, dst, k):
        for q in range(n_py):

            @pl.when(my_py != q)
            def _():
                group_copy(src, dst, k, q, q).wait_recv()

    def group_send_wait(src, dst, k):
        for q in range(n_py):

            @pl.when(my_py != q)
            def _():
                group_copy(src, dst, k, q, my_py).wait_send()

    group_send(pay_send, pay_ref, 0)
    group_wait(pay_send, pay_ref, 0)
    for xl in range(width):
        n_air = pay_ref[:, pl.ds(xl, nyl, stride=width), :].reshape(ny, 4 * az_n)
        t = n_air.T
        for f in range(4):
            air_ref[f, xl] = t[f * az_n : (f + 1) * az_n]
        n_bulk = pay_ref[:, pl.ds(nyl * width + xl, nyl, stride=width), :].reshape(ny, 4 * az_n)
        air_ref[4, xl] = n_bulk.T[0:az_n]


    for k in range(3):
        for z in range(az_n):
            coef_ref[k, pl.ds(z, 1), :] = jnp.full((1, ny), scal_ref[k * az_n + z], jnp.float32)

    tl = send_l.at[0]
    tr = send_r.at[0]
    left_rows = [st_ref[f, 0] for f in (0, 3, 4, 1, 5, 2)] + [vel_ref[1, 0], vel_ref[2, 0]]
    for k, value in enumerate(left_rows):
        tl[pl.ds(k * gz, gz), :] = value
    tl[pl.ds(8 * gz, az_n), :] = air_ref[0, 0]
    tl[pl.ds(8 * gz + az_n, gz), :] = b_ref[0]
    right_rows = [st_ref[f, width - 1] for f in (0, 3, 4)] + [vel_ref[0, width - 1]]
    for k, value in enumerate(right_rows):
        tr[pl.ds(k * gz, gz), :] = value
    o = 4 * gz
    tr[pl.ds(o, az_n), :] = air_ref[1, width - 2]
    for k, f in enumerate((1, 2, 3, 0)):
        tr[pl.ds(o + (k + 1) * az_n, az_n), :] = air_ref[f, width - 1]
    tr[pl.ds(o + 5 * az_n, gz), :] = b_ref[width - 1]

    def copies(n, count_l, count_r):
        to_left = pltpu.make_async_remote_copy(
            src_ref=send_l.at[n, pl.ds(0, count_l)],
            dst_ref=recv_r.at[n, pl.ds(0, count_l)],
            send_sem=send_sem.at[n, 0],
            recv_sem=recv_sem.at[n, 1],
            device_id=left,
            device_id_type=MESH,
        )
        to_right = pltpu.make_async_remote_copy(
            src_ref=send_r.at[n, pl.ds(0, count_r)],
            dst_ref=recv_l.at[n, pl.ds(0, count_r)],
            send_sem=send_sem.at[n, 1],
            recv_sem=recv_sem.at[n, 0],
            device_id=right,
            device_id_type=MESH,
        )

        return to_left, to_right

    def start(n, count_l, count_r):
        to_left, to_right = copies(n, count_l, count_r)

        @pl.when(has_left)
        def _():
            to_left.start()

        @pl.when(has_right)
        def _():
            to_right.start()

    def wait_recv(n, count_l, count_r):
        to_left, to_right = copies(n, count_l, count_r)

        @pl.when(has_left)
        def _():
            to_right.wait_recv()

        @pl.when(has_right)
        def _():
            to_left.wait_recv()

    def wait_send(n, count_l, count_r):
        to_left, to_right = copies(n, count_l, count_r)

        @pl.when(has_left)
        def _():
            to_left.wait_send()

        @pl.when(has_right)
        def _():
            to_right.wait_send()

    full_l = 8 * gz + az_n
    full_r = 4 * gz + 5 * az_n
    counts = [(rows_l, rows_r)] + [(full_l, full_r)] * (STEPS - 1)
    start(0, *counts[0])
    wait_recv(0, *counts[0])
    states = [
        (air_ref, vel_ref, st_ref),
        (air_a, vel_a, st_a),
        (air_b, vel_b, st_b),
        (air_out, vel_out, st_out),
    ]
    for n in range(STEPS):
        src = states[n] if n < len(states) - 1 else states[-2]
        dst = states[n + 1] if n + 1 < STEPS else states[-1]
        last = n + 1 == STEPS
        one_step(
            src[0], air_ref.at[4], src[1], src[2], mod_ref, b_ref, recv_l.at[0], recv_r.at[0],
            recv_l.at[n], recv_r.at[n], scal_ref, dst[0], dst[1], dst[2],
            None if last else send_l.at[n + 1], None if last else send_r.at[n + 1], coef_ref,
            None if last else functools.partial(start, n + 1, *counts[n + 1]),
        )
        if not last:
            wait_recv(n + 1, *counts[n + 1])
    for xl in range(width):
        m = jnp.concatenate([air_out[f, xl] for f in range(4)], 0)
        t = m.T.reshape(n_py, nyl, 4 * az_n)
        pay_out[:, pl.ds(xl * nyl, nyl), :] = t
    group_send(pay_out, pay_back, 2)
    group_wait(pay_out, pay_back, 2)
    for yl in range(nyl):
        nb = pay_back[:, pl.ds(yl, width, stride=nyl), :].reshape(n_py * width, 4 * nz)
        tb = nb.T
        for f in range(4):
            airblk_out[f, pl.ds(yl, nz, stride=nyl), :] = tb[f * nz : (f + 1) * nz]
    for n in range(STEPS):
        wait_send(n, *counts[n])
    group_send_wait(pay_send, pay_ref, 0)
    group_send_wait(pay_out, pay_back, 2)


def fused(blk, bulkblk, ground, mod, b, wind, lift, az_n, gz, width):
    n_py = lax.axis_size("py")
    n_ring = lax.axis_size(RING)
    nyl = blk.shape[1] // az_n
    ny = nyl * n_py
    fields = (4, width, az_n, ny)
    rows_l = 9 * gz + az_n
    rows_r = 5 * gz + 5 * az_n
    vmem = pl.BlockSpec(memory_space=pltpu.VMEM)
    return pl.pallas_call(
        functools.partial(fused_kernel, n_py, n_ring, gz, width),
        out_shape=(
            jax.ShapeDtypeStruct(blk.shape, jnp.float32),
            jax.ShapeDtypeStruct(ground.shape, jnp.float32),
        ),
        in_specs=[vmem] * 5 + [pl.BlockSpec(memory_space=pltpu.SMEM)] * 2,
        out_specs=(vmem, vmem),
        scratch_shapes=[
            pltpu.VMEM((n_py, 2 * nyl * width, 4 * az_n), jnp.float32),
            pltpu.VMEM((n_py, 2 * nyl * width, 4 * az_n), jnp.float32),
            pltpu.VMEM((n_py, nyl * width, 4 * az_n), jnp.float32),
            pltpu.VMEM((n_py, nyl * width, 4 * az_n), jnp.float32),
            pltpu.SemaphoreType.DMA((4, n_py)),
            pltpu.VMEM((5, width, az_n, ny), jnp.float32),
            pltpu.VMEM(fields, jnp.float32),
            pltpu.VMEM(fields, jnp.float32),
            pltpu.VMEM((3, width, gz, ny), jnp.float32),
            pltpu.VMEM((6, width, gz, ny), jnp.float32),
            pltpu.VMEM(fields, jnp.float32),
            pltpu.VMEM((3, width, gz, ny), jnp.float32),
            pltpu.VMEM((6, width, gz, ny), jnp.float32),
            pltpu.VMEM((3, az_n, ny), jnp.float32),
            pltpu.VMEM((STEPS, rows_l, ny), jnp.float32),
            pltpu.VMEM((STEPS, rows_r, ny), jnp.float32),
            pltpu.VMEM((STEPS, rows_r, ny), jnp.float32),
            pltpu.VMEM((STEPS, rows_l, ny), jnp.float32),
            pltpu.SemaphoreType.DMA((STEPS, 2)),
            pltpu.SemaphoreType.DMA((STEPS, 2)),
        ],
        compiler_params=pltpu.CompilerParams(collective_id=0, has_side_effects=True),
        interpret=INTERPRET,
    )(blk, bulkblk, ground, mod, b, wind, lift)


def body(air_state, air_bulk, air_buoyancy, air_wind, ground_state, ground_moduli, ground_buoyancy):
    f_n, az_n, ny_l, nx_l = air_state.shape
    nf, gz, width, ny = ground_state.shape
    blk = air_state.reshape(f_n, az_n * ny_l, nx_l)
    bulkblk = air_bulk.reshape(az_n * ny_l, nx_l)
    ground = ground_state.reshape(nf, gz * width, ny)
    mod = ground_moduli.reshape(ground_moduli.shape[0], gz * width, ny)
    b = ground_buoyancy.reshape(gz * width, ny)
    air, ground_after = fused(blk, bulkblk, ground, mod, b, air_wind, air_buoyancy, az_n, gz, width)
    return (air.reshape(air_state.shape), ground_after.reshape(ground_state.shape))


def solution(mesh):
    placed = (
        P(None, None, "py", "px"),
        P(None, "py", "px"),
        P(),
        P(),
        P(None, None, ("px", "py"), None),
        P(None, None, ("px", "py"), None),
        P(None, ("px", "py"), None),
    )
    return jax.shard_map(
        body,
        mesh=mesh,
        in_specs=placed,
        out_specs=(P(None, None, "py", "px"), P(None, None, ("px", "py"), None)),
        check_vma=False,
    )
```

```python
import functools
import os

import jax
import jax.numpy as jnp
from jax import lax
from jax.experimental import pallas as pl
from jax.experimental.pallas import tpu as pltpu
from jax.sharding import PartitionSpec as P

STEPS = 3
RING = ("px", "py")
INTERPRET = os.environ.get("STENCIL_INTERPRET") == "1"


def trade(to_left, to_right):
    n = lax.axis_size(RING)
    from_right = lax.ppermute(to_left, RING, [(i, i - 1) for i in range(1, n)])
    from_left = lax.ppermute(to_right, RING, [(i, i + 1) for i in range(n - 1)])
    return from_left, from_right


def to_strips(block):
    f, z, ny, nx = block.shape
    parts = lax.axis_size("py")
    split = block.reshape(f, z, ny, parts, nx // parts)
    moved = lax.all_to_all(split, "py", 3, 3, tiled=True)
    return moved.transpose(0, 4, 1, 3, 2).reshape(f, nx // parts, z, parts * ny)


def from_strips(strip):
    f, nx, z, ny_all = strip.shape
    parts = lax.axis_size("py")
    split = strip.reshape(f, nx, z, parts, ny_all // parts)
    moved = lax.all_to_all(split, "py", 3, 3, tiled=True)
    return moved.transpose(0, 2, 4, 3, 1).reshape(f, z, ny_all // parts, parts * nx)


def _rows(a):
    return lax.broadcasted_iota(jnp.int32, a.shape, 0)


def _lanes(a):
    return lax.broadcasted_iota(jnp.int32, a.shape, 1)


def bz(a):
    return jnp.where(_rows(a) == 0, 0.0, pltpu.roll(a, 1, 0))


def az(a):
    n = a.shape[0]
    return jnp.where(_rows(a) == n - 1, 0.0, pltpu.roll(a, n - 1, 0))


def by(a):
    return jnp.where(_lanes(a) == 0, 0.0, pltpu.roll(a, 1, 1))


def ay(a):
    n = a.shape[1]
    return jnp.where(_lanes(a) == n - 1, 0.0, pltpu.roll(a, n - 1, 1))


def one_step(
    air_ref, bulk_ref, vel_ref, st_ref, mod_ref, b_ref, bl_ref, br_ref, fl_ref, fr_ref, scal_ref,
    air_out, vel_out, st_out, tl_out, tr_out, coef_ref, after_edges=None,
):
    width = air_ref.shape[1]
    az_n = air_ref.shape[2]
    gz = vel_ref.shape[2]

    def fl(start, count):
        return fl_ref[pl.ds(start, count), :]

    def fr(start, count):
        return fr_ref[pl.ds(start, count), :]

    def gcol(field_ref, k, left, right):
        cols = [left] + [field_ref[k, c] for c in range(width)] + [right]
        return cols

    sxx = gcol(st_ref, 0, fl(0, gz), fr(0, gz))
    sxy = gcol(st_ref, 3, fl(gz, gz), fr(gz, gz))
    sxz = gcol(st_ref, 4, fl(2 * gz, gz), fr(2 * gz, gz))
    syy = gcol(st_ref, 1, None, fr(3 * gz, gz))
    syz = gcol(st_ref, 5, None, fr(4 * gz, gz))
    szz = gcol(st_ref, 2, None, fr(5 * gz, gz))
    vx = gcol(vel_ref, 0, fl(3 * gz, gz), None)
    vy = gcol(vel_ref, 1, None, fr(6 * gz, gz))
    vz = gcol(vel_ref, 2, None, fr(7 * gz, gz))
    bb = (
        [bl_ref[pl.ds(4 * gz + 5 * az_n, gz), :]]
        + [b_ref[c] for c in range(width)]
        + [br_ref[pl.ds(8 * gz + az_n, gz), :]]
    )
    o = 4 * gz
    pr = fr(8 * gz, az_n)
    u = [fl(o, az_n), fl(o + az_n, az_n)] + [air_ref[1, c] for c in range(width)]
    v = [None, fl(o + 2 * az_n, az_n)] + [air_ref[2, c] for c in range(width)]
    w = [None, fl(o + 3 * az_n, az_n)] + [air_ref[3, c] for c in range(width)]
    p = [None, fl(o + 4 * az_n, az_n)] + [air_ref[0, c] for c in range(width)] + [pr]

    grow = lax.broadcasted_iota(jnp.int32, (gz, sxx[1].shape[1]), 0)
    arow = lax.broadcasted_iota(jnp.int32, (az_n, sxx[1].shape[1]), 0)

    vx1 = [None] * (width + 2)
    vy1 = [None] * (width + 2)
    vz1 = [None] * (width + 2)
    for e in range(width + 2):
        if e <= width:
            force_x = sxx[e + 1] - sxx[e] + sxy[e] - by(sxy[e]) + sxz[e] - bz(sxz[e])
            vx1[e] = vx[e] + bb[e] * force_x
        if e >= 1:
            force_y = sxy[e] - sxy[e - 1] + ay(syy[e]) - syy[e] + syz[e] - bz(syz[e])
            vy1[e] = vy[e] + bb[e] * force_y
            plane = jnp.broadcast_to(p[e + 1][0:1, :], szz[e].shape)
            ghost = jnp.where(grow == gz - 1, -plane, pltpu.roll(szz[e], gz - 1, 0))
            force_z = sxz[e] - sxz[e - 1] + syz[e] - by(syz[e]) + ghost - szz[e]
            vz1[e] = vz[e] + bb[e] * force_z

    def ground_col(c):
        e = c + 1
        mx, my, mz = vx1[e], vy1[e], vz1[e]
        lam = mod_ref[0, c]
        mu = mod_ref[1, c]
        longitudinal = lam + 2.0 * mu
        strain_x = mx - vx1[e - 1]
        strain_y = my - by(my)
        strain_z = mz - bz(mz)
        st_out[0, c] = st_ref[0, c] + longitudinal * strain_x + lam * (strain_y + strain_z)
        st_out[1, c] = st_ref[1, c] + longitudinal * strain_y + lam * (strain_x + strain_z)
        st_out[2, c] = st_ref[2, c] + longitudinal * strain_z + lam * (strain_x + strain_y)
        st_out[3, c] = st_ref[3, c] + mu * (ay(mx) - mx + vy1[e + 1] - my)
        sxz1 = st_ref[4, c] + mu * (az(mx) - mx + vz1[e + 1] - mz)
        syz1 = st_ref[5, c] + mu * (az(my) - my + ay(mz) - mz)
        st_out[4, c] = jnp.where(grow == gz - 1, 0.0, sxz1)
        st_out[5, c] = jnp.where(grow == gz - 1, 0.0, syz1)
        vel_out[0, c] = mx
        vel_out[1, c] = my
        vel_out[2, c] = mz
        if c == 0 and tl_out is not None:
            for k, (ref, f) in enumerate(
                [(st_out, 0), (st_out, 3), (st_out, 4), (st_out, 1), (st_out, 5), (st_out, 2),
                 (vel_out, 1), (vel_out, 2)]
            ):
                tl_out[pl.ds(k * gz, gz), :] = ref[f, 0]
        if c == width - 1 and tr_out is not None:
            for k, (ref, f) in enumerate([(st_out, 0), (st_out, 3), (st_out, 4), (vel_out, 0)]):
                tr_out[pl.ds(k * gz, gz), :] = ref[f, c]

    wind_x = coef_ref[0]
    wind_y = coef_ref[1]
    lift = coef_ref[2]
    u1 = [None] * (width + 2)
    for a in range(1, width + 2):
        u1[a] = (
            u[a]
            - wind_x * (u[a] - u[a - 1])
            - wind_y * (u[a] - by(u[a]))
            - lift * (p[a + 1] - p[a])
        )
    u1[1] = jnp.where(scal_ref[3 * az_n] > 0.5, u1[1], 0.0)

    def air_col(c):
        a = c + 2
        v1 = v[a] - wind_x * (v[a] - v[a - 1]) - wind_y * (v[a] - by(v[a])) - lift * (ay(p[a]) - p[a])
        w1 = w[a] - wind_x * (w[a] - w[a - 1]) - wind_y * (w[a] - by(w[a])) - lift * (p[a] - bz(p[a]))
        surface = jnp.broadcast_to(vz1[c + 1][gz - 1 : gz, :], w1.shape)
        w1 = jnp.where(arow == 0, surface, w1)
        pm = p[a]
        p1 = (
            pm
            - wind_x * (pm - p[a - 1])
            - wind_y * (pm - by(pm))
            - bulk_ref[c] * ((u1[a] - u1[a - 1]) + (v1 - by(v1)) + (az(w1) - w1))
        )
        air_out[0, c] = p1
        air_out[1, c] = u1[a]
        air_out[2, c] = v1
        air_out[3, c] = w1
        if c == 0 and tl_out is not None:
            tl_out[pl.ds(8 * gz, az_n), :] = p1
        if c == width - 2 and tr_out is not None:
            tr_out[pl.ds(4 * gz, az_n), :] = u1[a]
        if c == width - 1 and tr_out is not None:
            o = 4 * gz
            tr_out[pl.ds(o + az_n, az_n), :] = u1[a]
            tr_out[pl.ds(o + 2 * az_n, az_n), :] = v1
            tr_out[pl.ds(o + 3 * az_n, az_n), :] = w1
            tr_out[pl.ds(o + 4 * az_n, az_n), :] = p1

    ground_edges = [0, width - 1]
    air_edges = [0, width - 2, width - 1]
    for c in ground_edges:
        ground_col(c)
    for c in air_edges:
        air_col(c)
    if after_edges is not None:
        after_edges()
    for c in range(width):
        if c not in ground_edges:
            ground_col(c)
    for c in range(width):
        if c not in air_edges:
            air_col(c)


MESH = pl.DeviceIdType.MESH


def send_layout_kernel(air_ref, bulk_ref, out_ref):
    fields = air_ref.shape[0]
    rows = air_ref.shape[1]
    nyl = out_ref.shape[1] // 16
    nz = rows // nyl
    parts = out_ref.shape[0]
    width = air_ref.shape[2] // parts
    for yl in range(nyl):
        m = jnp.concatenate(
            [air_ref[f, pl.ds(yl, nz, stride=nyl), :] for f in range(fields)], 0
        )
        t = m.T.reshape(parts, width, m.shape[0])
        out_ref[:, pl.ds(yl * width, width), :] = t
        mb = jnp.concatenate(
            [bulk_ref[pl.ds(yl, nz, stride=nyl), :], jnp.zeros((m.shape[0] - nz, m.shape[1]), jnp.float32)], 0
        )
        tb = mb.T.reshape(parts, width, m.shape[0])
        out_ref[:, pl.ds(nyl * width + yl * width, width), :] = tb


def recv_layout_kernel(width, nyl, pay_ref, out_ref):
    fields = out_ref.shape[0]
    parts = pay_ref.shape[0]
    nz = pay_ref.shape[2] // fields
    for yl in range(nyl):
        n = pay_ref[:, pl.ds(yl, width, stride=nyl), :].reshape(parts * width, fields * nz)
        t = n.T
        for f in range(fields):
            out_ref[f, pl.ds(yl, nz, stride=nyl), :] = t[f * nz : (f + 1) * nz]


def from_strips_fast(payload, fields, az_n, width):
    parts = payload.shape[0]
    nyl = payload.shape[1] // width
    got = lax.all_to_all(payload, "py", 0, 0, tiled=True)
    out = pl.pallas_call(
        functools.partial(recv_layout_kernel, width, nyl),
        out_shape=jax.ShapeDtypeStruct((fields, az_n * nyl, width * parts), jnp.float32),
        interpret=INTERPRET,
    )(got)
    return out.reshape(fields, az_n, nyl, width * parts)


def to_strips_fast(air_state, air_bulk):
    f, z, ny, nx = air_state.shape
    parts = lax.axis_size("py")
    width = nx // parts
    flat = air_state.reshape(f, z * ny, nx)
    bulk = air_bulk.reshape(z * ny, nx)
    payload = pl.pallas_call(
        send_layout_kernel,
        out_shape=jax.ShapeDtypeStruct((parts, 2 * ny * width, f * z), jnp.float32),
        interpret=INTERPRET,
    )(flat, bulk)
    return lax.all_to_all(payload, "py", 0, 0, tiled=True)


class Strided:
    def __init__(self, ref, layers, width, offset=0, fields=None, clear=()):
        self.ref = ref
        self.layers = layers
        self.width = width
        self.offset = offset
        self.clear = clear
        n = ref.shape[0] - offset if fields is None else fields
        self.shape = (n, width, layers, ref.shape[-1])

    def _rows(self, c):
        return pl.ds(c, self.layers, stride=self.width)

    def __getitem__(self, index):
        f, c = index
        value = self.ref[self.offset + f, self._rows(c), :]
        if f in self.clear:
            top = lax.broadcasted_iota(jnp.int32, value.shape, 0) == self.layers - 1
            value = jnp.where(top, 0.0, value)
        return value

    def __setitem__(self, index, value):
        f, c = index
        self.ref[self.offset + f, self._rows(c), :] = value


class Plane:
    def __init__(self, ref, layers, width):
        self.ref = ref
        self.layers = layers
        self.width = width

    def __getitem__(self, c):
        return self.ref[pl.ds(c, self.layers, stride=self.width), :]


class Scalars:
    def __init__(self, wind_ref, lift_ref, keep):
        self.wind_ref = wind_ref
        self.lift_ref = lift_ref
        self.keep = keep
        self.levels = lift_ref.shape[0]

    def __getitem__(self, i):
        n = self.levels
        if i < 2 * n:
            return self.wind_ref[i // n, i % n]
        if i < 3 * n:
            return self.lift_ref[i - 2 * n]
        return self.keep


def fused_kernel(
    n_py, n_ring, gz, width, blk_ref, bulkblk_ref, gin_ref, modin_ref, bin_ref, wind_ref, lift_ref,
    airblk_out, gout_ref, pay_ref, pay_send, pay_out, pay_back, a2a_sem, air_ref, air_out,
    air_a, vel_a, st_a, air_b, vel_b, st_b, coef_ref, send_l, send_r, recv_l, recv_r,
    send_sem, recv_sem,
):
    az_n = air_ref.shape[2]
    ny = air_ref.shape[3]
    me = lax.axis_index("px") * n_py + lax.axis_index("py")
    vel_ref = Strided(gin_ref, gz, width, 0, 3)
    st_ref = Strided(gin_ref, gz, width, 3, 6, clear=(4, 5))
    mod_ref = Strided(modin_ref, gz, width)
    b_ref = Plane(bin_ref, gz, width)
    vel_out = Strided(gout_ref, gz, width, 0, 3)
    st_out = Strided(gout_ref, gz, width, 3, 6)
    scal_ref = Scalars(wind_ref, lift_ref, jnp.where(me > 0, 1.0, 0.0))
    has_left = me > 0
    has_right = me < n_ring - 1
    left = ((me - 1) // n_py, (me - 1) % n_py)
    right = ((me + 1) // n_py, (me + 1) % n_py)
    rows_l = send_l.shape[1]
    rows_r = send_r.shape[1]

    nyl = ny // n_py
    my_py = lax.axis_index("py")
    my_px = lax.axis_index("px")
    n_px = n_ring // n_py
    extra_l = (my_py == 0) & (my_px > 0)
    extra_r = (my_py == n_py - 1) & (my_px < n_px - 1)
    nz = az_n
    for yl in range(nyl):
        m = jnp.concatenate([blk_ref[f, pl.ds(yl, nz, stride=nyl), :] for f in range(4)], 0)
        pay_send[:, pl.ds(yl * width, width), :] = m.T.reshape(n_py, width, 4 * nz)
        mb = jnp.concatenate(
            [bulkblk_ref[pl.ds(yl, nz, stride=nyl), :], jnp.zeros((3 * nz, n_py * width), jnp.float32)], 0
        )
        pay_send[:, pl.ds(nyl * width + yl * width, width), :] = mb.T.reshape(n_py, width, 4 * nz)

    @pl.when(jnp.logical_not(has_left))
    def _():
        recv_l[...] = jnp.zeros_like(recv_l)

    @pl.when(jnp.logical_not(has_right))
    def _():
        recv_r[...] = jnp.zeros_like(recv_r)

    barrier = pltpu.get_barrier_semaphore()

    for q in range(n_py):

        @pl.when(my_py != q)
        def _():
            pl.semaphore_signal(barrier, inc=1, device_id=(my_px, q), device_id_type=MESH)

    @pl.when(extra_l)
    def _():
        pl.semaphore_signal(barrier, inc=1, device_id=left, device_id_type=MESH)

    @pl.when(extra_r)
    def _():
        pl.semaphore_signal(barrier, inc=1, device_id=right, device_id_type=MESH)

    for count in range(3):

        @pl.when(extra_l.astype(jnp.int32) + extra_r.astype(jnp.int32) == count)
        def _():
            pl.semaphore_wait(barrier, n_py - 1 + count)

    def group_copy(src, dst, k, q, slot):
        return pltpu.make_async_remote_copy(
            src_ref=src.at[q],
            dst_ref=dst.at[slot],
            send_sem=a2a_sem.at[k, q],
            recv_sem=a2a_sem.at[k + 1, slot],
            device_id=(my_px, q),
            device_id_type=MESH,
        )

    def group_send(src, dst, k):
        for q in range(n_py):

            @pl.when(my_py != q)
            def _():
                group_copy(src, dst, k, q, my_py).start()

        dst[my_py] = src[my_py]

    def group_wait(src, dst, k):
        for q in range(n_py):

            @pl.when(my_py != q)
            def _():
                group_copy(src, dst, k, q, q).wait_recv()

    def group_send_wait(src, dst, k):
        for q in range(n_py):

            @pl.when(my_py != q)
            def _():
                group_copy(src, dst, k, q, my_py).wait_send()

    def copies(n, count_l, count_r, first_l=0, first_r=0, slot=None):
        slot = n if slot is None else slot
        to_left = pltpu.make_async_remote_copy(
            src_ref=send_l.at[n, pl.ds(first_l, count_l)],
            dst_ref=recv_r.at[n, pl.ds(first_l, count_l)],
            send_sem=send_sem.at[slot, 0],
            recv_sem=recv_sem.at[slot, 1],
            device_id=left,
            device_id_type=MESH,
        )
        to_right = pltpu.make_async_remote_copy(
            src_ref=send_r.at[n, pl.ds(first_r, count_r)],
            dst_ref=recv_l.at[n, pl.ds(first_r, count_r)],
            send_sem=send_sem.at[slot, 1],
            recv_sem=recv_sem.at[slot, 0],
            device_id=right,
            device_id_type=MESH,
        )

        return to_left, to_right

    def start(n, *args):
        to_left, to_right = copies(n, *args)

        @pl.when(has_left)
        def _():
            to_left.start()

        @pl.when(has_right)
        def _():
            to_right.start()

    def wait_recv(n, *args):
        to_left, to_right = copies(n, *args)

        @pl.when(has_left)
        def _():
            to_right.wait_recv()

        @pl.when(has_right)
        def _():
            to_left.wait_recv()

    def wait_send(n, *args):
        to_left, to_right = copies(n, *args)

        @pl.when(has_left)
        def _():
            to_left.wait_send()

        @pl.when(has_right)
        def _():
            to_right.wait_send()

    tl = send_l.at[0]
    tr = send_r.at[0]
    left_rows = [st_ref[f, 0] for f in (0, 3, 4, 1, 5, 2)] + [vel_ref[1, 0], vel_ref[2, 0]]
    for k, value in enumerate(left_rows):
        tl[pl.ds(k * gz, gz), :] = value
    right_rows = [st_ref[f, width - 1] for f in (0, 3, 4)] + [vel_ref[0, width - 1]]
    for k, value in enumerate(right_rows):
        tr[pl.ds(k * gz, gz), :] = value
    ground_part = (8 * gz, 4 * gz, 0, 0, STEPS)
    start(0, *ground_part)

    group_send(pay_send, pay_ref, 0)
    group_wait(pay_send, pay_ref, 0)
    for xl in range(width):
        n_air = pay_ref[:, pl.ds(xl, nyl, stride=width), :].reshape(ny, 4 * az_n)
        t = n_air.T
        for f in range(4):
            air_ref[f, xl] = t[f * az_n : (f + 1) * az_n]
        n_bulk = pay_ref[:, pl.ds(nyl * width + xl, nyl, stride=width), :].reshape(ny, 4 * az_n)
        air_ref[4, xl] = n_bulk.T[0:az_n]


    for k in range(3):
        for z in range(az_n):
            coef_ref[k, pl.ds(z, 1), :] = jnp.full((1, ny), scal_ref[k * az_n + z], jnp.float32)

    tl[pl.ds(8 * gz, az_n), :] = air_ref[0, 0]
    tl[pl.ds(8 * gz + az_n, gz), :] = b_ref[0]
    o = 4 * gz
    tr[pl.ds(o, az_n), :] = air_ref[1, width - 2]
    for k, f in enumerate((1, 2, 3, 0)):
        tr[pl.ds(o + (k + 1) * az_n, az_n), :] = air_ref[f, width - 1]
    tr[pl.ds(o + 5 * az_n, gz), :] = b_ref[width - 1]

    full_l = 8 * gz + az_n
    full_r = 4 * gz + 5 * az_n
    counts = [(rows_l, rows_r)] + [(full_l, full_r)] * (STEPS - 1)
    air_part = (rows_l - 8 * gz, rows_r - 4 * gz, 8 * gz, 4 * gz, 0)
    start(0, *air_part)
    wait_recv(0, *ground_part)
    wait_recv(0, *air_part)
    states = [
        (air_ref, vel_ref, st_ref),
        (air_a, vel_a, st_a),
        (air_b, vel_b, st_b),
        (air_out, vel_out, st_out),
    ]
    for n in range(STEPS):
        src = states[n] if n < len(states) - 1 else states[-2]
        dst = states[n + 1] if n + 1 < STEPS else states[-1]
        last = n + 1 == STEPS
        one_step(
            src[0], air_ref.at[4], src[1], src[2], mod_ref, b_ref, recv_l.at[0], recv_r.at[0],
            recv_l.at[n], recv_r.at[n], scal_ref, dst[0], dst[1], dst[2],
            None if last else send_l.at[n + 1], None if last else send_r.at[n + 1], coef_ref,
            None if last else functools.partial(start, n + 1, *counts[n + 1]),
        )
        if not last:
            wait_recv(n + 1, *counts[n + 1])
    for xl in range(width):
        m = jnp.concatenate([air_out[f, xl] for f in range(4)], 0)
        t = m.T.reshape(n_py, nyl, 4 * az_n)
        pay_out[:, pl.ds(xl * nyl, nyl), :] = t
    group_send(pay_out, pay_back, 2)
    group_wait(pay_out, pay_back, 2)
    for yl in range(nyl):
        nb = pay_back[:, pl.ds(yl, width, stride=nyl), :].reshape(n_py * width, 4 * nz)
        tb = nb.T
        for f in range(4):
            airblk_out[f, pl.ds(yl, nz, stride=nyl), :] = tb[f * nz : (f + 1) * nz]
    wait_send(0, *ground_part)
    wait_send(0, *air_part)
    for n in range(1, STEPS):
        wait_send(n, *counts[n])
    group_send_wait(pay_send, pay_ref, 0)
    group_send_wait(pay_out, pay_back, 2)


def fused(blk, bulkblk, ground, mod, b, wind, lift, az_n, gz, width):
    n_py = lax.axis_size("py")
    n_ring = lax.axis_size(RING)
    nyl = blk.shape[1] // az_n
    ny = nyl * n_py
    fields = (4, width, az_n, ny)
    rows_l = 9 * gz + az_n
    rows_r = 5 * gz + 5 * az_n
    vmem = pl.BlockSpec(memory_space=pltpu.VMEM)
    return pl.pallas_call(
        functools.partial(fused_kernel, n_py, n_ring, gz, width),
        out_shape=(
            jax.ShapeDtypeStruct(blk.shape, jnp.float32),
            jax.ShapeDtypeStruct(ground.shape, jnp.float32),
        ),
        in_specs=[vmem] * 5 + [pl.BlockSpec(memory_space=pltpu.SMEM)] * 2,
        out_specs=(vmem, vmem),
        scratch_shapes=[
            pltpu.VMEM((n_py, 2 * nyl * width, 4 * az_n), jnp.float32),
            pltpu.VMEM((n_py, 2 * nyl * width, 4 * az_n), jnp.float32),
            pltpu.VMEM((n_py, nyl * width, 4 * az_n), jnp.float32),
            pltpu.VMEM((n_py, nyl * width, 4 * az_n), jnp.float32),
            pltpu.SemaphoreType.DMA((4, n_py)),
            pltpu.VMEM((5, width, az_n, ny), jnp.float32),
            pltpu.VMEM(fields, jnp.float32),
            pltpu.VMEM(fields, jnp.float32),
            pltpu.VMEM((3, width, gz, ny), jnp.float32),
            pltpu.VMEM((6, width, gz, ny), jnp.float32),
            pltpu.VMEM(fields, jnp.float32),
            pltpu.VMEM((3, width, gz, ny), jnp.float32),
            pltpu.VMEM((6, width, gz, ny), jnp.float32),
            pltpu.VMEM((3, az_n, ny), jnp.float32),
            pltpu.VMEM((STEPS, rows_l, ny), jnp.float32),
            pltpu.VMEM((STEPS, rows_r, ny), jnp.float32),
            pltpu.VMEM((STEPS, rows_r, ny), jnp.float32),
            pltpu.VMEM((STEPS, rows_l, ny), jnp.float32),
            pltpu.SemaphoreType.DMA((STEPS + 1, 2)),
            pltpu.SemaphoreType.DMA((STEPS + 1, 2)),
        ],
        compiler_params=pltpu.CompilerParams(collective_id=0, has_side_effects=True),
        interpret=INTERPRET,
    )(blk, bulkblk, ground, mod, b, wind, lift)


def body(air_state, air_bulk, air_buoyancy, air_wind, ground_state, ground_moduli, ground_buoyancy):
    f_n, az_n, ny_l, nx_l = air_state.shape
    nf, gz, width, ny = ground_state.shape
    blk = air_state.reshape(f_n, az_n * ny_l, nx_l)
    bulkblk = air_bulk.reshape(az_n * ny_l, nx_l)
    ground = ground_state.reshape(nf, gz * width, ny)
    mod = ground_moduli.reshape(ground_moduli.shape[0], gz * width, ny)
    b = ground_buoyancy.reshape(gz * width, ny)
    air, ground_after = fused(blk, bulkblk, ground, mod, b, air_wind, air_buoyancy, az_n, gz, width)
    return (air.reshape(air_state.shape), ground_after.reshape(ground_state.shape))


def solution(mesh):
    placed = (
        P(None, None, "py", "px"),
        P(None, "py", "px"),
        P(),
        P(),
        P(None, None, ("px", "py"), None),
        P(None, None, ("px", "py"), None),
        P(None, ("px", "py"), None),
    )
    return jax.shard_map(
        body,
        mesh=mesh,
        in_specs=placed,
        out_specs=(P(None, None, "py", "px"), P(None, None, ("px", "py"), None)),
        check_vma=False,
    )
```

```python
import functools
import os

import jax
import jax.numpy as jnp
from jax import lax
from jax.experimental import pallas as pl
from jax.experimental.pallas import tpu as pltpu
from jax.sharding import PartitionSpec as P

STEPS = 3
RING = ("px", "py")
INTERPRET = os.environ.get("STENCIL_INTERPRET") == "1"


def trade(to_left, to_right):
    n = lax.axis_size(RING)
    from_right = lax.ppermute(to_left, RING, [(i, i - 1) for i in range(1, n)])
    from_left = lax.ppermute(to_right, RING, [(i, i + 1) for i in range(n - 1)])
    return from_left, from_right


def to_strips(block):
    f, z, ny, nx = block.shape
    parts = lax.axis_size("py")
    split = block.reshape(f, z, ny, parts, nx // parts)
    moved = lax.all_to_all(split, "py", 3, 3, tiled=True)
    return moved.transpose(0, 4, 1, 3, 2).reshape(f, nx // parts, z, parts * ny)


def from_strips(strip):
    f, nx, z, ny_all = strip.shape
    parts = lax.axis_size("py")
    split = strip.reshape(f, nx, z, parts, ny_all // parts)
    moved = lax.all_to_all(split, "py", 3, 3, tiled=True)
    return moved.transpose(0, 2, 4, 3, 1).reshape(f, z, ny_all // parts, parts * nx)


def _rows(a):
    return lax.broadcasted_iota(jnp.int32, a.shape, 0)


def _lanes(a):
    return lax.broadcasted_iota(jnp.int32, a.shape, 1)


def bz(a):
    return jnp.where(_rows(a) == 0, 0.0, pltpu.roll(a, 1, 0))


def az(a):
    n = a.shape[0]
    return jnp.where(_rows(a) == n - 1, 0.0, pltpu.roll(a, n - 1, 0))


def by(a):
    return jnp.where(_lanes(a) == 0, 0.0, pltpu.roll(a, 1, 1))


def ay(a):
    n = a.shape[1]
    return jnp.where(_lanes(a) == n - 1, 0.0, pltpu.roll(a, n - 1, 1))


def one_step(
    air_ref, bulk_ref, vel_ref, st_ref, mod_ref, b_ref, bl_ref, br_ref, fl_ref, fr_ref, scal_ref,
    air_out, vel_out, st_out, tl_out, tr_out, coef_ref, after_edges=None,
):
    width = air_ref.shape[1]
    az_n = air_ref.shape[2]
    gz = vel_ref.shape[2]

    def fl(start, count):
        return fl_ref[pl.ds(start, count), :]

    def fr(start, count):
        return fr_ref[pl.ds(start, count), :]

    def gcol(field_ref, k, left, right):
        cols = [left] + [field_ref[k, c] for c in range(width)] + [right]
        return cols

    sxx = gcol(st_ref, 0, fl(0, gz), fr(0, gz))
    sxy = gcol(st_ref, 3, fl(gz, gz), fr(gz, gz))
    sxz = gcol(st_ref, 4, fl(2 * gz, gz), fr(2 * gz, gz))
    syy = gcol(st_ref, 1, None, fr(3 * gz, gz))
    syz = gcol(st_ref, 5, None, fr(4 * gz, gz))
    szz = gcol(st_ref, 2, None, fr(5 * gz, gz))
    vx = gcol(vel_ref, 0, fl(3 * gz, gz), None)
    vy = gcol(vel_ref, 1, None, fr(6 * gz, gz))
    vz = gcol(vel_ref, 2, None, fr(7 * gz, gz))
    bb = (
        [bl_ref[pl.ds(4 * gz + 5 * az_n, gz), :]]
        + [b_ref[c] for c in range(width)]
        + [br_ref[pl.ds(8 * gz + az_n, gz), :]]
    )
    o = 4 * gz
    pr = fr(8 * gz, az_n)
    u = [fl(o, az_n), fl(o + az_n, az_n)] + [air_ref[1, c] for c in range(width)]
    v = [None, fl(o + 2 * az_n, az_n)] + [air_ref[2, c] for c in range(width)]
    w = [None, fl(o + 3 * az_n, az_n)] + [air_ref[3, c] for c in range(width)]
    p = [None, fl(o + 4 * az_n, az_n)] + [air_ref[0, c] for c in range(width)] + [pr]

    grow = lax.broadcasted_iota(jnp.int32, (gz, sxx[1].shape[1]), 0)
    arow = lax.broadcasted_iota(jnp.int32, (az_n, sxx[1].shape[1]), 0)

    vx1 = [None] * (width + 2)
    vy1 = [None] * (width + 2)
    vz1 = [None] * (width + 2)
    for e in range(width + 2):
        if e <= width:
            force_x = sxx[e + 1] - sxx[e] + sxy[e] - by(sxy[e]) + sxz[e] - bz(sxz[e])
            vx1[e] = vx[e] + bb[e] * force_x
        if e >= 1:
            force_y = sxy[e] - sxy[e - 1] + ay(syy[e]) - syy[e] + syz[e] - bz(syz[e])
            vy1[e] = vy[e] + bb[e] * force_y
            plane = jnp.broadcast_to(p[e + 1][0:1, :], szz[e].shape)
            ghost = jnp.where(grow == gz - 1, -plane, pltpu.roll(szz[e], gz - 1, 0))
            force_z = sxz[e] - sxz[e - 1] + syz[e] - by(syz[e]) + ghost - szz[e]
            vz1[e] = vz[e] + bb[e] * force_z

    def ground_col(c):
        e = c + 1
        mx, my, mz = vx1[e], vy1[e], vz1[e]
        lam = mod_ref[0, c]
        mu = mod_ref[1, c]
        longitudinal = lam + 2.0 * mu
        strain_x = mx - vx1[e - 1]
        strain_y = my - by(my)
        strain_z = mz - bz(mz)
        st_out[0, c] = st_ref[0, c] + longitudinal * strain_x + lam * (strain_y + strain_z)
        st_out[1, c] = st_ref[1, c] + longitudinal * strain_y + lam * (strain_x + strain_z)
        st_out[2, c] = st_ref[2, c] + longitudinal * strain_z + lam * (strain_x + strain_y)
        st_out[3, c] = st_ref[3, c] + mu * (ay(mx) - mx + vy1[e + 1] - my)
        sxz1 = st_ref[4, c] + mu * (az(mx) - mx + vz1[e + 1] - mz)
        syz1 = st_ref[5, c] + mu * (az(my) - my + ay(mz) - mz)
        st_out[4, c] = jnp.where(grow == gz - 1, 0.0, sxz1)
        st_out[5, c] = jnp.where(grow == gz - 1, 0.0, syz1)
        vel_out[0, c] = mx
        vel_out[1, c] = my
        vel_out[2, c] = mz
        if c == 0 and tl_out is not None:
            for k, (ref, f) in enumerate(
                [(st_out, 0), (st_out, 3), (st_out, 4), (st_out, 1), (st_out, 5), (st_out, 2),
                 (vel_out, 1), (vel_out, 2)]
            ):
                tl_out[pl.ds(k * gz, gz), :] = ref[f, 0]
        if c == width - 1 and tr_out is not None:
            for k, (ref, f) in enumerate([(st_out, 0), (st_out, 3), (st_out, 4), (vel_out, 0)]):
                tr_out[pl.ds(k * gz, gz), :] = ref[f, c]

    wind_x = coef_ref[0]
    wind_y = coef_ref[1]
    lift = coef_ref[2]
    u1 = [None] * (width + 2)
    for a in range(1, width + 2):
        u1[a] = (
            u[a]
            - wind_x * (u[a] - u[a - 1])
            - wind_y * (u[a] - by(u[a]))
            - lift * (p[a + 1] - p[a])
        )
    u1[1] = jnp.where(scal_ref[3 * az_n] > 0.5, u1[1], 0.0)

    def air_col(c):
        a = c + 2
        v1 = v[a] - wind_x * (v[a] - v[a - 1]) - wind_y * (v[a] - by(v[a])) - lift * (ay(p[a]) - p[a])
        w1 = w[a] - wind_x * (w[a] - w[a - 1]) - wind_y * (w[a] - by(w[a])) - lift * (p[a] - bz(p[a]))
        surface = jnp.broadcast_to(vz1[c + 1][gz - 1 : gz, :], w1.shape)
        w1 = jnp.where(arow == 0, surface, w1)
        pm = p[a]
        p1 = (
            pm
            - wind_x * (pm - p[a - 1])
            - wind_y * (pm - by(pm))
            - bulk_ref[c] * ((u1[a] - u1[a - 1]) + (v1 - by(v1)) + (az(w1) - w1))
        )
        air_out[0, c] = p1
        air_out[1, c] = u1[a]
        air_out[2, c] = v1
        air_out[3, c] = w1
        if c == 0 and tl_out is not None:
            tl_out[pl.ds(8 * gz, az_n), :] = p1
        if c == width - 2 and tr_out is not None:
            tr_out[pl.ds(4 * gz, az_n), :] = u1[a]
        if c == width - 1 and tr_out is not None:
            o = 4 * gz
            tr_out[pl.ds(o + az_n, az_n), :] = u1[a]
            tr_out[pl.ds(o + 2 * az_n, az_n), :] = v1
            tr_out[pl.ds(o + 3 * az_n, az_n), :] = w1
            tr_out[pl.ds(o + 4 * az_n, az_n), :] = p1

    ground_edges = [0, width - 1]
    air_edges = [0, width - 2, width - 1]
    for c in ground_edges:
        ground_col(c)
    for c in air_edges:
        air_col(c)
    if after_edges is not None:
        after_edges()
    for c in range(width):
        if c not in ground_edges:
            ground_col(c)
    for c in range(width):
        if c not in air_edges:
            air_col(c)


MESH = pl.DeviceIdType.MESH


def send_layout_kernel(air_ref, bulk_ref, out_ref):
    fields = air_ref.shape[0]
    rows = air_ref.shape[1]
    nyl = out_ref.shape[1] // 16
    nz = rows // nyl
    parts = out_ref.shape[0]
    width = air_ref.shape[2] // parts
    for yl in range(nyl):
        m = jnp.concatenate(
            [air_ref[f, pl.ds(yl, nz, stride=nyl), :] for f in range(fields)], 0
        )
        t = m.T.reshape(parts, width, m.shape[0])
        out_ref[:, pl.ds(yl * width, width), :] = t
        mb = jnp.concatenate(
            [bulk_ref[pl.ds(yl, nz, stride=nyl), :], jnp.zeros((m.shape[0] - nz, m.shape[1]), jnp.float32)], 0
        )
        tb = mb.T.reshape(parts, width, m.shape[0])
        out_ref[:, pl.ds(nyl * width + yl * width, width), :] = tb


def recv_layout_kernel(width, nyl, pay_ref, out_ref):
    fields = out_ref.shape[0]
    parts = pay_ref.shape[0]
    nz = pay_ref.shape[2] // fields
    for yl in range(nyl):
        n = pay_ref[:, pl.ds(yl, width, stride=nyl), :].reshape(parts * width, fields * nz)
        t = n.T
        for f in range(fields):
            out_ref[f, pl.ds(yl, nz, stride=nyl), :] = t[f * nz : (f + 1) * nz]


def from_strips_fast(payload, fields, az_n, width):
    parts = payload.shape[0]
    nyl = payload.shape[1] // width
    got = lax.all_to_all(payload, "py", 0, 0, tiled=True)
    out = pl.pallas_call(
        functools.partial(recv_layout_kernel, width, nyl),
        out_shape=jax.ShapeDtypeStruct((fields, az_n * nyl, width * parts), jnp.float32),
        interpret=INTERPRET,
    )(got)
    return out.reshape(fields, az_n, nyl, width * parts)


def to_strips_fast(air_state, air_bulk):
    f, z, ny, nx = air_state.shape
    parts = lax.axis_size("py")
    width = nx // parts
    flat = air_state.reshape(f, z * ny, nx)
    bulk = air_bulk.reshape(z * ny, nx)
    payload = pl.pallas_call(
        send_layout_kernel,
        out_shape=jax.ShapeDtypeStruct((parts, 2 * ny * width, f * z), jnp.float32),
        interpret=INTERPRET,
    )(flat, bulk)
    return lax.all_to_all(payload, "py", 0, 0, tiled=True)


class Strided:
    def __init__(self, ref, layers, width, offset=0, fields=None, clear=()):
        self.ref = ref
        self.layers = layers
        self.width = width
        self.offset = offset
        self.clear = clear
        n = ref.shape[0] - offset if fields is None else fields
        self.shape = (n, width, layers, ref.shape[-1])

    def _rows(self, c):
        return pl.ds(c, self.layers, stride=self.width)

    def __getitem__(self, index):
        f, c = index
        value = self.ref[self.offset + f, self._rows(c), :]
        if f in self.clear:
            top = lax.broadcasted_iota(jnp.int32, value.shape, 0) == self.layers - 1
            value = jnp.where(top, 0.0, value)
        return value

    def __setitem__(self, index, value):
        f, c = index
        self.ref[self.offset + f, self._rows(c), :] = value


class Plane:
    def __init__(self, ref, layers, width):
        self.ref = ref
        self.layers = layers
        self.width = width

    def __getitem__(self, c):
        return self.ref[pl.ds(c, self.layers, stride=self.width), :]


class Scalars:
    def __init__(self, wind_ref, lift_ref, keep):
        self.wind_ref = wind_ref
        self.lift_ref = lift_ref
        self.keep = keep
        self.levels = lift_ref.shape[0]

    def __getitem__(self, i):
        n = self.levels
        if i < 2 * n:
            return self.wind_ref[i // n, i % n]
        if i < 3 * n:
            return self.lift_ref[i - 2 * n]
        return self.keep


def fused_kernel(
    n_py, n_ring, gz, width, blk_ref, bulkblk_ref, gin_ref, modin_ref, bin_ref, wind_ref, lift_ref,
    airblk_out, gout_ref, pay_ref, pay_send, pay_out, pay_back, a2a_sem, air_ref, air_out,
    air_a, vel_a, st_a, air_b, vel_b, st_b, coef_ref, send_l, send_r, recv_l, recv_r,
    send_sem, recv_sem,
):
    az_n = air_ref.shape[2]
    ny = air_ref.shape[3]
    me = lax.axis_index("px") * n_py + lax.axis_index("py")
    vel_ref = Strided(gin_ref, gz, width, 0, 3)
    st_ref = Strided(gin_ref, gz, width, 3, 6, clear=(4, 5))
    mod_ref = Strided(modin_ref, gz, width)
    b_ref = Plane(bin_ref, gz, width)
    vel_out = Strided(gout_ref, gz, width, 0, 3)
    st_out = Strided(gout_ref, gz, width, 3, 6)
    scal_ref = Scalars(wind_ref, lift_ref, jnp.where(me > 0, 1.0, 0.0))
    has_left = me > 0
    has_right = me < n_ring - 1
    left = ((me - 1) // n_py, (me - 1) % n_py)
    right = ((me + 1) // n_py, (me + 1) % n_py)
    rows_l = send_l.shape[1]
    rows_r = send_r.shape[1]

    nyl = ny // n_py
    my_py = lax.axis_index("py")
    my_px = lax.axis_index("px")
    n_px = n_ring // n_py
    extra_l = (my_py == 0) & (my_px > 0)
    extra_r = (my_py == n_py - 1) & (my_px < n_px - 1)
    nz = az_n
    for yl in range(nyl):
        m = jnp.concatenate([blk_ref[f, pl.ds(yl, nz, stride=nyl), :] for f in range(4)], 0)
        pay_send[:, pl.ds(yl * width, width), :] = m.T.reshape(n_py, width, 4 * nz)
        mb = jnp.concatenate(
            [bulkblk_ref[pl.ds(yl, nz, stride=nyl), :], jnp.zeros((3 * nz, n_py * width), jnp.float32)], 0
        )
        pay_send[:, pl.ds(nyl * width + yl * width, width), :] = mb.T.reshape(n_py, width, 4 * nz)

    @pl.when(jnp.logical_not(has_left))
    def _():
        recv_l[...] = jnp.zeros_like(recv_l)

    @pl.when(jnp.logical_not(has_right))
    def _():
        recv_r[...] = jnp.zeros_like(recv_r)

    barrier = pltpu.get_barrier_semaphore()

    for q in range(n_py):

        @pl.when(my_py != q)
        def _():
            pl.semaphore_signal(barrier, inc=1, device_id=(my_px, q), device_id_type=MESH)

    @pl.when(extra_l)
    def _():
        pl.semaphore_signal(barrier, inc=1, device_id=left, device_id_type=MESH)

    @pl.when(extra_r)
    def _():
        pl.semaphore_signal(barrier, inc=1, device_id=right, device_id_type=MESH)

    for count in range(3):

        @pl.when(extra_l.astype(jnp.int32) + extra_r.astype(jnp.int32) == count)
        def _():
            pl.semaphore_wait(barrier, n_py - 1 + count)

    def group_copy(src, dst, k, q, slot):
        return pltpu.make_async_remote_copy(
            src_ref=src.at[q],
            dst_ref=dst.at[slot],
            send_sem=a2a_sem.at[k, q],
            recv_sem=a2a_sem.at[k + 1, slot],
            device_id=(my_px, q),
            device_id_type=MESH,
        )

    def group_send(src, dst, k):
        for step in range(1, n_py):
            group_copy(src, dst, k, lax.rem(my_py + step, n_py), my_py).start()

        dst[my_py] = src[my_py]

    def group_wait(src, dst, k):
        for q in range(n_py):

            @pl.when(my_py != q)
            def _():
                group_copy(src, dst, k, q, q).wait_recv()

    def group_send_wait(src, dst, k):
        for q in range(n_py):

            @pl.when(my_py != q)
            def _():
                group_copy(src, dst, k, q, my_py).wait_send()

    def copies(n, count_l, count_r, first_l=0, first_r=0, slot=None):
        slot = n if slot is None else slot
        to_left = pltpu.make_async_remote_copy(
            src_ref=send_l.at[n, pl.ds(first_l, count_l)],
            dst_ref=recv_r.at[n, pl.ds(first_l, count_l)],
            send_sem=send_sem.at[slot, 0],
            recv_sem=recv_sem.at[slot, 1],
            device_id=left,
            device_id_type=MESH,
        )
        to_right = pltpu.make_async_remote_copy(
            src_ref=send_r.at[n, pl.ds(first_r, count_r)],
            dst_ref=recv_l.at[n, pl.ds(first_r, count_r)],
            send_sem=send_sem.at[slot, 1],
            recv_sem=recv_sem.at[slot, 0],
            device_id=right,
            device_id_type=MESH,
        )

        return to_left, to_right

    def start(n, *args):
        to_left, to_right = copies(n, *args)

        @pl.when(has_left)
        def _():
            to_left.start()

        @pl.when(has_right)
        def _():
            to_right.start()

    def wait_recv(n, *args):
        to_left, to_right = copies(n, *args)

        @pl.when(has_left)
        def _():
            to_right.wait_recv()

        @pl.when(has_right)
        def _():
            to_left.wait_recv()

    def wait_send(n, *args):
        to_left, to_right = copies(n, *args)

        @pl.when(has_left)
        def _():
            to_left.wait_send()

        @pl.when(has_right)
        def _():
            to_right.wait_send()

    tl = send_l.at[0]
    tr = send_r.at[0]
    left_rows = [st_ref[f, 0] for f in (0, 3, 4, 1, 5, 2)] + [vel_ref[1, 0], vel_ref[2, 0]]
    for k, value in enumerate(left_rows):
        tl[pl.ds(k * gz, gz), :] = value
    right_rows = [st_ref[f, width - 1] for f in (0, 3, 4)] + [vel_ref[0, width - 1]]
    for k, value in enumerate(right_rows):
        tr[pl.ds(k * gz, gz), :] = value
    ground_part = (8 * gz, 4 * gz, 0, 0, STEPS)
    start(0, *ground_part)

    group_send(pay_send, pay_ref, 0)
    group_wait(pay_send, pay_ref, 0)
    for xl in range(width):
        n_air = pay_ref[:, pl.ds(xl, nyl, stride=width), :].reshape(ny, 4 * az_n)
        t = n_air.T
        for f in range(4):
            air_ref[f, xl] = t[f * az_n : (f + 1) * az_n]
        n_bulk = pay_ref[:, pl.ds(nyl * width + xl, nyl, stride=width), :].reshape(ny, 4 * az_n)
        air_ref[4, xl] = n_bulk.T[0:az_n]


    for k in range(3):
        for z in range(az_n):
            coef_ref[k, pl.ds(z, 1), :] = jnp.full((1, ny), scal_ref[k * az_n + z], jnp.float32)

    tl[pl.ds(8 * gz, az_n), :] = air_ref[0, 0]
    tl[pl.ds(8 * gz + az_n, gz), :] = b_ref[0]
    o = 4 * gz
    tr[pl.ds(o, az_n), :] = air_ref[1, width - 2]
    for k, f in enumerate((1, 2, 3, 0)):
        tr[pl.ds(o + (k + 1) * az_n, az_n), :] = air_ref[f, width - 1]
    tr[pl.ds(o + 5 * az_n, gz), :] = b_ref[width - 1]

    full_l = 8 * gz + az_n
    full_r = 4 * gz + 5 * az_n
    counts = [(rows_l, rows_r)] + [(full_l, full_r)] * (STEPS - 1)
    air_part = (rows_l - 8 * gz, rows_r - 4 * gz, 8 * gz, 4 * gz, 0)
    start(0, *air_part)
    wait_recv(0, *ground_part)
    wait_recv(0, *air_part)
    states = [
        (air_ref, vel_ref, st_ref),
        (air_a, vel_a, st_a),
        (air_b, vel_b, st_b),
        (air_out, vel_out, st_out),
    ]
    for n in range(STEPS):
        src = states[n] if n < len(states) - 1 else states[-2]
        dst = states[n + 1] if n + 1 < STEPS else states[-1]
        last = n + 1 == STEPS
        one_step(
            src[0], air_ref.at[4], src[1], src[2], mod_ref, b_ref, recv_l.at[0], recv_r.at[0],
            recv_l.at[n], recv_r.at[n], scal_ref, dst[0], dst[1], dst[2],
            None if last else send_l.at[n + 1], None if last else send_r.at[n + 1], coef_ref,
            None if last else functools.partial(start, n + 1, *counts[n + 1]),
        )
        if not last:
            wait_recv(n + 1, *counts[n + 1])
    for xl in range(width):
        m = jnp.concatenate([air_out[f, xl] for f in range(4)], 0)
        t = m.T.reshape(n_py, nyl, 4 * az_n)
        pay_out[:, pl.ds(xl * nyl, nyl), :] = t
    group_send(pay_out, pay_back, 2)
    group_wait(pay_out, pay_back, 2)
    for yl in range(nyl):
        nb = pay_back[:, pl.ds(yl, width, stride=nyl), :].reshape(n_py * width, 4 * nz)
        tb = nb.T
        for f in range(4):
            airblk_out[f, pl.ds(yl, nz, stride=nyl), :] = tb[f * nz : (f + 1) * nz]
    wait_send(0, *ground_part)
    wait_send(0, *air_part)
    for n in range(1, STEPS):
        wait_send(n, *counts[n])
    group_send_wait(pay_send, pay_ref, 0)
    group_send_wait(pay_out, pay_back, 2)


def fused(blk, bulkblk, ground, mod, b, wind, lift, az_n, gz, width):
    n_py = lax.axis_size("py")
    n_ring = lax.axis_size(RING)
    nyl = blk.shape[1] // az_n
    ny = nyl * n_py
    fields = (4, width, az_n, ny)
    rows_l = 9 * gz + az_n
    rows_r = 5 * gz + 5 * az_n
    vmem = pl.BlockSpec(memory_space=pltpu.VMEM)
    return pl.pallas_call(
        functools.partial(fused_kernel, n_py, n_ring, gz, width),
        out_shape=(
            jax.ShapeDtypeStruct(blk.shape, jnp.float32),
            jax.ShapeDtypeStruct(ground.shape, jnp.float32),
        ),
        in_specs=[vmem] * 5 + [pl.BlockSpec(memory_space=pltpu.SMEM)] * 2,
        out_specs=(vmem, vmem),
        scratch_shapes=[
            pltpu.VMEM((n_py, 2 * nyl * width, 4 * az_n), jnp.float32),
            pltpu.VMEM((n_py, 2 * nyl * width, 4 * az_n), jnp.float32),
            pltpu.VMEM((n_py, nyl * width, 4 * az_n), jnp.float32),
            pltpu.VMEM((n_py, nyl * width, 4 * az_n), jnp.float32),
            pltpu.SemaphoreType.DMA((4, n_py)),
            pltpu.VMEM((5, width, az_n, ny), jnp.float32),
            pltpu.VMEM(fields, jnp.float32),
            pltpu.VMEM(fields, jnp.float32),
            pltpu.VMEM((3, width, gz, ny), jnp.float32),
            pltpu.VMEM((6, width, gz, ny), jnp.float32),
            pltpu.VMEM(fields, jnp.float32),
            pltpu.VMEM((3, width, gz, ny), jnp.float32),
            pltpu.VMEM((6, width, gz, ny), jnp.float32),
            pltpu.VMEM((3, az_n, ny), jnp.float32),
            pltpu.VMEM((STEPS, rows_l, ny), jnp.float32),
            pltpu.VMEM((STEPS, rows_r, ny), jnp.float32),
            pltpu.VMEM((STEPS, rows_r, ny), jnp.float32),
            pltpu.VMEM((STEPS, rows_l, ny), jnp.float32),
            pltpu.SemaphoreType.DMA((STEPS + 1, 2)),
            pltpu.SemaphoreType.DMA((STEPS + 1, 2)),
        ],
        compiler_params=pltpu.CompilerParams(collective_id=0, has_side_effects=True),
        interpret=INTERPRET,
    )(blk, bulkblk, ground, mod, b, wind, lift)


def body(air_state, air_bulk, air_buoyancy, air_wind, ground_state, ground_moduli, ground_buoyancy):
    f_n, az_n, ny_l, nx_l = air_state.shape
    nf, gz, width, ny = ground_state.shape
    blk = air_state.reshape(f_n, az_n * ny_l, nx_l)
    bulkblk = air_bulk.reshape(az_n * ny_l, nx_l)
    ground = ground_state.reshape(nf, gz * width, ny)
    mod = ground_moduli.reshape(ground_moduli.shape[0], gz * width, ny)
    b = ground_buoyancy.reshape(gz * width, ny)
    air, ground_after = fused(blk, bulkblk, ground, mod, b, air_wind, air_buoyancy, az_n, gz, width)
    return (air.reshape(air_state.shape), ground_after.reshape(ground_state.shape))


def solution(mesh):
    placed = (
        P(None, None, "py", "px"),
        P(None, "py", "px"),
        P(),
        P(),
        P(None, None, ("px", "py"), None),
        P(None, None, ("px", "py"), None),
        P(None, ("px", "py"), None),
    )
    return jax.shard_map(
        body,
        mesh=mesh,
        in_specs=placed,
        out_specs=(P(None, None, "py", "px"), P(None, None, ("px", "py"), None)),
        check_vma=False,
    )
```

```python
import functools
import os

import jax
import jax.numpy as jnp
from jax import lax
from jax.experimental import pallas as pl
from jax.experimental.pallas import tpu as pltpu
from jax.sharding import PartitionSpec as P

STEPS = 3
RING = ("px", "py")
INTERPRET = os.environ.get("STENCIL_INTERPRET") == "1"


def trade(to_left, to_right):
    n = lax.axis_size(RING)
    from_right = lax.ppermute(to_left, RING, [(i, i - 1) for i in range(1, n)])
    from_left = lax.ppermute(to_right, RING, [(i, i + 1) for i in range(n - 1)])
    return from_left, from_right


def to_strips(block):
    f, z, ny, nx = block.shape
    parts = lax.axis_size("py")
    split = block.reshape(f, z, ny, parts, nx // parts)
    moved = lax.all_to_all(split, "py", 3, 3, tiled=True)
    return moved.transpose(0, 4, 1, 3, 2).reshape(f, nx // parts, z, parts * ny)


def from_strips(strip):
    f, nx, z, ny_all = strip.shape
    parts = lax.axis_size("py")
    split = strip.reshape(f, nx, z, parts, ny_all // parts)
    moved = lax.all_to_all(split, "py", 3, 3, tiled=True)
    return moved.transpose(0, 2, 4, 3, 1).reshape(f, z, ny_all // parts, parts * nx)


def _rows(a):
    return lax.broadcasted_iota(jnp.int32, a.shape, 0)


def _lanes(a):
    return lax.broadcasted_iota(jnp.int32, a.shape, 1)


def bz(a):
    return jnp.where(_rows(a) == 0, 0.0, pltpu.roll(a, 1, 0))


def az(a):
    n = a.shape[0]
    return jnp.where(_rows(a) == n - 1, 0.0, pltpu.roll(a, n - 1, 0))


def by(a):
    return jnp.where(_lanes(a) == 0, 0.0, pltpu.roll(a, 1, 1))


def ay(a):
    n = a.shape[1]
    return jnp.where(_lanes(a) == n - 1, 0.0, pltpu.roll(a, n - 1, 1))


def one_step(
    air_ref, bulk_ref, vel_ref, st_ref, mod_ref, b_ref, bl_ref, br_ref, fl_ref, fr_ref, scal_ref,
    air_out, vel_out, st_out, tl_out, tr_out, coef_ref, after_edges=None,
):
    width = air_ref.shape[1]
    az_n = air_ref.shape[2]
    gz = vel_ref.shape[2]

    def fl(start, count):
        return fl_ref[pl.ds(start, count), :]

    def fr(start, count):
        return fr_ref[pl.ds(start, count), :]

    def gcol(field_ref, k, left, right):
        cols = [left] + [field_ref[k, c] for c in range(width)] + [right]
        return cols

    sxx = gcol(st_ref, 0, fl(0, gz), fr(0, gz))
    sxy = gcol(st_ref, 3, fl(gz, gz), fr(gz, gz))
    sxz = gcol(st_ref, 4, fl(2 * gz, gz), fr(2 * gz, gz))
    syy = gcol(st_ref, 1, None, fr(3 * gz, gz))
    syz = gcol(st_ref, 5, None, fr(4 * gz, gz))
    szz = gcol(st_ref, 2, None, fr(5 * gz, gz))
    vx = gcol(vel_ref, 0, fl(3 * gz, gz), None)
    vy = gcol(vel_ref, 1, None, fr(6 * gz, gz))
    vz = gcol(vel_ref, 2, None, fr(7 * gz, gz))
    bb = (
        [bl_ref[pl.ds(4 * gz + 5 * az_n, gz), :]]
        + [b_ref[c] for c in range(width)]
        + [br_ref[pl.ds(8 * gz + az_n, gz), :]]
    )
    o = 4 * gz
    pr = fr(8 * gz, az_n)
    u = [fl(o, az_n), fl(o + az_n, az_n)] + [air_ref[1, c] for c in range(width)]
    v = [None, fl(o + 2 * az_n, az_n)] + [air_ref[2, c] for c in range(width)]
    w = [None, fl(o + 3 * az_n, az_n)] + [air_ref[3, c] for c in range(width)]
    p = [None, fl(o + 4 * az_n, az_n)] + [air_ref[0, c] for c in range(width)] + [pr]

    grow = lax.broadcasted_iota(jnp.int32, (gz, sxx[1].shape[1]), 0)
    arow = lax.broadcasted_iota(jnp.int32, (az_n, sxx[1].shape[1]), 0)

    vx1 = [None] * (width + 2)
    vy1 = [None] * (width + 2)
    vz1 = [None] * (width + 2)
    for e in range(width + 2):
        if e <= width:
            force_x = sxx[e + 1] - sxx[e] + sxy[e] - by(sxy[e]) + sxz[e] - bz(sxz[e])
            vx1[e] = vx[e] + bb[e] * force_x
        if e >= 1:
            force_y = sxy[e] - sxy[e - 1] + ay(syy[e]) - syy[e] + syz[e] - bz(syz[e])
            vy1[e] = vy[e] + bb[e] * force_y
            plane = jnp.broadcast_to(p[e + 1][0:1, :], szz[e].shape)
            ghost = jnp.where(grow == gz - 1, -plane, pltpu.roll(szz[e], gz - 1, 0))
            force_z = sxz[e] - sxz[e - 1] + syz[e] - by(syz[e]) + ghost - szz[e]
            vz1[e] = vz[e] + bb[e] * force_z

    def ground_col(c):
        e = c + 1
        mx, my, mz = vx1[e], vy1[e], vz1[e]
        lam = mod_ref[0, c]
        mu = mod_ref[1, c]
        longitudinal = lam + 2.0 * mu
        strain_x = mx - vx1[e - 1]
        strain_y = my - by(my)
        strain_z = mz - bz(mz)
        st_out[0, c] = st_ref[0, c] + longitudinal * strain_x + lam * (strain_y + strain_z)
        st_out[1, c] = st_ref[1, c] + longitudinal * strain_y + lam * (strain_x + strain_z)
        st_out[2, c] = st_ref[2, c] + longitudinal * strain_z + lam * (strain_x + strain_y)
        st_out[3, c] = st_ref[3, c] + mu * (ay(mx) - mx + vy1[e + 1] - my)
        sxz1 = st_ref[4, c] + mu * (az(mx) - mx + vz1[e + 1] - mz)
        syz1 = st_ref[5, c] + mu * (az(my) - my + ay(mz) - mz)
        st_out[4, c] = jnp.where(grow == gz - 1, 0.0, sxz1)
        st_out[5, c] = jnp.where(grow == gz - 1, 0.0, syz1)
        vel_out[0, c] = mx
        vel_out[1, c] = my
        vel_out[2, c] = mz
        if c == 0 and tl_out is not None:
            for k, (ref, f) in enumerate(
                [(st_out, 0), (st_out, 3), (st_out, 4), (st_out, 1), (st_out, 5), (st_out, 2),
                 (vel_out, 1), (vel_out, 2)]
            ):
                tl_out[pl.ds(k * gz, gz), :] = ref[f, 0]
        if c == width - 1 and tr_out is not None:
            for k, (ref, f) in enumerate([(st_out, 0), (st_out, 3), (st_out, 4), (vel_out, 0)]):
                tr_out[pl.ds(k * gz, gz), :] = ref[f, c]

    wind_x = coef_ref[0]
    wind_y = coef_ref[1]
    lift = coef_ref[2]
    u1 = [None] * (width + 2)
    for a in range(1, width + 2):
        u1[a] = (
            u[a]
            - wind_x * (u[a] - u[a - 1])
            - wind_y * (u[a] - by(u[a]))
            - lift * (p[a + 1] - p[a])
        )
    u1[1] = jnp.where(scal_ref[3 * az_n] > 0.5, u1[1], 0.0)

    def air_col(c):
        a = c + 2
        v1 = v[a] - wind_x * (v[a] - v[a - 1]) - wind_y * (v[a] - by(v[a])) - lift * (ay(p[a]) - p[a])
        w1 = w[a] - wind_x * (w[a] - w[a - 1]) - wind_y * (w[a] - by(w[a])) - lift * (p[a] - bz(p[a]))
        surface = jnp.broadcast_to(vz1[c + 1][gz - 1 : gz, :], w1.shape)
        w1 = jnp.where(arow == 0, surface, w1)
        pm = p[a]
        p1 = (
            pm
            - wind_x * (pm - p[a - 1])
            - wind_y * (pm - by(pm))
            - bulk_ref[c] * ((u1[a] - u1[a - 1]) + (v1 - by(v1)) + (az(w1) - w1))
        )
        air_out[0, c] = p1
        air_out[1, c] = u1[a]
        air_out[2, c] = v1
        air_out[3, c] = w1
        if c == 0 and tl_out is not None:
            tl_out[pl.ds(8 * gz, az_n), :] = p1
        if c == width - 2 and tr_out is not None:
            tr_out[pl.ds(4 * gz, az_n), :] = u1[a]
        if c == width - 1 and tr_out is not None:
            o = 4 * gz
            tr_out[pl.ds(o + az_n, az_n), :] = u1[a]
            tr_out[pl.ds(o + 2 * az_n, az_n), :] = v1
            tr_out[pl.ds(o + 3 * az_n, az_n), :] = w1
            tr_out[pl.ds(o + 4 * az_n, az_n), :] = p1

    ground_edges = [0, width - 1]
    air_edges = [0, width - 2, width - 1]
    for c in ground_edges:
        ground_col(c)
    for c in air_edges:
        air_col(c)
    if after_edges is not None:
        after_edges()
    for c in range(width):
        if c not in ground_edges:
            ground_col(c)
    for c in range(width):
        if c not in air_edges:
            air_col(c)


MESH = pl.DeviceIdType.MESH


def send_layout_kernel(air_ref, bulk_ref, out_ref):
    fields = air_ref.shape[0]
    rows = air_ref.shape[1]
    nyl = out_ref.shape[1] // 16
    nz = rows // nyl
    parts = out_ref.shape[0]
    width = air_ref.shape[2] // parts
    for yl in range(nyl):
        m = jnp.concatenate(
            [air_ref[f, pl.ds(yl, nz, stride=nyl), :] for f in range(fields)], 0
        )
        t = m.T.reshape(parts, width, m.shape[0])
        out_ref[:, pl.ds(yl * width, width), :] = t
        mb = jnp.concatenate(
            [bulk_ref[pl.ds(yl, nz, stride=nyl), :], jnp.zeros((m.shape[0] - nz, m.shape[1]), jnp.float32)], 0
        )
        tb = mb.T.reshape(parts, width, m.shape[0])
        out_ref[:, pl.ds(nyl * width + yl * width, width), :] = tb


def recv_layout_kernel(width, nyl, pay_ref, out_ref):
    fields = out_ref.shape[0]
    parts = pay_ref.shape[0]
    nz = pay_ref.shape[2] // fields
    for yl in range(nyl):
        n = pay_ref[:, pl.ds(yl, width, stride=nyl), :].reshape(parts * width, fields * nz)
        t = n.T
        for f in range(fields):
            out_ref[f, pl.ds(yl, nz, stride=nyl), :] = t[f * nz : (f + 1) * nz]


def from_strips_fast(payload, fields, az_n, width):
    parts = payload.shape[0]
    nyl = payload.shape[1] // width
    got = lax.all_to_all(payload, "py", 0, 0, tiled=True)
    out = pl.pallas_call(
        functools.partial(recv_layout_kernel, width, nyl),
        out_shape=jax.ShapeDtypeStruct((fields, az_n * nyl, width * parts), jnp.float32),
        interpret=INTERPRET,
    )(got)
    return out.reshape(fields, az_n, nyl, width * parts)


def to_strips_fast(air_state, air_bulk):
    f, z, ny, nx = air_state.shape
    parts = lax.axis_size("py")
    width = nx // parts
    flat = air_state.reshape(f, z * ny, nx)
    bulk = air_bulk.reshape(z * ny, nx)
    payload = pl.pallas_call(
        send_layout_kernel,
        out_shape=jax.ShapeDtypeStruct((parts, 2 * ny * width, f * z), jnp.float32),
        interpret=INTERPRET,
    )(flat, bulk)
    return lax.all_to_all(payload, "py", 0, 0, tiled=True)


class Strided:
    def __init__(self, ref, layers, width, offset=0, fields=None, clear=()):
        self.ref = ref
        self.layers = layers
        self.width = width
        self.offset = offset
        self.clear = clear
        n = ref.shape[0] - offset if fields is None else fields
        self.shape = (n, width, layers, ref.shape[-1])

    def _rows(self, c):
        return pl.ds(c, self.layers, stride=self.width)

    def __getitem__(self, index):
        f, c = index
        value = self.ref[self.offset + f, self._rows(c), :]
        if f in self.clear:
            top = lax.broadcasted_iota(jnp.int32, value.shape, 0) == self.layers - 1
            value = jnp.where(top, 0.0, value)
        return value

    def __setitem__(self, index, value):
        f, c = index
        self.ref[self.offset + f, self._rows(c), :] = value


class Plane:
    def __init__(self, ref, layers, width):
        self.ref = ref
        self.layers = layers
        self.width = width

    def __getitem__(self, c):
        return self.ref[pl.ds(c, self.layers, stride=self.width), :]


class Scalars:
    def __init__(self, wind_ref, lift_ref, keep):
        self.wind_ref = wind_ref
        self.lift_ref = lift_ref
        self.keep = keep
        self.levels = lift_ref.shape[0]

    def __getitem__(self, i):
        n = self.levels
        if i < 2 * n:
            return self.wind_ref[i // n, i % n]
        if i < 3 * n:
            return self.lift_ref[i - 2 * n]
        return self.keep


def fused_kernel(
    n_py, n_ring, gz, width, blk_ref, bulkblk_ref, gin_ref, modin_ref, bin_ref, wind_ref, lift_ref,
    airblk_out, gout_ref, pay_ref, pay_send, pay_out, pay_back, a2a_sem, air_ref, air_out,
    air_a, vel_a, st_a, air_b, vel_b, st_b, coef_ref, send_l, send_r, recv_l, recv_r,
    send_sem, recv_sem,
):
    az_n = air_ref.shape[2]
    ny = air_ref.shape[3]
    me = lax.axis_index("px") * n_py + lax.axis_index("py")
    vel_ref = Strided(gin_ref, gz, width, 0, 3)
    st_ref = Strided(gin_ref, gz, width, 3, 6, clear=(4, 5))
    mod_ref = Strided(modin_ref, gz, width)
    b_ref = Plane(bin_ref, gz, width)
    vel_out = Strided(gout_ref, gz, width, 0, 3)
    st_out = Strided(gout_ref, gz, width, 3, 6)
    scal_ref = Scalars(wind_ref, lift_ref, jnp.where(me > 0, 1.0, 0.0))
    has_left = me > 0
    has_right = me < n_ring - 1
    left = ((me - 1) // n_py, (me - 1) % n_py)
    right = ((me + 1) // n_py, (me + 1) % n_py)
    rows_l = send_l.shape[1]
    rows_r = send_r.shape[1]

    nyl = ny // n_py
    my_py = lax.axis_index("py")
    my_px = lax.axis_index("px")
    n_px = n_ring // n_py
    extra_l = (my_py == 0) & (my_px > 0)
    extra_r = (my_py == n_py - 1) & (my_px < n_px - 1)
    nz = az_n
    for yl in range(nyl):
        m = jnp.concatenate([blk_ref[f, pl.ds(yl, nz, stride=nyl), :] for f in range(4)], 0)
        pay_send[:, pl.ds(yl * width, width), :] = m.T.reshape(n_py, width, 4 * nz)
        mb = jnp.concatenate(
            [bulkblk_ref[pl.ds(yl, nz, stride=nyl), :], jnp.zeros((3 * nz, n_py * width), jnp.float32)], 0
        )
        pay_send[:, pl.ds(nyl * width + yl * width, width), :] = mb.T.reshape(n_py, width, 4 * nz)

    @pl.when(jnp.logical_not(has_left))
    def _():
        recv_l[...] = jnp.zeros_like(recv_l)

    @pl.when(jnp.logical_not(has_right))
    def _():
        recv_r[...] = jnp.zeros_like(recv_r)

    barrier = pltpu.get_barrier_semaphore()

    for q in range(n_py):

        @pl.when(my_py != q)
        def _():
            pl.semaphore_signal(barrier, inc=1, device_id=(my_px, q), device_id_type=MESH)

    @pl.when(extra_l)
    def _():
        pl.semaphore_signal(barrier, inc=1, device_id=left, device_id_type=MESH)

    @pl.when(extra_r)
    def _():
        pl.semaphore_signal(barrier, inc=1, device_id=right, device_id_type=MESH)

    for count in range(3):

        @pl.when(extra_l.astype(jnp.int32) + extra_r.astype(jnp.int32) == count)
        def _():
            pl.semaphore_wait(barrier, n_py - 1 + count)

    def group_copy(src, dst, k, q, slot):
        return pltpu.make_async_remote_copy(
            src_ref=src.at[q],
            dst_ref=dst.at[slot],
            send_sem=a2a_sem.at[k, q],
            recv_sem=a2a_sem.at[k + 1, slot],
            device_id=(my_px, q),
            device_id_type=MESH,
        )

    def group_send(src, dst, k):
        for step in range(1, n_py):
            group_copy(src, dst, k, lax.rem(my_py + step, n_py), my_py).start()

        dst[my_py] = src[my_py]

    def group_wait(src, dst, k):
        for q in range(n_py):

            @pl.when(my_py != q)
            def _():
                group_copy(src, dst, k, q, q).wait_recv()

    def group_send_wait(src, dst, k):
        for q in range(n_py):

            @pl.when(my_py != q)
            def _():
                group_copy(src, dst, k, q, my_py).wait_send()

    def copies(n, count_l, count_r, first_l=0, first_r=0, slot=None):
        slot = n if slot is None else slot
        to_left = pltpu.make_async_remote_copy(
            src_ref=send_l.at[n, pl.ds(first_l, count_l)],
            dst_ref=recv_r.at[n, pl.ds(first_l, count_l)],
            send_sem=send_sem.at[slot, 0],
            recv_sem=recv_sem.at[slot, 1],
            device_id=left,
            device_id_type=MESH,
        )
        to_right = pltpu.make_async_remote_copy(
            src_ref=send_r.at[n, pl.ds(first_r, count_r)],
            dst_ref=recv_l.at[n, pl.ds(first_r, count_r)],
            send_sem=send_sem.at[slot, 1],
            recv_sem=recv_sem.at[slot, 0],
            device_id=right,
            device_id_type=MESH,
        )

        return to_left, to_right

    def start(n, *args):
        to_left, to_right = copies(n, *args)

        @pl.when(has_left)
        def _():
            to_left.start()

        @pl.when(has_right)
        def _():
            to_right.start()

    def wait_recv(n, *args):
        to_left, to_right = copies(n, *args)

        @pl.when(has_left)
        def _():
            to_right.wait_recv()

        @pl.when(has_right)
        def _():
            to_left.wait_recv()

    def wait_send(n, *args):
        to_left, to_right = copies(n, *args)

        @pl.when(has_left)
        def _():
            to_left.wait_send()

        @pl.when(has_right)
        def _():
            to_right.wait_send()

    tl = send_l.at[0]
    tr = send_r.at[0]
    left_rows = [st_ref[f, 0] for f in (0, 3, 4, 1, 5, 2)] + [vel_ref[1, 0], vel_ref[2, 0]]
    for k, value in enumerate(left_rows):
        tl[pl.ds(k * gz, gz), :] = value
    right_rows = [st_ref[f, width - 1] for f in (0, 3, 4)] + [vel_ref[0, width - 1]]
    for k, value in enumerate(right_rows):
        tr[pl.ds(k * gz, gz), :] = value
    ground_part = (8 * gz, 4 * gz, 0, 0, STEPS)
    start(0, *ground_part)

    group_send(pay_send, pay_ref, 0)
    for k in range(3):
        for z in range(az_n):
            coef_ref[k, pl.ds(z, 1), :] = jnp.full((1, ny), scal_ref[k * az_n + z], jnp.float32)
    group_wait(pay_send, pay_ref, 0)
    for xl in range(width):
        n_air = pay_ref[:, pl.ds(xl, nyl, stride=width), :].reshape(ny, 4 * az_n)
        t = n_air.T
        for f in range(4):
            air_ref[f, xl] = t[f * az_n : (f + 1) * az_n]
        n_bulk = pay_ref[:, pl.ds(nyl * width + xl, nyl, stride=width), :].reshape(ny, 4 * az_n)
        air_ref[4, xl] = n_bulk.T[0:az_n]


    tl[pl.ds(8 * gz, az_n), :] = air_ref[0, 0]
    tl[pl.ds(8 * gz + az_n, gz), :] = b_ref[0]
    o = 4 * gz
    tr[pl.ds(o, az_n), :] = air_ref[1, width - 2]
    for k, f in enumerate((1, 2, 3, 0)):
        tr[pl.ds(o + (k + 1) * az_n, az_n), :] = air_ref[f, width - 1]
    tr[pl.ds(o + 5 * az_n, gz), :] = b_ref[width - 1]

    full_l = 8 * gz + az_n
    full_r = 4 * gz + 5 * az_n
    counts = [(rows_l, rows_r)] + [(full_l, full_r)] * (STEPS - 1)
    air_part = (rows_l - 8 * gz, rows_r - 4 * gz, 8 * gz, 4 * gz, 0)
    start(0, *air_part)
    wait_recv(0, *ground_part)
    wait_recv(0, *air_part)
    states = [
        (air_ref, vel_ref, st_ref),
        (air_a, vel_a, st_a),
        (air_b, vel_b, st_b),
        (air_out, vel_out, st_out),
    ]
    for n in range(STEPS):
        src = states[n] if n < len(states) - 1 else states[-2]
        dst = states[n + 1] if n + 1 < STEPS else states[-1]
        last = n + 1 == STEPS
        one_step(
            src[0], air_ref.at[4], src[1], src[2], mod_ref, b_ref, recv_l.at[0], recv_r.at[0],
            recv_l.at[n], recv_r.at[n], scal_ref, dst[0], dst[1], dst[2],
            None if last else send_l.at[n + 1], None if last else send_r.at[n + 1], coef_ref,
            None if last else functools.partial(start, n + 1, *counts[n + 1]),
        )
        if not last:
            wait_recv(n + 1, *counts[n + 1])
    for xl in range(width):
        m = jnp.concatenate([air_out[f, xl] for f in range(4)], 0)
        t = m.T.reshape(n_py, nyl, 4 * az_n)
        pay_out[:, pl.ds(xl * nyl, nyl), :] = t
    group_send(pay_out, pay_back, 2)
    group_wait(pay_out, pay_back, 2)
    for yl in range(nyl):
        nb = pay_back[:, pl.ds(yl, width, stride=nyl), :].reshape(n_py * width, 4 * nz)
        tb = nb.T
        for f in range(4):
            airblk_out[f, pl.ds(yl, nz, stride=nyl), :] = tb[f * nz : (f + 1) * nz]
    wait_send(0, *ground_part)
    wait_send(0, *air_part)
    for n in range(1, STEPS):
        wait_send(n, *counts[n])
    group_send_wait(pay_send, pay_ref, 0)
    group_send_wait(pay_out, pay_back, 2)


def fused(blk, bulkblk, ground, mod, b, wind, lift, az_n, gz, width):
    n_py = lax.axis_size("py")
    n_ring = lax.axis_size(RING)
    nyl = blk.shape[1] // az_n
    ny = nyl * n_py
    fields = (4, width, az_n, ny)
    rows_l = 9 * gz + az_n
    rows_r = 5 * gz + 5 * az_n
    vmem = pl.BlockSpec(memory_space=pltpu.VMEM)
    return pl.pallas_call(
        functools.partial(fused_kernel, n_py, n_ring, gz, width),
        out_shape=(
            jax.ShapeDtypeStruct(blk.shape, jnp.float32),
            jax.ShapeDtypeStruct(ground.shape, jnp.float32),
        ),
        in_specs=[vmem] * 5 + [pl.BlockSpec(memory_space=pltpu.SMEM)] * 2,
        out_specs=(vmem, vmem),
        scratch_shapes=[
            pltpu.VMEM((n_py, 2 * nyl * width, 4 * az_n), jnp.float32),
            pltpu.VMEM((n_py, 2 * nyl * width, 4 * az_n), jnp.float32),
            pltpu.VMEM((n_py, nyl * width, 4 * az_n), jnp.float32),
            pltpu.VMEM((n_py, nyl * width, 4 * az_n), jnp.float32),
            pltpu.SemaphoreType.DMA((4, n_py)),
            pltpu.VMEM((5, width, az_n, ny), jnp.float32),
            pltpu.VMEM(fields, jnp.float32),
            pltpu.VMEM(fields, jnp.float32),
            pltpu.VMEM((3, width, gz, ny), jnp.float32),
            pltpu.VMEM((6, width, gz, ny), jnp.float32),
            pltpu.VMEM(fields, jnp.float32),
            pltpu.VMEM((3, width, gz, ny), jnp.float32),
            pltpu.VMEM((6, width, gz, ny), jnp.float32),
            pltpu.VMEM((3, az_n, ny), jnp.float32),
            pltpu.VMEM((STEPS, rows_l, ny), jnp.float32),
            pltpu.VMEM((STEPS, rows_r, ny), jnp.float32),
            pltpu.VMEM((STEPS, rows_r, ny), jnp.float32),
            pltpu.VMEM((STEPS, rows_l, ny), jnp.float32),
            pltpu.SemaphoreType.DMA((STEPS + 1, 2)),
            pltpu.SemaphoreType.DMA((STEPS + 1, 2)),
        ],
        compiler_params=pltpu.CompilerParams(collective_id=0, has_side_effects=True),
        interpret=INTERPRET,
    )(blk, bulkblk, ground, mod, b, wind, lift)


def body(air_state, air_bulk, air_buoyancy, air_wind, ground_state, ground_moduli, ground_buoyancy):
    f_n, az_n, ny_l, nx_l = air_state.shape
    nf, gz, width, ny = ground_state.shape
    blk = air_state.reshape(f_n, az_n * ny_l, nx_l)
    bulkblk = air_bulk.reshape(az_n * ny_l, nx_l)
    ground = ground_state.reshape(nf, gz * width, ny)
    mod = ground_moduli.reshape(ground_moduli.shape[0], gz * width, ny)
    b = ground_buoyancy.reshape(gz * width, ny)
    air, ground_after = fused(blk, bulkblk, ground, mod, b, air_wind, air_buoyancy, az_n, gz, width)
    return (air.reshape(air_state.shape), ground_after.reshape(ground_state.shape))


def solution(mesh):
    placed = (
        P(None, None, "py", "px"),
        P(None, "py", "px"),
        P(),
        P(),
        P(None, None, ("px", "py"), None),
        P(None, None, ("px", "py"), None),
        P(None, ("px", "py"), None),
    )
    return jax.shard_map(
        body,
        mesh=mesh,
        in_specs=placed,
        out_specs=(P(None, None, "py", "px"), P(None, None, ("px", "py"), None)),
        check_vma=False,
    )
```

```python
import functools
import os

import jax
import jax.numpy as jnp
from jax import lax
from jax.experimental import pallas as pl
from jax.experimental.pallas import tpu as pltpu
from jax.sharding import PartitionSpec as P

STEPS = 3
RING = ("px", "py")
INTERPRET = os.environ.get("STENCIL_INTERPRET") == "1"


def trade(to_left, to_right):
    n = lax.axis_size(RING)
    from_right = lax.ppermute(to_left, RING, [(i, i - 1) for i in range(1, n)])
    from_left = lax.ppermute(to_right, RING, [(i, i + 1) for i in range(n - 1)])
    return from_left, from_right


def to_strips(block):
    f, z, ny, nx = block.shape
    parts = lax.axis_size("py")
    split = block.reshape(f, z, ny, parts, nx // parts)
    moved = lax.all_to_all(split, "py", 3, 3, tiled=True)
    return moved.transpose(0, 4, 1, 3, 2).reshape(f, nx // parts, z, parts * ny)


def from_strips(strip):
    f, nx, z, ny_all = strip.shape
    parts = lax.axis_size("py")
    split = strip.reshape(f, nx, z, parts, ny_all // parts)
    moved = lax.all_to_all(split, "py", 3, 3, tiled=True)
    return moved.transpose(0, 2, 4, 3, 1).reshape(f, z, ny_all // parts, parts * nx)


def _rows(a):
    return lax.broadcasted_iota(jnp.int32, a.shape, 0)


def _lanes(a):
    return lax.broadcasted_iota(jnp.int32, a.shape, 1)


def bz(a):
    return jnp.where(_rows(a) == 0, 0.0, pltpu.roll(a, 1, 0))


def az(a):
    n = a.shape[0]
    return jnp.where(_rows(a) == n - 1, 0.0, pltpu.roll(a, n - 1, 0))


def by(a):
    return jnp.where(_lanes(a) == 0, 0.0, pltpu.roll(a, 1, 1))


def ay(a):
    n = a.shape[1]
    return jnp.where(_lanes(a) == n - 1, 0.0, pltpu.roll(a, n - 1, 1))


def one_step(
    air_ref, bulk_ref, vel_ref, st_ref, mod_ref, b_ref, bl_ref, br_ref, fl_ref, fr_ref, scal_ref,
    air_out, vel_out, st_out, tl_out, tr_out, coef_ref, after_edges=None,
):
    width = air_ref.shape[1]
    az_n = air_ref.shape[2]
    gz = vel_ref.shape[2]

    def fl(start, count):
        return fl_ref[pl.ds(start, count), :]

    def fr(start, count):
        return fr_ref[pl.ds(start, count), :]

    def gcol(field_ref, k, left, right):
        cols = [left] + [field_ref[k, c] for c in range(width)] + [right]
        return cols

    sxx = gcol(st_ref, 0, fl(0, gz), fr(0, gz))
    sxy = gcol(st_ref, 3, fl(gz, gz), fr(gz, gz))
    sxz = gcol(st_ref, 4, fl(2 * gz, gz), fr(2 * gz, gz))
    syy = gcol(st_ref, 1, None, fr(3 * gz, gz))
    syz = gcol(st_ref, 5, None, fr(4 * gz, gz))
    szz = gcol(st_ref, 2, None, fr(5 * gz, gz))
    vx = gcol(vel_ref, 0, fl(3 * gz, gz), None)
    vy = gcol(vel_ref, 1, None, fr(6 * gz, gz))
    vz = gcol(vel_ref, 2, None, fr(7 * gz, gz))
    bb = (
        [bl_ref[pl.ds(4 * gz + 5 * az_n, gz), :]]
        + [b_ref[c] for c in range(width)]
        + [br_ref[pl.ds(8 * gz + az_n, gz), :]]
    )
    o = 4 * gz
    pr = fr(8 * gz, az_n)
    u = [fl(o, az_n), fl(o + az_n, az_n)] + [air_ref[1, c] for c in range(width)]
    v = [None, fl(o + 2 * az_n, az_n)] + [air_ref[2, c] for c in range(width)]
    w = [None, fl(o + 3 * az_n, az_n)] + [air_ref[3, c] for c in range(width)]
    p = [None, fl(o + 4 * az_n, az_n)] + [air_ref[0, c] for c in range(width)] + [pr]

    grow = lax.broadcasted_iota(jnp.int32, (gz, sxx[1].shape[1]), 0)
    arow = lax.broadcasted_iota(jnp.int32, (az_n, sxx[1].shape[1]), 0)

    vx1 = [None] * (width + 2)
    vy1 = [None] * (width + 2)
    vz1 = [None] * (width + 2)
    for e in range(width + 2):
        if e <= width:
            force_x = sxx[e + 1] - sxx[e] + sxy[e] - by(sxy[e]) + sxz[e] - bz(sxz[e])
            vx1[e] = vx[e] + bb[e] * force_x
        if e >= 1:
            force_y = sxy[e] - sxy[e - 1] + ay(syy[e]) - syy[e] + syz[e] - bz(syz[e])
            vy1[e] = vy[e] + bb[e] * force_y
            plane = jnp.broadcast_to(p[e + 1][0:1, :], szz[e].shape)
            ghost = jnp.where(grow == gz - 1, -plane, pltpu.roll(szz[e], gz - 1, 0))
            force_z = sxz[e] - sxz[e - 1] + syz[e] - by(syz[e]) + ghost - szz[e]
            vz1[e] = vz[e] + bb[e] * force_z

    def ground_col(c):
        e = c + 1
        mx, my, mz = vx1[e], vy1[e], vz1[e]
        lam = mod_ref[0, c]
        mu = mod_ref[1, c]
        longitudinal = lam + 2.0 * mu
        strain_x = mx - vx1[e - 1]
        strain_y = my - by(my)
        strain_z = mz - bz(mz)
        st_out[0, c] = st_ref[0, c] + longitudinal * strain_x + lam * (strain_y + strain_z)
        st_out[1, c] = st_ref[1, c] + longitudinal * strain_y + lam * (strain_x + strain_z)
        st_out[2, c] = st_ref[2, c] + longitudinal * strain_z + lam * (strain_x + strain_y)
        st_out[3, c] = st_ref[3, c] + mu * (ay(mx) - mx + vy1[e + 1] - my)
        sxz1 = st_ref[4, c] + mu * (az(mx) - mx + vz1[e + 1] - mz)
        syz1 = st_ref[5, c] + mu * (az(my) - my + ay(mz) - mz)
        st_out[4, c] = jnp.where(grow == gz - 1, 0.0, sxz1)
        st_out[5, c] = jnp.where(grow == gz - 1, 0.0, syz1)
        vel_out[0, c] = mx
        vel_out[1, c] = my
        vel_out[2, c] = mz
        if c == 0 and tl_out is not None:
            for k, (ref, f) in enumerate(
                [(st_out, 0), (st_out, 3), (st_out, 4), (st_out, 1), (st_out, 5), (st_out, 2),
                 (vel_out, 1), (vel_out, 2)]
            ):
                tl_out[pl.ds(k * gz, gz), :] = ref[f, 0]
        if c == width - 1 and tr_out is not None:
            for k, (ref, f) in enumerate([(st_out, 0), (st_out, 3), (st_out, 4), (vel_out, 0)]):
                tr_out[pl.ds(k * gz, gz), :] = ref[f, c]

    wind_x = coef_ref[0]
    wind_y = coef_ref[1]
    lift = coef_ref[2]
    u1 = [None] * (width + 2)
    for a in range(1, width + 2):
        u1[a] = (
            u[a]
            - wind_x * (u[a] - u[a - 1])
            - wind_y * (u[a] - by(u[a]))
            - lift * (p[a + 1] - p[a])
        )
    u1[1] = jnp.where(scal_ref[3 * az_n] > 0.5, u1[1], 0.0)

    def air_col(c):
        a = c + 2
        v1 = v[a] - wind_x * (v[a] - v[a - 1]) - wind_y * (v[a] - by(v[a])) - lift * (ay(p[a]) - p[a])
        w1 = w[a] - wind_x * (w[a] - w[a - 1]) - wind_y * (w[a] - by(w[a])) - lift * (p[a] - bz(p[a]))
        surface = jnp.broadcast_to(vz1[c + 1][gz - 1 : gz, :], w1.shape)
        w1 = jnp.where(arow == 0, surface, w1)
        pm = p[a]
        p1 = (
            pm
            - wind_x * (pm - p[a - 1])
            - wind_y * (pm - by(pm))
            - bulk_ref[c] * ((u1[a] - u1[a - 1]) + (v1 - by(v1)) + (az(w1) - w1))
        )
        air_out[0, c] = p1
        air_out[1, c] = u1[a]
        air_out[2, c] = v1
        air_out[3, c] = w1
        if c == 0 and tl_out is not None:
            tl_out[pl.ds(8 * gz, az_n), :] = p1
        if c == width - 2 and tr_out is not None:
            tr_out[pl.ds(4 * gz, az_n), :] = u1[a]
        if c == width - 1 and tr_out is not None:
            o = 4 * gz
            tr_out[pl.ds(o + az_n, az_n), :] = u1[a]
            tr_out[pl.ds(o + 2 * az_n, az_n), :] = v1
            tr_out[pl.ds(o + 3 * az_n, az_n), :] = w1
            tr_out[pl.ds(o + 4 * az_n, az_n), :] = p1

    ground_edges = [0, width - 1]
    air_edges = [0, width - 2, width - 1]
    for c in ground_edges:
        ground_col(c)
    for c in air_edges:
        air_col(c)
    if after_edges is not None:
        after_edges()
    for c in range(width):
        if c not in ground_edges:
            ground_col(c)
    for c in range(width):
        if c not in air_edges:
            air_col(c)


MESH = pl.DeviceIdType.MESH


def send_layout_kernel(air_ref, bulk_ref, out_ref):
    fields = air_ref.shape[0]
    rows = air_ref.shape[1]
    nyl = out_ref.shape[1] // 16
    nz = rows // nyl
    parts = out_ref.shape[0]
    width = air_ref.shape[2] // parts
    for yl in range(nyl):
        m = jnp.concatenate(
            [air_ref[f, pl.ds(yl, nz, stride=nyl), :] for f in range(fields)], 0
        )
        t = m.T.reshape(parts, width, m.shape[0])
        out_ref[:, pl.ds(yl * width, width), :] = t
        mb = jnp.concatenate(
            [bulk_ref[pl.ds(yl, nz, stride=nyl), :], jnp.zeros((m.shape[0] - nz, m.shape[1]), jnp.float32)], 0
        )
        tb = mb.T.reshape(parts, width, m.shape[0])
        out_ref[:, pl.ds(nyl * width + yl * width, width), :] = tb


def recv_layout_kernel(width, nyl, pay_ref, out_ref):
    fields = out_ref.shape[0]
    parts = pay_ref.shape[0]
    nz = pay_ref.shape[2] // fields
    for yl in range(nyl):
        n = pay_ref[:, pl.ds(yl, width, stride=nyl), :].reshape(parts * width, fields * nz)
        t = n.T
        for f in range(fields):
            out_ref[f, pl.ds(yl, nz, stride=nyl), :] = t[f * nz : (f + 1) * nz]


def from_strips_fast(payload, fields, az_n, width):
    parts = payload.shape[0]
    nyl = payload.shape[1] // width
    got = lax.all_to_all(payload, "py", 0, 0, tiled=True)
    out = pl.pallas_call(
        functools.partial(recv_layout_kernel, width, nyl),
        out_shape=jax.ShapeDtypeStruct((fields, az_n * nyl, width * parts), jnp.float32),
        interpret=INTERPRET,
    )(got)
    return out.reshape(fields, az_n, nyl, width * parts)


def to_strips_fast(air_state, air_bulk):
    f, z, ny, nx = air_state.shape
    parts = lax.axis_size("py")
    width = nx // parts
    flat = air_state.reshape(f, z * ny, nx)
    bulk = air_bulk.reshape(z * ny, nx)
    payload = pl.pallas_call(
        send_layout_kernel,
        out_shape=jax.ShapeDtypeStruct((parts, 2 * ny * width, f * z), jnp.float32),
        interpret=INTERPRET,
    )(flat, bulk)
    return lax.all_to_all(payload, "py", 0, 0, tiled=True)


class Strided:
    def __init__(self, ref, layers, width, offset=0, fields=None, clear=()):
        self.ref = ref
        self.layers = layers
        self.width = width
        self.offset = offset
        self.clear = clear
        n = ref.shape[0] - offset if fields is None else fields
        self.shape = (n, width, layers, ref.shape[-1])

    def _rows(self, c):
        return pl.ds(c, self.layers, stride=self.width)

    def __getitem__(self, index):
        f, c = index
        value = self.ref[self.offset + f, self._rows(c), :]
        if f in self.clear:
            top = lax.broadcasted_iota(jnp.int32, value.shape, 0) == self.layers - 1
            value = jnp.where(top, 0.0, value)
        return value

    def __setitem__(self, index, value):
        f, c = index
        self.ref[self.offset + f, self._rows(c), :] = value


class Plane:
    def __init__(self, ref, layers, width):
        self.ref = ref
        self.layers = layers
        self.width = width

    def __getitem__(self, c):
        return self.ref[pl.ds(c, self.layers, stride=self.width), :]


class Scalars:
    def __init__(self, wind_ref, lift_ref, keep):
        self.wind_ref = wind_ref
        self.lift_ref = lift_ref
        self.keep = keep
        self.levels = lift_ref.shape[0]

    def __getitem__(self, i):
        n = self.levels
        if i < 2 * n:
            return self.wind_ref[i // n, i % n]
        if i < 3 * n:
            return self.lift_ref[i - 2 * n]
        return self.keep


def fused_kernel(
    n_py, n_ring, gz, width, blk_ref, bulkblk_ref, gin_ref, modin_ref, bin_ref, wind_ref, lift_ref,
    airblk_out, gout_ref, pay_ref, pay_send, pay_out, pay_back, a2a_sem, air_ref, air_out,
    air_a, vel_a, st_a, air_b, vel_b, st_b, coef_ref, send_l, send_r, recv_l, recv_r,
    send_sem, recv_sem,
):
    az_n = air_ref.shape[2]
    ny = air_ref.shape[3]
    me = lax.axis_index("px") * n_py + lax.axis_index("py")
    vel_ref = Strided(gin_ref, gz, width, 0, 3)
    st_ref = Strided(gin_ref, gz, width, 3, 6, clear=(4, 5))
    mod_ref = Strided(modin_ref, gz, width)
    b_ref = Plane(bin_ref, gz, width)
    vel_out = Strided(gout_ref, gz, width, 0, 3)
    st_out = Strided(gout_ref, gz, width, 3, 6)
    scal_ref = Scalars(wind_ref, lift_ref, jnp.where(me > 0, 1.0, 0.0))
    has_left = me > 0
    has_right = me < n_ring - 1
    left = ((me - 1) // n_py, (me - 1) % n_py)
    right = ((me + 1) // n_py, (me + 1) % n_py)
    rows_l = send_l.shape[1]
    rows_r = send_r.shape[1]

    nyl = ny // n_py
    my_py = lax.axis_index("py")
    my_px = lax.axis_index("px")
    n_px = n_ring // n_py
    extra_l = (my_py == 0) & (my_px > 0)
    extra_r = (my_py == n_py - 1) & (my_px < n_px - 1)
    nz = az_n
    for yl in range(nyl):
        m = jnp.concatenate([blk_ref[f, pl.ds(yl, nz, stride=nyl), :] for f in range(4)], 0)
        pay_send[:, pl.ds(yl * width, width), :] = m.T.reshape(n_py, width, 4 * nz)
        mb = jnp.concatenate(
            [bulkblk_ref[pl.ds(yl, nz, stride=nyl), :], jnp.zeros((3 * nz, n_py * width), jnp.float32)], 0
        )
        pay_send[:, pl.ds(nyl * width + yl * width, width), :] = mb.T.reshape(n_py, width, 4 * nz)

    @pl.when(jnp.logical_not(has_left))
    def _():
        recv_l[...] = jnp.zeros_like(recv_l)

    @pl.when(jnp.logical_not(has_right))
    def _():
        recv_r[...] = jnp.zeros_like(recv_r)

    barrier = pltpu.get_barrier_semaphore()

    for q in range(n_py):

        @pl.when(my_py != q)
        def _():
            pl.semaphore_signal(barrier, inc=1, device_id=(my_px, q), device_id_type=MESH)

    @pl.when(extra_l)
    def _():
        pl.semaphore_signal(barrier, inc=1, device_id=left, device_id_type=MESH)

    @pl.when(extra_r)
    def _():
        pl.semaphore_signal(barrier, inc=1, device_id=right, device_id_type=MESH)

    for count in range(3):

        @pl.when(extra_l.astype(jnp.int32) + extra_r.astype(jnp.int32) == count)
        def _():
            pl.semaphore_wait(barrier, n_py - 1 + count)

    def group_copy(src, dst, k, q, slot):
        return pltpu.make_async_remote_copy(
            src_ref=src.at[q],
            dst_ref=dst.at[slot],
            send_sem=a2a_sem.at[k, q],
            recv_sem=a2a_sem.at[k + 1, slot],
            device_id=(my_px, q),
            device_id_type=MESH,
        )

    def group_send(src, dst, k):
        for step in range(1, n_py):
            group_copy(src, dst, k, lax.rem(my_py + step, n_py), my_py).start()

        dst[my_py] = src[my_py]

    def group_wait(src, dst, k):
        for q in range(n_py):

            @pl.when(my_py != q)
            def _():
                group_copy(src, dst, k, q, q).wait_recv()

    def group_send_wait(src, dst, k):
        for q in range(n_py):

            @pl.when(my_py != q)
            def _():
                group_copy(src, dst, k, q, my_py).wait_send()

    def copies(n, count_l, count_r, first_l=0, first_r=0, slot=None):
        slot = n if slot is None else slot
        to_left = pltpu.make_async_remote_copy(
            src_ref=send_l.at[n, pl.ds(first_l, count_l)],
            dst_ref=recv_r.at[n, pl.ds(first_l, count_l)],
            send_sem=send_sem.at[slot, 0],
            recv_sem=recv_sem.at[slot, 1],
            device_id=left,
            device_id_type=MESH,
        )
        to_right = pltpu.make_async_remote_copy(
            src_ref=send_r.at[n, pl.ds(first_r, count_r)],
            dst_ref=recv_l.at[n, pl.ds(first_r, count_r)],
            send_sem=send_sem.at[slot, 1],
            recv_sem=recv_sem.at[slot, 0],
            device_id=right,
            device_id_type=MESH,
        )

        return to_left, to_right

    def start(n, *args):
        to_left, to_right = copies(n, *args)

        @pl.when(has_left)
        def _():
            to_left.start()

        @pl.when(has_right)
        def _():
            to_right.start()

    def wait_recv(n, *args):
        to_left, to_right = copies(n, *args)

        @pl.when(has_left)
        def _():
            to_right.wait_recv()

        @pl.when(has_right)
        def _():
            to_left.wait_recv()

    def wait_send(n, *args):
        to_left, to_right = copies(n, *args)

        @pl.when(has_left)
        def _():
            to_left.wait_send()

        @pl.when(has_right)
        def _():
            to_right.wait_send()

    tl = send_l.at[0]
    tr = send_r.at[0]
    left_rows = [st_ref[f, 0] for f in (0, 3, 4, 1, 5, 2)] + [vel_ref[1, 0], vel_ref[2, 0]]
    for k, value in enumerate(left_rows):
        tl[pl.ds(k * gz, gz), :] = value
    right_rows = [st_ref[f, width - 1] for f in (0, 3, 4)] + [vel_ref[0, width - 1]]
    for k, value in enumerate(right_rows):
        tr[pl.ds(k * gz, gz), :] = value
    ground_part = (8 * gz, 4 * gz, 0, 0, STEPS)
    start(0, *ground_part)

    group_send(pay_send, pay_ref, 0)
    for k in range(3):
        for z in range(az_n):
            coef_ref[k, pl.ds(z, 1), :] = jnp.full((1, ny), scal_ref[k * az_n + z], jnp.float32)
    group_wait(pay_send, pay_ref, 0)
    for xl in range(width):
        n_air = pay_ref[:, pl.ds(xl, nyl, stride=width), :].reshape(ny, 4 * az_n)
        t = n_air.T
        for f in range(4):
            air_ref[f, xl] = t[f * az_n : (f + 1) * az_n]


    tl[pl.ds(8 * gz, az_n), :] = air_ref[0, 0]
    tl[pl.ds(8 * gz + az_n, gz), :] = b_ref[0]
    o = 4 * gz
    tr[pl.ds(o, az_n), :] = air_ref[1, width - 2]
    for k, f in enumerate((1, 2, 3, 0)):
        tr[pl.ds(o + (k + 1) * az_n, az_n), :] = air_ref[f, width - 1]
    tr[pl.ds(o + 5 * az_n, gz), :] = b_ref[width - 1]

    full_l = 8 * gz + az_n
    full_r = 4 * gz + 5 * az_n
    counts = [(rows_l, rows_r)] + [(full_l, full_r)] * (STEPS - 1)
    air_part = (rows_l - 8 * gz, rows_r - 4 * gz, 8 * gz, 4 * gz, 0)
    start(0, *air_part)
    for xl in range(width):
        n_bulk = pay_ref[:, pl.ds(nyl * width + xl, nyl, stride=width), :].reshape(ny, 4 * az_n)
        air_ref[4, xl] = n_bulk.T[0:az_n]
    wait_recv(0, *ground_part)
    wait_recv(0, *air_part)
    states = [
        (air_ref, vel_ref, st_ref),
        (air_a, vel_a, st_a),
        (air_b, vel_b, st_b),
        (air_out, vel_out, st_out),
    ]
    for n in range(STEPS):
        src = states[n] if n < len(states) - 1 else states[-2]
        dst = states[n + 1] if n + 1 < STEPS else states[-1]
        last = n + 1 == STEPS
        one_step(
            src[0], air_ref.at[4], src[1], src[2], mod_ref, b_ref, recv_l.at[0], recv_r.at[0],
            recv_l.at[n], recv_r.at[n], scal_ref, dst[0], dst[1], dst[2],
            None if last else send_l.at[n + 1], None if last else send_r.at[n + 1], coef_ref,
            None if last else functools.partial(start, n + 1, *counts[n + 1]),
        )
        if not last:
            wait_recv(n + 1, *counts[n + 1])
    for xl in range(width):
        m = jnp.concatenate([air_out[f, xl] for f in range(4)], 0)
        t = m.T.reshape(n_py, nyl, 4 * az_n)
        pay_out[:, pl.ds(xl * nyl, nyl), :] = t
    group_send(pay_out, pay_back, 2)
    group_wait(pay_out, pay_back, 2)
    for yl in range(nyl):
        nb = pay_back[:, pl.ds(yl, width, stride=nyl), :].reshape(n_py * width, 4 * nz)
        tb = nb.T
        for f in range(4):
            airblk_out[f, pl.ds(yl, nz, stride=nyl), :] = tb[f * nz : (f + 1) * nz]
    wait_send(0, *ground_part)
    wait_send(0, *air_part)
    for n in range(1, STEPS):
        wait_send(n, *counts[n])
    group_send_wait(pay_send, pay_ref, 0)
    group_send_wait(pay_out, pay_back, 2)


def fused(blk, bulkblk, ground, mod, b, wind, lift, az_n, gz, width):
    n_py = lax.axis_size("py")
    n_ring = lax.axis_size(RING)
    nyl = blk.shape[1] // az_n
    ny = nyl * n_py
    fields = (4, width, az_n, ny)
    rows_l = 9 * gz + az_n
    rows_r = 5 * gz + 5 * az_n
    vmem = pl.BlockSpec(memory_space=pltpu.VMEM)
    return pl.pallas_call(
        functools.partial(fused_kernel, n_py, n_ring, gz, width),
        out_shape=(
            jax.ShapeDtypeStruct(blk.shape, jnp.float32),
            jax.ShapeDtypeStruct(ground.shape, jnp.float32),
        ),
        in_specs=[vmem] * 5 + [pl.BlockSpec(memory_space=pltpu.SMEM)] * 2,
        out_specs=(vmem, vmem),
        scratch_shapes=[
            pltpu.VMEM((n_py, 2 * nyl * width, 4 * az_n), jnp.float32),
            pltpu.VMEM((n_py, 2 * nyl * width, 4 * az_n), jnp.float32),
            pltpu.VMEM((n_py, nyl * width, 4 * az_n), jnp.float32),
            pltpu.VMEM((n_py, nyl * width, 4 * az_n), jnp.float32),
            pltpu.SemaphoreType.DMA((4, n_py)),
            pltpu.VMEM((5, width, az_n, ny), jnp.float32),
            pltpu.VMEM(fields, jnp.float32),
            pltpu.VMEM(fields, jnp.float32),
            pltpu.VMEM((3, width, gz, ny), jnp.float32),
            pltpu.VMEM((6, width, gz, ny), jnp.float32),
            pltpu.VMEM(fields, jnp.float32),
            pltpu.VMEM((3, width, gz, ny), jnp.float32),
            pltpu.VMEM((6, width, gz, ny), jnp.float32),
            pltpu.VMEM((3, az_n, ny), jnp.float32),
            pltpu.VMEM((STEPS, rows_l, ny), jnp.float32),
            pltpu.VMEM((STEPS, rows_r, ny), jnp.float32),
            pltpu.VMEM((STEPS, rows_r, ny), jnp.float32),
            pltpu.VMEM((STEPS, rows_l, ny), jnp.float32),
            pltpu.SemaphoreType.DMA((STEPS + 1, 2)),
            pltpu.SemaphoreType.DMA((STEPS + 1, 2)),
        ],
        compiler_params=pltpu.CompilerParams(collective_id=0, has_side_effects=True),
        interpret=INTERPRET,
    )(blk, bulkblk, ground, mod, b, wind, lift)


def body(air_state, air_bulk, air_buoyancy, air_wind, ground_state, ground_moduli, ground_buoyancy):
    f_n, az_n, ny_l, nx_l = air_state.shape
    nf, gz, width, ny = ground_state.shape
    blk = air_state.reshape(f_n, az_n * ny_l, nx_l)
    bulkblk = air_bulk.reshape(az_n * ny_l, nx_l)
    ground = ground_state.reshape(nf, gz * width, ny)
    mod = ground_moduli.reshape(ground_moduli.shape[0], gz * width, ny)
    b = ground_buoyancy.reshape(gz * width, ny)
    air, ground_after = fused(blk, bulkblk, ground, mod, b, air_wind, air_buoyancy, az_n, gz, width)
    return (air.reshape(air_state.shape), ground_after.reshape(ground_state.shape))


def solution(mesh):
    placed = (
        P(None, None, "py", "px"),
        P(None, "py", "px"),
        P(),
        P(),
        P(None, None, ("px", "py"), None),
        P(None, None, ("px", "py"), None),
        P(None, ("px", "py"), None),
    )
    return jax.shard_map(
        body,
        mesh=mesh,
        in_specs=placed,
        out_specs=(P(None, None, "py", "px"), P(None, None, ("px", "py"), None)),
        check_vma=False,
    )
```
